256 devices in a mesh: band: 16 (over x_hi, y, core), ga: 16 (over z, x_lo).
Axes of the slice: x: 4 (x_hi: 2, x_lo: 2; x = x_hi * 2 + x_lo), y: 4, z: 8, core: 2. Of those that a mesh axis runs over, the one named last changes fastest.
Arguments:
- coeffs: float32 [1024, 65536], P('band', 'ga'), may hold values from -90 to 90, as said below
Outputs:
- orthonormal: float32 [1024, 65536], P('band', 'ga')
The draws below stay inside these ranges and needn't reach their ends.
Inputs may be any that keep to these rules, and one draw needn't show every extreme that they name: `coeffs`: bands are linearly independent.
All inputs are finite; a program needn't handle non-finite values.
Results may differ from the reference program's by a relative error of at most 0.00029.
Values sent between devices are 32-bit elements; how exact they have to be, the bound alone decides.
A program may use at most 128 MiB of HBM per device.

```python
import jax
import jax.numpy as jnp
from jax import lax

NB = 1024
NGT = 65536


def draw_coeffs(key, part):
    key_noise, key_scale, key_common = jax.random.split(key, 3)
    noise = jnp.clip(jax.random.normal(key_noise, (NB, NGT), jnp.float32), -5.0, 5.0)
    common_weight = 0.3
    scales = jnp.exp(jax.random.uniform(key_scale, (NB, 1), jnp.float32, 0.0, 2.302585))
    common = jnp.clip(jax.random.normal(key_common, (1, NGT), jnp.float32), -5.0, 5.0)
    return scales * (noise + 0.6 * jnp.roll(noise, 1, axis=0)) + common_weight * common


def setup_inputs(seed: int = 0) -> dict:
    arg_keys = jax.random.split(jax.random.key(seed), 2)
    coeffs = draw_coeffs(jax.random.fold_in(arg_keys[1], 71), 0)
    return dict(coeffs=coeffs)


def reference(coeffs):
    columns_all = coeffs.shape[1]
    margin = jnp.dot(coeffs.astype(jnp.float32), coeffs.T.astype(jnp.float32), precision=lax.Precision.HIGHEST, preferred_element_type=jnp.float32) / columns_all
    factor = jnp.linalg.cholesky(margin)
    return lax.linalg.triangular_solve(factor, coeffs, left_side=True, lower=True)
```

```python
import functools

import jax
import jax.numpy as jnp
from jax import lax
from jax.experimental import pallas as pl
from jax.experimental.pallas import tpu as pltpu
from jax.sharding import PartitionSpec as P

MESH = pl.DeviceIdType.MESH

B = 128
V = 8


def split(x):
    hi = x.astype(jnp.bfloat16)
    return hi, (x - hi.astype(jnp.float32)).astype(jnp.bfloat16)


def dot3(a, b, dims):
    (ca,), (cb,) = dims
    ah, al = a
    bh, bl = b
    left = jnp.concatenate([ah, al, ah], axis=ca)
    right = jnp.concatenate([bh, bh, bl], axis=cb)
    return lax.dot_general(left, right, (dims, ((), ())), preferred_element_type=jnp.float32)


def lane_col(t, c):
    return jnp.broadcast_to(t[:, c : c + 1], (V, B))


def sub_row(t, k):
    return jnp.broadcast_to(t[k : k + 1, :], (V, B))


def factor_inverse(rows):
    n = len(rows)
    sub = lax.broadcasted_iota(jnp.int32, (V, B), 0)
    lane = lax.broadcasted_iota(jnp.int32, (V, B), 1)
    out = []
    for p in range(n):
        c0 = p * V
        in_block = (lane >= c0) & (lane < c0 + V)
        cols = [lane_col(rows[p], c0 + k) for k in range(V)]
        t = jnp.where(in_block, jnp.where(lane - c0 == sub, 1.0, 0.0), rows[p])
        f = jnp.where(lane < c0 + V, t, 0.0)
        pivots = jnp.zeros((V, B), jnp.float32)
        for k in range(V):
            d = sub_row(cols[k], k)
            r = 1.0 / d
            pivots = jnp.where(sub == k, d, pivots)
            here = sub == k
            mult = jnp.where(here, 0.0, cols[k])
            below = jnp.where(sub > k, cols[k], 0.0)
            for j in range(k + 1, V):
                u = sub_row(cols[j], k) * r
                cols[j] = jnp.where(here, u, cols[j] - mult * u)
            u = sub_row(t, k) * r
            t = jnp.where(here, u, t - mult * u)
            if k < V - 1:
                f = f - below * (sub_row(f, k) * r)
        out.append(f * lax.rsqrt(pivots))
        w = [sub_row(t, k) for k in range(V)]
        for q in range(p + 1, n):
            acc = jnp.where(in_block, 0.0, rows[q])
            m = [lane_col(rows[q], c0 + k) * w[k] for k in range(V)]
            while len(m) > 1:
                m = [m[2 * e] + m[2 * e + 1] for e in range(len(m) // 2)]
            rows[q] = acc - m[0]
    return out


def blocks_of(n):
    order, at = [], {}
    for i in range(n):
        for j in range(i, n):
            at[i, j] = len(order)
            order.append((i, j))
    return order, at


def elim_kernel(n, g_ref, c_ref, x_ref, a_ref, z_ref):
    width = c_ref.shape[1]
    order, at = blocks_of(n)
    tiles = B // V
    for i, j in order:
        a_ref[i, :, j * B : (j + 1) * B] = g_ref[at[i, j] * tiles : (at[i, j] + 1) * tiles].reshape(B, B)
    for i in range(n):
        a_ref[i, :, n * B :] = c_ref[i * B : (i + 1) * B, :]

    def step(i, carry):
        here = pl.multiple_of(i * B, B)
        rows = [a_ref[i, q * V : (q + 1) * V, pl.ds(here, B)] for q in range(tiles)]
        for q, z in enumerate(factor_inverse(rows)):
            z_ref[q * V : (q + 1) * V, :] = z
        for k in range(n):

            @pl.when(i == k)
            def _():
                z = split(z_ref[...])
                panel = dot3(z, split(a_ref[k, :, (k + 1) * B :]), ((1,), (0,)))
                x_ref[k * B : (k + 1) * B, :] = panel[:, panel.shape[1] - width :]
                ph, plo = split(panel)
                for j in range(k + 1, n):
                    at_j = (j - k - 1) * B
                    left = (ph[:, at_j : at_j + B], plo[:, at_j : at_j + B])
                    right = (ph[:, at_j:], plo[:, at_j:])
                    a_ref[j, :, j * B :] -= dot3(left, right, ((0,), (0,)))

        return carry

    lax.fori_loop(0, n, step, 0)


def eliminate(g, c):
    rows, width = c.shape
    n = rows // B
    return pl.pallas_call(
        lambda *refs: elim_kernel(n, *refs),
        out_shape=jax.ShapeDtypeStruct((rows, width), jnp.float32),
        in_specs=[pl.BlockSpec(memory_space=pltpu.VMEM)] * 2,
        out_specs=pl.BlockSpec(memory_space=pltpu.VMEM),
        scratch_shapes=[
            pltpu.VMEM((n, B, n * B + width), jnp.float32),
            pltpu.VMEM((B, B), jnp.float32),
        ],
        compiler_params=pltpu.CompilerParams(vmem_limit_bytes=48 << 20),
        name="eliminate",
    )(g, c)


def gram_kernel(scale, c_ref, g_ref):
    rows, depth = c_ref.shape
    n = rows // B
    order, at = blocks_of(n)
    tiles = B // V
    hi, lo = split(c_ref[...])
    for i in range(n):
        left = (hi[i * B : (i + 1) * B], lo[i * B : (i + 1) * B])
        right = (hi[i * B :], lo[i * B :])
        out = dot3(left, right, ((1,), (1,))) * scale
        for j in range(i, n):
            block = out[:, (j - i) * B : (j - i + 1) * B]
            g_ref[at[i, j] * tiles : (at[i, j] + 1) * tiles] = block.reshape(tiles, V, B)


def gram(c, columns_all):
    rows, _ = c.shape
    n = rows // B
    total = n * (n + 1) // 2 * (B // V)
    return pl.pallas_call(
        lambda *refs: gram_kernel(1.0 / columns_all, *refs),
        out_shape=jax.ShapeDtypeStruct((total, V, B), jnp.float32),
        in_specs=[pl.BlockSpec(memory_space=pltpu.VMEM)],
        out_specs=pl.BlockSpec(memory_space=pltpu.VMEM),
        compiler_params=pltpu.CompilerParams(vmem_limit_bytes=48 << 20),
        name="gram",
    )(c)


def exchange_kernel(n, forward, src_ref, dst_ref, send_sem, recv_sem, own_sem):
    me = lax.axis_index("band")
    barrier = pltpu.get_barrier_semaphore()
    rows, cols = (src_ref if forward else dst_ref).shape
    width = cols // n

    def part(ref, split_columns, index):
        if split_columns:
            return ref.at[:, pl.ds(pl.multiple_of(index * width, width), width)]
        return ref.at[pl.ds(pl.multiple_of(index * rows, rows), rows), :]

    def greet(s, carry):
        pl.semaphore_signal(
            barrier, inc=1, device_id={"band": lax.rem(me + s, n)}, device_id_type=MESH
        )
        return carry

    lax.fori_loop(1, n, greet, 0)
    own = pltpu.make_async_copy(part(src_ref, forward, me), part(dst_ref, not forward, me), own_sem)
    own.start()
    pl.semaphore_wait(barrier, n - 1)

    def copy(s):
        peer = lax.rem(me + s, n)
        return pltpu.make_async_remote_copy(
            src_ref=part(src_ref, forward, peer),
            dst_ref=part(dst_ref, not forward, me),
            send_sem=send_sem.at[s],
            recv_sem=recv_sem.at[s],
            device_id={"band": peer},
            device_id_type=MESH,
        )

    def start(s, carry):
        copy(s).start()
        return carry

    def wait(s, carry):
        peer = lax.rem(me - s + n, n)
        got = pltpu.make_async_remote_copy(
            src_ref=part(src_ref, forward, lax.rem(me + s, n)),
            dst_ref=part(dst_ref, not forward, peer),
            send_sem=send_sem.at[s],
            recv_sem=recv_sem.at[s],
            device_id={"band": lax.rem(me + s, n)},
            device_id_type=MESH,
        )
        got.wait()
        return carry

    lax.fori_loop(1, n, start, 0)
    own.wait()
    lax.fori_loop(1, n, wait, 0)


def exchange(x, n, forward):
    rows, cols = x.shape
    shape = (rows * n, cols // n) if forward else (rows // n, cols * n)
    return pl.pallas_call(
        functools.partial(exchange_kernel, n, forward),
        out_shape=jax.ShapeDtypeStruct(shape, x.dtype),
        in_specs=[pl.BlockSpec(memory_space=pl.ANY)],
        out_specs=pl.BlockSpec(memory_space=pl.ANY),
        scratch_shapes=[
            pltpu.SemaphoreType.DMA((n,)),
            pltpu.SemaphoreType.DMA((n,)),
            pltpu.SemaphoreType.DMA,
        ],
        compiler_params=pltpu.CompilerParams(
            collective_id=0 if forward else 1, has_side_effects=True
        ),
        name="exchange" if forward else "exchange_back",
    )(x)


CORES, YS, XS, ZS = 2, 4, 4, 8
HALF = 288
FIRST = HALF // 4
SECOND = FIRST // 4
Z_USED = 6
THIRD = SECOND // Z_USED


def coordinates():
    band, ga = lax.axis_index("band"), lax.axis_index("ga")
    core, y = lax.rem(band, CORES), lax.rem(band // CORES, YS)
    x = (band // (CORES * YS)) * 2 + lax.rem(ga, 2)
    return core, x, y, ga // 2


def device(core, x, y, z):
    return {"band": ((x // 2) * YS + y) * CORES + core, "ga": z * 2 + lax.rem(x, 2)}


def sum_kernel(p_ref, o_ref, acc1, acc2, acc3, got0, got1, got2, got3, send, recv):
    core, x, y, z = coordinates()
    first_is_y = core == 0
    a = jnp.where(first_is_y, y, x)
    b = jnp.where(first_is_y, x, y)

    def first_peer(s):
        to = lax.rem(a + s, 4)
        return to, device(core, jnp.where(first_is_y, x, to), jnp.where(first_is_y, to, y), z)

    def second_peer(s):
        to = lax.rem(b + s, 4)
        return to, device(core, jnp.where(first_is_y, to, x), jnp.where(first_is_y, y, to), z)

    def z_peer(s):
        to = lax.rem(z + s, ZS)
        return to, device(core, x, y, to)

    partner = device(1 - core, x, y, z)

    barrier = pltpu.get_barrier_semaphore()
    peers = [partner]
    peers += [first_peer(s)[1] for s in range(1, 4)]
    peers += [second_peer(s)[1] for s in range(1, 4)]
    peers += [z_peer(s)[1] for s in range(1, ZS)]
    for peer in peers:
        pl.semaphore_signal(barrier, inc=1, device_id=peer, device_id_type=MESH)
    pl.semaphore_wait(barrier, len(peers))

    def copy(src, dst, index, peer):
        return pltpu.make_async_remote_copy(
            src_ref=src,
            dst_ref=dst,
            send_sem=send.at[index],
            recv_sem=recv.at[index],
            device_id=peer,
            device_id_type=MESH,
        )

    mine = core * HALF
    c = copy(p_ref.at[pl.ds((1 - core) * HALF, HALF)], got0, 0, partner)
    c.start()
    c.wait()

    def add0(t, carry):
        at = pl.ds(t * 8, 8)
        acc1[at] = p_ref[pl.ds(mine + t * 8, 8)] + got0[at]
        return carry

    lax.fori_loop(0, HALF // 8, add0, 0)

    started = []
    for s in range(1, 4):
        to, peer = first_peer(s)
        c = copy(acc1.at[pl.ds(to * FIRST, FIRST)], got1.at[s - 1], s, peer)
        c.start()
        started.append(c)
    for c in started:
        c.wait()

    def add1(t, carry):
        at = pl.ds(t * 8, 8)
        acc2[at] = (acc1[pl.ds(a * FIRST + t * 8, 8)] + got1[0, at]) + (got1[1, at] + got1[2, at])
        return carry

    lax.fori_loop(0, FIRST // 8, add1, 0)
    started = []
    for s in range(1, 4):
        to, peer = second_peer(s)
        c = copy(acc2.at[pl.ds(to * SECOND, SECOND)], got2.at[s - 1], 3 + s, peer)
        c.start()
        started.append(c)
    for c in started:
        c.wait()
    at = pl.ds(b * SECOND, SECOND)
    acc3[...] = (acc2[at] + got2[0]) + (got2[1] + got2[2])

    for s in range(1, ZS):
        to, peer = z_peer(s)

        @pl.when(to < Z_USED)
        def _():
            copy(acc3.at[pl.ds(to * THIRD, THIRD)], got3.at[s - 1], 6 + s, peer).start()

    base2 = mine + a * FIRST
    base3 = base2 + b * SECOND
    own = base3 + z * THIRD

    @pl.when(z < Z_USED)
    def _():
        for s in range(1, ZS):
            copy(acc3.at[pl.ds(0, THIRD)], got3.at[s - 1], 6 + s, partner).wait_recv()
        total = acc3[pl.ds(z * THIRD, THIRD)]
        for s in range(1, ZS):
            total = total + got3[s - 1]
        o_ref[pl.ds(own, THIRD)] = total

    for s in range(1, ZS):
        to, peer = z_peer(s)

        @pl.when(to < Z_USED)
        def _():
            copy(acc3.at[pl.ds(0, THIRD)], got3.at[s - 1], 6 + s, peer).wait_send()

    @pl.when(z < Z_USED)
    def _():
        for s in range(1, ZS):
            to, peer = z_peer(s)
            copy(o_ref.at[pl.ds(own, THIRD)], o_ref.at[pl.ds(own, THIRD)], 13 + s, peer).start()

    for s in range(1, ZS):
        sender = lax.rem(z + ZS - s, ZS)

        @pl.when(sender < Z_USED)
        def _():
            chunk = o_ref.at[pl.ds(base3 + sender * THIRD, THIRD)]
            copy(chunk, chunk, 13 + s, partner).wait_recv()

    @pl.when(z < Z_USED)
    def _():
        for s in range(1, ZS):
            to, peer = z_peer(s)
            copy(o_ref.at[pl.ds(own, THIRD)], o_ref.at[pl.ds(own, THIRD)], 13 + s, peer).wait_send()

    def spread(base, at, size, index, peers_of, count):
        chunk = o_ref.at[pl.ds(base + at * size, size)]
        for s in range(1, count):
            copy(chunk, chunk, index + s, peers_of(s)[1]).start()
        for s in range(1, count):
            sender = lax.rem(at + count - s, count)
            got = o_ref.at[pl.ds(base + sender * size, size)]
            copy(chunk, got, index + s, peers_of(s)[1]).wait()

    spread(base2, b, SECOND, 20, second_peer, 4)
    spread(mine, a, FIRST, 23, first_peer, 4)
    spread(0, core, HALF, 26, lambda s: (1 - core, partner), 2)


def sum_tiles(p):
    vmem = pl.BlockSpec(memory_space=pltpu.VMEM)
    tiles = lambda *shape: pltpu.VMEM((*shape, V, B), jnp.float32)
    return pl.pallas_call(
        sum_kernel,
        out_shape=jax.ShapeDtypeStruct(p.shape, p.dtype),
        in_specs=[vmem],
        out_specs=vmem,
        scratch_shapes=[
            tiles(HALF),
            tiles(FIRST),
            tiles(SECOND),
            tiles(HALF),
            tiles(3, FIRST),
            tiles(3, SECOND),
            tiles(7, THIRD),
            pltpu.SemaphoreType.DMA((28,)),
            pltpu.SemaphoreType.DMA((28,)),
        ],
        compiler_params=pltpu.CompilerParams(
            collective_id=2, has_side_effects=True, vmem_limit_bytes=48 << 20
        ),
        name="sum_tiles",
    )(p)


def local(coeffs):
    bands = lax.axis_size("band")
    columns_all = coeffs.shape[1] * lax.axis_size("ga")
    held = exchange(coeffs, bands, True)
    margin = sum_tiles(gram(held, columns_all))
    return exchange(eliminate(margin, held), bands, False)


def solution(mesh):
    return jax.shard_map(
        local,
        mesh=mesh,
        in_specs=(P("band", "ga"),),
        out_specs=P("band", "ga"),
        check_vma=False,
    )
```

```python
import functools

import jax
import jax.numpy as jnp
from jax import lax
from jax.experimental import pallas as pl
from jax.experimental.pallas import tpu as pltpu
from jax.sharding import PartitionSpec as P

MESH = pl.DeviceIdType.MESH

B = 128
V = 8


def split(x):
    hi = x.astype(jnp.bfloat16)
    return hi, (x - hi.astype(jnp.float32)).astype(jnp.bfloat16)


def dot3(a, b, dims):
    (ca,), (cb,) = dims
    ah, al = a
    bh, bl = b
    left = jnp.concatenate([ah, al, ah], axis=ca)
    right = jnp.concatenate([bh, bh, bl], axis=cb)
    return lax.dot_general(left, right, (dims, ((), ())), preferred_element_type=jnp.float32)


def lane_col(t, c):
    return jnp.take_along_axis(t, jnp.full((V, B), c, jnp.int32), axis=1)


def sub_row(t, k):
    return jnp.broadcast_to(t[k : k + 1, :], (V, B))


def tree(m):
    while len(m) > 1:
        m = [m[e] + m[e + 1] if e + 1 < len(m) else m[e] for e in range(0, len(m), 2)]
    return m[0]


def factor_inverse(rows):
    n = len(rows)
    rows = list(rows)
    sub = lax.broadcasted_iota(jnp.int32, (V, B), 0)
    lane = lax.broadcasted_iota(jnp.int32, (V, B), 1)
    out = []
    cols = [lane_col(rows[0], k) for k in range(V)]
    for p in range(n):
        c0 = p * V
        last = p == n - 1
        in_block = (lane >= c0) & (lane < c0 + V)
        t = jnp.where(in_block, jnp.where(lane - c0 == sub, 1.0, 0.0), rows[p])
        f = jnp.where(lane < c0 + V, t, 0.0)
        pivots = None
        below_m = {q: [lane_col(rows[q], c0 + k) for k in range(V)] for q in range(p + 1, n)}
        if not last:
            a = list(below_m[p + 1])
            ahead = [lane_col(rows[p + 1], c0 + V + k) for k in range(V)]
        for k in range(0, V, 2):
            h1, h2 = sub == k, sub == k + 1
            here = h1 | h2
            d11, d12, d22 = sub_row(cols[k], k), sub_row(cols[k + 1], k), sub_row(cols[k + 1], k + 1)
            det = d11 * d22 - d12 * d12
            r = 1.0 / det
            m1, m2 = jnp.where(here, 0.0, cols[k]), jnp.where(here, 0.0, cols[k + 1])

            def solve(col):
                v1, v2 = sub_row(col, k), sub_row(col, k + 1)
                return (d22 * v1 - d12 * v2) * r, (d11 * v2 - d12 * v1) * r

            def eliminate(col):
                u1, u2 = solve(col)
                return jnp.where(h1, u1, jnp.where(h2, u2, col - (m1 * u1 + m2 * u2))), u1, u2

            for j in range(k + 2, V):
                cols[j], u1, u2 = eliminate(cols[j])
                if not last:
                    a[j] = a[j] - (a[k] * u1 + a[k + 1] * u2)
            if not last:
                s1 = (d22 * a[k] - d12 * a[k + 1]) * r
                s2 = (d11 * a[k + 1] - d12 * a[k]) * r
                for j in range(V):
                    ahead[j] = ahead[j] - (s1 * sub_row(a[k], j) + s2 * sub_row(a[k + 1], j))
            q = 1.0 / d11
            ratio = d12 * q
            f1 = sub_row(f, k)
            f2 = sub_row(f, k + 1) - ratio * f1
            g2 = d11 * r
            g1 = q
            below = sub > k + 1
            b1 = jnp.where(below, cols[k], 0.0)
            b2 = jnp.where(below, cols[k + 1], 0.0)
            l2 = b2 - b1 * ratio
            f = jnp.where(h2, f2, f - b1 * (f1 * g1) - l2 * (f2 * g2))
            t, _, _ = eliminate(t)
            scale = jnp.where(h1, g1, g2)
            pivots = scale if pivots is None else jnp.where(here, scale, pivots)
        out.append(f * jnp.sqrt(pivots))
        if last:
            break
        cols = ahead
        w = [sub_row(t, k) for k in range(V)]
        for q in range(p + 1, n):
            acc = jnp.where(in_block, 0.0, rows[q])
            rows[q] = acc - tree([below_m[q][k] * w[k] for k in range(V)])
    return out


def blocks_of(n):
    order, at = [], {}
    for i in range(n):
        for j in range(i, n):
            at[i, j] = len(order)
            order.append((i, j))
    return order, at


def elim_kernel(n, g_ref, c_ref, out_ref, a_ref, z_ref, x_ref, send_sem, recv_sem, own_sem):
    width = c_ref.shape[1]
    rows_each = out_ref.shape[0]
    bands = n * B // rows_each
    per_panel = B // rows_each
    me = lax.axis_index("band")
    barrier = pltpu.get_barrier_semaphore()

    def greet(s, carry):
        pl.semaphore_signal(
            barrier, inc=1, device_id={"band": lax.rem(me + s, bands)}, device_id_type=MESH
        )
        return carry

    lax.fori_loop(1, bands, greet, 0)
    order, at = blocks_of(n)
    tiles = B // V

    sub = lax.broadcasted_iota(jnp.int32, (V, B), 0)
    lane = lax.broadcasted_iota(jnp.int32, (V, B), 1)
    lane_scale, row_scale = [], []
    for i in range(n):
        on_diagonal = [
            jnp.where(lane == q * V + sub, g_ref[at[i, i] * tiles + q], 0.0) for q in range(tiles)
        ]
        diagonal = jnp.sum(tree(on_diagonal), axis=0, keepdims=True)
        scale = jnp.broadcast_to(lax.rsqrt(diagonal), (V, B))
        lane_scale.append(scale)
        row_scale.append([jnp.take_along_axis(scale, q * V + sub, axis=1) for q in range(tiles)])
    for i, j in order:
        for q in range(tiles):
            a_ref[i, q * V : (q + 1) * V, j * B : (j + 1) * B] = (
                g_ref[at[i, j] * tiles + q] * row_scale[i][q] * lane_scale[j]
            )
    for i in range(n):
        for q in range(tiles):
            for h in range(width // B):
                a_ref[i, q * V : (q + 1) * V, (n + h) * B : (n + h + 1) * B] = (
                    c_ref[i * B + q * V : i * B + (q + 1) * V, h * B : (h + 1) * B] * row_scale[i][q]
                )

    def remote(peer, sender):
        return pltpu.make_async_remote_copy(
            src_ref=x_ref.at[pl.ds(peer * rows_each, rows_each), :],
            dst_ref=out_ref.at[:, pl.ds(pl.multiple_of(sender * width, width), width)],
            send_sem=send_sem.at[peer],
            recv_sem=recv_sem.at[sender],
            device_id={"band": peer},
            device_id_type=MESH,
        )

    own = pltpu.make_async_copy(
        x_ref.at[pl.ds(me * rows_each, rows_each), :],
        out_ref.at[:, pl.ds(pl.multiple_of(me * width, width), width)],
        own_sem,
    )

    def step(i, carry):
        here = pl.multiple_of(i * B, B)
        rows = [a_ref[i, q * V : (q + 1) * V, pl.ds(here, B)] for q in range(tiles)]
        for q, z in enumerate(factor_inverse(rows)):
            z_ref[q * V : (q + 1) * V, :] = z
        for k in range(n):

            @pl.when(i == k)
            def _():
                z = split(z_ref[...])
                panel = dot3(z, split(a_ref[k, :, (k + 1) * B :]), ((1,), (0,)))
                x_ref[k * B : (k + 1) * B, :] = panel[:, panel.shape[1] - width :]
                if k == 0:
                    pl.semaphore_wait(barrier, bands - 1)
                for peer in range(k * per_panel, (k + 1) * per_panel):

                    @pl.when(peer != me)
                    def _():
                        remote(peer, me).start()

                    @pl.when(peer == me)
                    def _():
                        own.start()

                ph, plo = split(panel)
                for j in range(k + 1, n):
                    at_j = (j - k - 1) * B
                    left = (ph[:, at_j : at_j + B], plo[:, at_j : at_j + B])
                    right = (ph[:, at_j:], plo[:, at_j:])
                    a_ref[j, :, j * B :] -= dot3(left, right, ((0,), (0,)))

        return carry

    lax.fori_loop(0, n, step, 0)
    own.wait()
    for other in range(bands):

        @pl.when(other != me)
        def _():
            remote(other, me).wait_send()
            remote(other, other).wait_recv()


def eliminate(g, c, bands):
    rows, width = c.shape
    n = rows // B
    return pl.pallas_call(
        functools.partial(elim_kernel, n),
        out_shape=jax.ShapeDtypeStruct((rows // bands, width * bands), jnp.float32),
        in_specs=[pl.BlockSpec(memory_space=pltpu.VMEM)] * 2,
        out_specs=pl.BlockSpec(memory_space=pltpu.VMEM),
        scratch_shapes=[
            pltpu.VMEM((n, B, n * B + width), jnp.float32),
            pltpu.VMEM((B, B), jnp.float32),
            pltpu.VMEM((rows, width), jnp.float32),
            pltpu.SemaphoreType.DMA((bands,)),
            pltpu.SemaphoreType.DMA((bands,)),
            pltpu.SemaphoreType.DMA,
        ],
        compiler_params=pltpu.CompilerParams(
            collective_id=1, has_side_effects=True, vmem_limit_bytes=48 << 20
        ),
        name="eliminate",
    )(g, c)


def gram_kernel(scale, c_ref, g_ref):
    rows, depth = c_ref.shape
    n = rows // B
    order, at = blocks_of(n)
    tiles = B // V
    hi, lo = split(c_ref[...])
    for i in range(n):
        left = (hi[i * B : (i + 1) * B], lo[i * B : (i + 1) * B])
        right = (hi[i * B :], lo[i * B :])
        out = dot3(left, right, ((1,), (1,))) * scale
        for j in range(i, n):
            block = out[:, (j - i) * B : (j - i + 1) * B]
            g_ref[at[i, j] * tiles : (at[i, j] + 1) * tiles] = block.reshape(tiles, V, B)


def gram(c, columns_all):
    rows, _ = c.shape
    n = rows // B
    total = n * (n + 1) // 2 * (B // V)
    return pl.pallas_call(
        lambda *refs: gram_kernel(1.0 / columns_all, *refs),
        out_shape=jax.ShapeDtypeStruct((total, V, B), jnp.float32),
        in_specs=[pl.BlockSpec(memory_space=pltpu.VMEM)],
        out_specs=pl.BlockSpec(memory_space=pltpu.VMEM),
        compiler_params=pltpu.CompilerParams(vmem_limit_bytes=48 << 20),
        name="gram",
    )(c)


def exchange_kernel(n, forward, src_ref, dst_ref, send_sem, recv_sem, own_sem):
    me = lax.axis_index("band")
    barrier = pltpu.get_barrier_semaphore()
    rows, cols = (src_ref if forward else dst_ref).shape
    width = cols // n

    def part(ref, split_columns, index):
        if split_columns:
            return ref.at[:, pl.ds(pl.multiple_of(index * width, width), width)]
        return ref.at[pl.ds(pl.multiple_of(index * rows, rows), rows), :]

    def greet(s, carry):
        pl.semaphore_signal(
            barrier, inc=1, device_id={"band": lax.rem(me + s, n)}, device_id_type=MESH
        )
        return carry

    lax.fori_loop(1, n, greet, 0)
    own = pltpu.make_async_copy(part(src_ref, forward, me), part(dst_ref, not forward, me), own_sem)
    own.start()
    pl.semaphore_wait(barrier, n - 1)

    def copy(s):
        peer = lax.rem(me + s, n)
        return pltpu.make_async_remote_copy(
            src_ref=part(src_ref, forward, peer),
            dst_ref=part(dst_ref, not forward, me),
            send_sem=send_sem.at[s],
            recv_sem=recv_sem.at[s],
            device_id={"band": peer},
            device_id_type=MESH,
        )

    def start(s, carry):
        copy(s).start()
        return carry

    def wait(s, carry):
        peer = lax.rem(me - s + n, n)
        got = pltpu.make_async_remote_copy(
            src_ref=part(src_ref, forward, lax.rem(me + s, n)),
            dst_ref=part(dst_ref, not forward, peer),
            send_sem=send_sem.at[s],
            recv_sem=recv_sem.at[s],
            device_id={"band": lax.rem(me + s, n)},
            device_id_type=MESH,
        )
        got.wait()
        return carry

    lax.fori_loop(1, n, start, 0)
    own.wait()
    lax.fori_loop(1, n, wait, 0)


def exchange(x, n, forward):
    rows, cols = x.shape
    shape = (rows * n, cols // n) if forward else (rows // n, cols * n)
    return pl.pallas_call(
        functools.partial(exchange_kernel, n, forward),
        out_shape=jax.ShapeDtypeStruct(shape, x.dtype),
        in_specs=[pl.BlockSpec(memory_space=pl.ANY)],
        out_specs=pl.BlockSpec(memory_space=pl.ANY),
        scratch_shapes=[
            pltpu.SemaphoreType.DMA((n,)),
            pltpu.SemaphoreType.DMA((n,)),
            pltpu.SemaphoreType.DMA,
        ],
        compiler_params=pltpu.CompilerParams(
            collective_id=0 if forward else 1, has_side_effects=True
        ),
        name="exchange" if forward else "exchange_back",
    )(x)


CORES, YS, XS, ZS = 2, 4, 4, 8
HALF = 288
FIRST = HALF // 4
SECOND = FIRST // 4
Z_USED = 6
THIRD = SECOND // Z_USED


def coordinates():
    band, ga = lax.axis_index("band"), lax.axis_index("ga")
    core, y = lax.rem(band, CORES), lax.rem(band // CORES, YS)
    x = (band // (CORES * YS)) * 2 + lax.rem(ga, 2)
    return core, x, y, ga // 2


def device(core, x, y, z):
    return {"band": ((x // 2) * YS + y) * CORES + core, "ga": z * 2 + lax.rem(x, 2)}


def sum_kernel(p_ref, o_ref, acc1, acc2, acc3, got0, got1, got2, got3, send, recv):
    core, x, y, z = coordinates()
    first_is_y = core == 0
    a = jnp.where(first_is_y, y, x)
    b = jnp.where(first_is_y, x, y)

    def first_peer(s):
        to = lax.rem(a + s, 4)
        return to, device(core, jnp.where(first_is_y, x, to), jnp.where(first_is_y, to, y), z)

    def second_peer(s):
        to = lax.rem(b + s, 4)
        return to, device(core, jnp.where(first_is_y, to, x), jnp.where(first_is_y, y, to), z)

    def z_peer(s):
        to = lax.rem(z + s, ZS)
        return to, device(core, x, y, to)

    partner = device(1 - core, x, y, z)

    barrier = pltpu.get_barrier_semaphore()
    peers = [partner]
    peers += [first_peer(s)[1] for s in range(1, 4)]
    peers += [second_peer(s)[1] for s in range(1, 4)]
    peers += [z_peer(s)[1] for s in range(1, ZS)]
    for peer in peers:
        pl.semaphore_signal(barrier, inc=1, device_id=peer, device_id_type=MESH)
    pl.semaphore_wait(barrier, len(peers))

    def copy(src, dst, index, peer):
        return pltpu.make_async_remote_copy(
            src_ref=src,
            dst_ref=dst,
            send_sem=send.at[index],
            recv_sem=recv.at[index],
            device_id=peer,
            device_id_type=MESH,
        )

    mine = core * HALF
    c = copy(p_ref.at[pl.ds((1 - core) * HALF, HALF)], got0, 0, partner)
    c.start()
    c.wait()

    def add0(t, carry):
        at = pl.ds(t * 8, 8)
        acc1[at] = p_ref[pl.ds(mine + t * 8, 8)] + got0[at]
        return carry

    lax.fori_loop(0, HALF // 8, add0, 0)

    started = []
    for s in range(1, 4):
        to, peer = first_peer(s)
        c = copy(acc1.at[pl.ds(to * FIRST, FIRST)], got1.at[s - 1], s, peer)
        c.start()
        started.append(c)
    for c in started:
        c.wait()

    def add1(t, carry):
        at = pl.ds(t * 8, 8)
        acc2[at] = (acc1[pl.ds(a * FIRST + t * 8, 8)] + got1[0, at]) + (got1[1, at] + got1[2, at])
        return carry

    lax.fori_loop(0, FIRST // 8, add1, 0)
    started = []
    for s in range(1, 4):
        to, peer = second_peer(s)
        c = copy(acc2.at[pl.ds(to * SECOND, SECOND)], got2.at[s - 1], 3 + s, peer)
        c.start()
        started.append(c)
    for c in started:
        c.wait()
    at = pl.ds(b * SECOND, SECOND)
    acc3[...] = (acc2[at] + got2[0]) + (got2[1] + got2[2])

    for s in range(1, ZS):
        to, peer = z_peer(s)

        @pl.when(to < Z_USED)
        def _():
            copy(acc3.at[pl.ds(to * THIRD, THIRD)], got3.at[s - 1], 6 + s, peer).start()

    base2 = mine + a * FIRST
    base3 = base2 + b * SECOND
    own = base3 + z * THIRD

    @pl.when(z < Z_USED)
    def _():
        for s in range(1, ZS):
            copy(acc3.at[pl.ds(0, THIRD)], got3.at[s - 1], 6 + s, partner).wait_recv()
        total = acc3[pl.ds(z * THIRD, THIRD)]
        for s in range(1, ZS):
            total = total + got3[s - 1]
        o_ref[pl.ds(own, THIRD)] = total

    for s in range(1, ZS):
        to, peer = z_peer(s)

        @pl.when(to < Z_USED)
        def _():
            copy(acc3.at[pl.ds(0, THIRD)], got3.at[s - 1], 6 + s, peer).wait_send()

    @pl.when(z < Z_USED)
    def _():
        for s in range(1, ZS):
            to, peer = z_peer(s)
            copy(o_ref.at[pl.ds(own, THIRD)], o_ref.at[pl.ds(own, THIRD)], 13 + s, peer).start()

    for s in range(1, ZS):
        sender = lax.rem(z + ZS - s, ZS)

        @pl.when(sender < Z_USED)
        def _():
            chunk = o_ref.at[pl.ds(base3 + sender * THIRD, THIRD)]
            copy(chunk, chunk, 13 + s, partner).wait_recv()

    @pl.when(z < Z_USED)
    def _():
        for s in range(1, ZS):
            to, peer = z_peer(s)
            copy(o_ref.at[pl.ds(own, THIRD)], o_ref.at[pl.ds(own, THIRD)], 13 + s, peer).wait_send()

    def spread(base, at, size, index, peers_of, count):
        chunk = o_ref.at[pl.ds(base + at * size, size)]
        for s in range(1, count):
            copy(chunk, chunk, index + s, peers_of(s)[1]).start()
        for s in range(1, count):
            sender = lax.rem(at + count - s, count)
            got = o_ref.at[pl.ds(base + sender * size, size)]
            copy(chunk, got, index + s, peers_of(s)[1]).wait()

    spread(base2, b, SECOND, 20, second_peer, 4)
    spread(mine, a, FIRST, 23, first_peer, 4)
    spread(0, core, HALF, 26, lambda s: (1 - core, partner), 2)


def sum_tiles(p):
    vmem = pl.BlockSpec(memory_space=pltpu.VMEM)
    tiles = lambda *shape: pltpu.VMEM((*shape, V, B), jnp.float32)
    return pl.pallas_call(
        sum_kernel,
        out_shape=jax.ShapeDtypeStruct(p.shape, p.dtype),
        in_specs=[vmem],
        out_specs=vmem,
        scratch_shapes=[
            tiles(HALF),
            tiles(FIRST),
            tiles(SECOND),
            tiles(HALF),
            tiles(3, FIRST),
            tiles(3, SECOND),
            tiles(7, THIRD),
            pltpu.SemaphoreType.DMA((28,)),
            pltpu.SemaphoreType.DMA((28,)),
        ],
        compiler_params=pltpu.CompilerParams(
            collective_id=2, has_side_effects=True, vmem_limit_bytes=48 << 20
        ),
        name="sum_tiles",
    )(p)


def local(coeffs):
    bands = lax.axis_size("band")
    columns_all = coeffs.shape[1] * lax.axis_size("ga")
    held = exchange(coeffs, bands, True)
    margin = sum_tiles(gram(held, columns_all))
    return eliminate(margin, held, bands)


def solution(mesh):
    return jax.shard_map(
        local,
        mesh=mesh,
        in_specs=(P("band", "ga"),),
        out_specs=P("band", "ga"),
        check_vma=False,
    )
```

```python
import functools

import jax
import jax.numpy as jnp
from jax import lax
from jax.experimental import pallas as pl
from jax.experimental.pallas import tpu as pltpu
from jax.sharding import PartitionSpec as P

MESH = pl.DeviceIdType.MESH

B = 128
V = 8


def split(x):
    hi = x.astype(jnp.bfloat16)
    return hi, (x - hi.astype(jnp.float32)).astype(jnp.bfloat16)


def dot3(a, b, dims):
    (ca,), (cb,) = dims
    ah, al = a
    bh, bl = b
    left = jnp.concatenate([ah, al, ah], axis=ca)
    right = jnp.concatenate([bh, bh, bl], axis=cb)
    return lax.dot_general(left, right, (dims, ((), ())), preferred_element_type=jnp.float32)


def lane_col(t, c):
    return jnp.take_along_axis(t, jnp.full((V, B), c, jnp.int32), axis=1)


def sub_row(t, k):
    return jnp.broadcast_to(t[k : k + 1, :], (V, B))


def tree(m):
    while len(m) > 1:
        m = [m[e] + m[e + 1] if e + 1 < len(m) else m[e] for e in range(0, len(m), 2)]
    return m[0]


def factor_inverse(rows):
    n = len(rows)
    rows = list(rows)
    sub = lax.broadcasted_iota(jnp.int32, (V, B), 0)
    lane = lax.broadcasted_iota(jnp.int32, (V, B), 1)
    out = []
    cols = [lane_col(rows[0], k) for k in range(V)]
    for p in range(n):
        c0 = p * V
        last = p == n - 1
        in_block = (lane >= c0) & (lane < c0 + V)
        t = jnp.where(in_block, jnp.where(lane - c0 == sub, 1.0, 0.0), rows[p])
        f = jnp.where(lane < c0 + V, t, 0.0)
        pivots = None
        below_m = {q: [lane_col(rows[q], c0 + k) for k in range(V)] for q in range(p + 1, n)}
        if not last:
            a = list(below_m[p + 1])
            ahead = [lane_col(rows[p + 1], c0 + V + k) for k in range(V)]
        for k in range(0, V, 2):
            h1, h2 = sub == k, sub == k + 1
            here = h1 | h2
            d11, d12, d22 = sub_row(cols[k], k), sub_row(cols[k + 1], k), sub_row(cols[k + 1], k + 1)
            det = d11 * d22 - d12 * d12
            r = 1.0 / det
            m1, m2 = jnp.where(here, 0.0, cols[k]), jnp.where(here, 0.0, cols[k + 1])

            def solve(col):
                v1, v2 = sub_row(col, k), sub_row(col, k + 1)
                return (d22 * v1 - d12 * v2) * r, (d11 * v2 - d12 * v1) * r

            def eliminate(col):
                u1, u2 = solve(col)
                return jnp.where(h1, u1, jnp.where(h2, u2, col - (m1 * u1 + m2 * u2))), u1, u2

            for j in range(k + 2, V):
                cols[j], u1, u2 = eliminate(cols[j])
                if not last:
                    a[j] = a[j] - (a[k] * u1 + a[k + 1] * u2)
            if not last:
                s1 = (d22 * a[k] - d12 * a[k + 1]) * r
                s2 = (d11 * a[k + 1] - d12 * a[k]) * r
                for j in range(V):
                    ahead[j] = ahead[j] - (s1 * sub_row(a[k], j) + s2 * sub_row(a[k + 1], j))
            q = 1.0 / d11
            ratio = d12 * q
            f1 = sub_row(f, k)
            f2 = sub_row(f, k + 1) - ratio * f1
            g2 = d11 * r
            g1 = q
            below = sub > k + 1
            b1 = jnp.where(below, cols[k], 0.0)
            b2 = jnp.where(below, cols[k + 1], 0.0)
            l2 = b2 - b1 * ratio
            f = jnp.where(h2, f2, f - b1 * (f1 * g1) - l2 * (f2 * g2))
            t, _, _ = eliminate(t)
            scale = jnp.where(h1, g1, g2)
            pivots = scale if pivots is None else jnp.where(here, scale, pivots)
        out.append(f * jnp.sqrt(pivots))
        if last:
            break
        cols = ahead
        w = [sub_row(t, k) for k in range(V)]
        for q in range(p + 1, n):
            acc = jnp.where(in_block, 0.0, rows[q])
            rows[q] = acc - tree([below_m[q][k] * w[k] for k in range(V)])
    return out


def grouped_blocks(n):
    early = [(i, j) for i in range(2) for j in range(i, n)] + [(2, 2)]
    late = [(i, j) for i in range(2, n) for j in range(i, n) if (i, j) not in early]
    return early, late


def gram_kernel(n, scale, own_ref, other_ref, p_ref):
    core = lax.rem(lax.axis_index("band"), CORES)
    tiles = B // V
    own, other = split(own_ref[...]), split(other_ref[...])
    hi, lo = (jnp.concatenate([o, t], axis=1) for o, t in zip(own, other))
    for c in range(CORES):

        @pl.when(core == c)
        def _():
            mine = []
            for group in grouped_blocks(n):
                half = len(group) // CORES
                mine += group[c * half : (c + 1) * half]
            for i in sorted({i for i, _ in mine}):
                wanted = [j for k, j in mine if k == i]
                first, end = min(wanted), max(wanted) + 1
                left = (hi[i * B : (i + 1) * B], lo[i * B : (i + 1) * B])
                right = (hi[first * B : end * B], lo[first * B : end * B])
                out = dot3(left, right, ((1,), (1,))) * scale
                for j in wanted:
                    at = mine.index((i, j)) * tiles
                    p_ref[at : at + tiles] = out[:, (j - first) * B : (j - first + 1) * B].reshape(tiles, V, B)


def gram(own, other, columns_all):
    n = own.shape[0] // B
    early, late = grouped_blocks(n)
    vmem = pl.BlockSpec(memory_space=pltpu.VMEM)
    return pl.pallas_call(
        functools.partial(gram_kernel, n, 1.0 / columns_all),
        out_shape=jax.ShapeDtypeStruct(((len(early) + len(late)) // CORES * (B // V), V, B), jnp.float32),
        in_specs=[vmem, vmem],
        out_specs=vmem,
        compiler_params=pltpu.CompilerParams(vmem_limit_bytes=48 << 20),
        name="gram",
    )(own, other)


def exchange_kernel(n, src_ref, own_ref, other_ref, send_sem, recv_sem, pass_send, pass_recv, own_sem):
    me = lax.axis_index("band")
    core = lax.rem(me, CORES)
    partner = {"band": me + 1 - 2 * core}
    barrier = pltpu.get_barrier_semaphore()
    rows, cols = src_ref.shape
    width = cols // n

    def columns(index):
        return src_ref.at[:, pl.ds(pl.multiple_of(index * width, width), width)]

    def band(ref, index):
        return ref.at[pl.ds(pl.multiple_of(index * rows, rows), rows), :]

    def greet(s, carry):
        pl.semaphore_signal(
            barrier, inc=1, device_id={"band": lax.rem(me + s, n)}, device_id_type=MESH
        )
        return carry

    lax.fori_loop(1, n, greet, 0)
    own = pltpu.make_async_copy(columns(me), band(own_ref, me), own_sem)
    own.start()
    pl.semaphore_wait(barrier, n - 1)

    def copy(s, source):
        peer = lax.rem(me + s, n)
        return pltpu.make_async_remote_copy(
            src_ref=columns(peer),
            dst_ref=band(own_ref, source),
            send_sem=send_sem.at[s],
            recv_sem=recv_sem.at[s],
            device_id={"band": peer},
            device_id_type=MESH,
        )

    def hand_over(source):
        return pltpu.make_async_remote_copy(
            src_ref=band(own_ref, source),
            dst_ref=band(other_ref, source),
            send_sem=pass_send.at[source],
            recv_sem=pass_recv.at[source],
            device_id=partner,
            device_id_type=MESH,
        )

    def start(s, carry):
        copy(s, me).start()
        return carry

    def arrive(s, carry):
        source = lax.rem(me - s + n, n)
        copy(s, source).wait_recv()
        hand_over(source).start()
        return carry

    def finish(s, carry):
        copy(s, me).wait_send()
        hand_over(lax.rem(me + s, n)).wait()
        return carry

    lax.fori_loop(1, n, start, 0)
    own.wait()
    hand_over(me).start()
    lax.fori_loop(1, n, arrive, 0)
    lax.fori_loop(1, n, finish, 0)
    hand_over(me).wait()


def exchange(x, n):
    rows, cols = x.shape
    shape = jax.ShapeDtypeStruct((rows * n, cols // n), x.dtype)
    vmem = pl.BlockSpec(memory_space=pltpu.VMEM)
    return pl.pallas_call(
        functools.partial(exchange_kernel, n),
        out_shape=(shape, shape),
        in_specs=[pl.BlockSpec(memory_space=pl.ANY)],
        out_specs=(vmem, vmem),
        scratch_shapes=[pltpu.SemaphoreType.DMA((n,))] * 4 + [pltpu.SemaphoreType.DMA],
        compiler_params=pltpu.CompilerParams(
            collective_id=0, has_side_effects=True, vmem_limit_bytes=48 << 20
        ),
        name="exchange",
    )(x)


CORES, YS, XS, ZS = 2, 4, 4, 8
EARLY, LATE = 0, 1
TOTAL = (256, 320)
HALF = tuple(t // 2 for t in TOTAL)
FIRST = tuple(t // 8 for t in TOTAL)
SECOND = tuple(t // 32 for t in TOTAL)
Z_USED = (8, 5)
CHUNK = tuple(t // z for t, z in zip(SECOND, Z_USED))
COPIES = 30


def coordinates():
    band, ga = lax.axis_index("band"), lax.axis_index("ga")
    core, y = lax.rem(band, CORES), lax.rem(band // CORES, YS)
    x = (band // (CORES * YS)) * 2 + lax.rem(ga, 2)
    return core, x, y, ga // 2


def device(core, x, y, z):
    return {"band": ((x // 2) * YS + y) * CORES + core, "ga": z * 2 + lax.rem(x, 2)}


class Summing:
    def __init__(self, group, p_ref, g_ref, scratch, send, recv):
        self.group, self.p_ref, self.g_ref = group, p_ref, g_ref
        self.acc2, self.acc3, self.got1, self.got2, self.got3 = scratch
        self.send, self.recv = send, recv
        core, x, y, z = self.at = coordinates()
        self.core, self.z = core, z
        self.a = jnp.where(core == 0, y, x)
        self.b = jnp.where(core == 0, x, y)
        self.partner = device(1 - core, x, y, z)
        self.from_p = group * HALF[EARLY]
        base = group * TOTAL[EARLY]
        self.half = base + core * HALF[group]
        self.first = self.half + self.a * FIRST[group]
        self.second = self.first + self.b * SECOND[group]
        self.other_half = base + (1 - core) * HALF[group]
        self.started = []

    def along(self, stage, s):
        core, x, y, z = self.at
        if stage == "z":
            to = lax.rem(z + s, ZS)
            return to, device(core, x, y, to)
        at = self.a if stage == "first" else self.b
        to = lax.rem(at + s, 4)
        on_y = core == (0 if stage == "first" else 1)
        return to, device(core, jnp.where(on_y, x, to), jnp.where(on_y, to, y), z)

    def copy(self, src, dst, index, peer):
        return pltpu.make_async_remote_copy(
            src_ref=src,
            dst_ref=dst,
            send_sem=self.send.at[self.group * COPIES + index],
            recv_sem=self.recv.at[self.group * COPIES + index],
            device_id=peer,
            device_id_type=MESH,
        )

    def start(self, src, dst, index, peer):
        self.copy(src, dst, index, peer).start()
        self.started.append((src.shape[0], index))

    def chunk(self, at, size):
        return self.g_ref.at[pl.ds(at, size)]

    def takes(self, z, then):
        if Z_USED[self.group] == ZS:
            then()
        else:
            pl.when(z < Z_USED[self.group])(then)

    def stage0(self):
        size = FIRST[self.group]
        for s in (2, 1, 3):
            to, peer = self.along("first", s)
            self.start(self.p_ref.at[pl.ds(self.from_p + to * size, size)], self.got1.at[s - 1], s - 1, peer)

    def stage1(self):
        size, step = FIRST[self.group], 8
        for s in range(3):
            self.copy(self.got1.at[s], self.got1.at[s], s, self.partner).wait_recv()

        def add(t, carry):
            at = pl.ds(t * step, step)
            own = self.p_ref[pl.ds(self.from_p + self.a * size + t * step, step)]
            self.acc2[at] = (own + self.got1[0, at]) + (self.got1[1, at] + self.got1[2, at])
            return carry

        lax.fori_loop(0, size // step, add, 0)
        size = SECOND[self.group]
        for s in (2, 1, 3):
            to, peer = self.along("second", s)
            self.start(self.acc2.at[pl.ds(to * size, size)], self.got2.at[s - 1], 2 + s, peer)

    def stage2(self):
        size = SECOND[self.group]
        for s in range(3):
            self.copy(self.got2.at[s], self.got2.at[s], 3 + s, self.partner).wait_recv()
        own = self.acc2[pl.ds(self.b * size, size)]
        self.acc3[...] = (own + self.got2[0]) + (self.got2[1] + self.got2[2])
        size = CHUNK[self.group]
        for s in (4, 3, 5, 2, 6, 1, 7):
            to, peer = self.along("z", s)

            def send():
                self.copy(self.acc3.at[pl.ds(to * size, size)], self.got3.at[s - 1], 5 + s, peer).start()

            self.takes(to, send)

    def stage3(self):
        size = CHUNK[self.group]
        own = self.second + self.z * size

        def total():
            for s in range(1, ZS):
                self.copy(self.got3.at[s - 1], self.got3.at[s - 1], 5 + s, self.partner).wait_recv()
            terms = [self.acc3[pl.ds(self.z * size, size)]] + [self.got3[s] for s in range(ZS - 1)]
            self.g_ref[pl.ds(own, size)] = tree(terms)
            for s in (4, 3, 5, 2, 6, 1, 7):
                to, peer = self.along("z", s)
                self.copy(self.chunk(own, size), self.chunk(own, size), 12 + s, peer).start()

        self.takes(self.z, total)

    def stage4(self):
        size = CHUNK[self.group]
        for s in range(1, ZS):
            sender = lax.rem(self.z + ZS - s, ZS)

            def receive():
                got = self.chunk(self.second + sender * size, size)
                self.copy(got, got, 12 + s, self.partner).wait_recv()

            self.takes(sender, receive)
        mine = self.chunk(self.second, SECOND[self.group])
        for s in (2, 1, 3):
            to, peer = self.along("second", s)
            self.start(mine, mine, 19 + s, peer)

    def stage5(self):
        size = SECOND[self.group]
        for s in range(1, 4):
            got = self.chunk(self.first + lax.rem(self.b + 4 - s, 4) * size, size)
            self.copy(got, got, 19 + s, self.partner).wait_recv()
        mine = self.chunk(self.first, FIRST[self.group])
        for s in (2, 1, 3):
            to, peer = self.along("first", s)
            self.start(mine, mine, 22 + s, peer)
        self.start(mine, mine, 26, self.partner)

    def stage6(self):
        size = FIRST[self.group]
        for s in (1, 3, 2):
            got = self.chunk(self.half + lax.rem(self.a + 4 - s, 4) * size, size)
            self.copy(got, got, 22 + s, self.partner).wait_recv()
            self.start(got, got, 26 + s, self.partner)

    def stage7(self):
        size = FIRST[self.group]
        for s in range(4):
            got = self.chunk(self.other_half + lax.rem(self.b + 4 - s, 4) * size, size)
            self.copy(got, got, 26 + s, self.partner).wait_recv()

    def finish(self):
        for size, index in self.started:
            part = self.chunk(0, size)
            self.copy(part, part, index, self.partner).wait_send()
        size = CHUNK[self.group]
        for s in range(1, ZS):
            to, peer = self.along("z", s)

            def sent():
                part = self.acc3.at[pl.ds(to * size, size)]
                self.copy(part, part, 5 + s, peer).wait_send()

            self.takes(to, sent)

            def sent_back():
                part = self.chunk(self.second, size)
                self.copy(part, part, 12 + s, peer).wait_send()

            self.takes(self.z, sent_back)


def orthonormalize_kernel(
    n, p_ref, c_ref, out_ref, g_ref, a_ref, z_ref, x_ref, hi_ref, lo_ref, lane_ref, row_ref, *rest
):
    early_scratch, late_scratch, (send, recv, send_sem, recv_sem, own_sem) = rest[:5], rest[5:10], rest[10:]
    width = c_ref.shape[1]
    rows_each = out_ref.shape[0]
    bands = n * B // rows_each
    per_panel = B // rows_each
    tiles = B // V
    me = lax.axis_index("band")
    core, x, y, z = coordinates()

    barrier = pltpu.get_barrier_semaphore()

    def greet(s, carry):
        pl.semaphore_signal(
            barrier, inc=1, device_id={"band": lax.rem(me + s, bands)}, device_id_type=MESH
        )
        return carry

    lax.fori_loop(1, bands, greet, 0)
    others = [device(core, lax.rem(x + s, XS), y, z) for s in (1, 3)]
    others += [device(core, x, y, lax.rem(z + s, ZS)) for s in range(1, ZS)]
    for peer in others:
        pl.semaphore_signal(barrier, inc=1, device_id=peer, device_id_type=MESH)
    pl.semaphore_wait(barrier, bands - 1 + len(others))

    early = Summing(EARLY, p_ref, g_ref, early_scratch, send, recv)
    late = Summing(LATE, p_ref, g_ref, late_scratch, send, recv)
    early.stage0()
    late.stage0()
    early.stage1()
    early.stage2()
    late.stage1()
    early.stage3()
    late.stage2()
    early.stage4()
    late.stage3()
    early.stage5()
    late.stage4()
    early.stage6()
    late.stage5()
    early.stage7()

    order = [block for group in grouped_blocks(n) for block in group]
    sub = lax.broadcasted_iota(jnp.int32, (V, B), 0)
    lane = lax.broadcasted_iota(jnp.int32, (V, B), 1)

    def load(panels):
        for i in panels:
            for j in range(i, n):
                at = order.index((i, j)) * tiles
                a_ref[i, :, j * B : (j + 1) * B] = g_ref[at : at + tiles].reshape(B, B)
            a_ref[i, :, n * B :] = c_ref[i * B : (i + 1) * B, :]
            at = order.index((i, i)) * tiles
            on_diagonal = [jnp.where(lane == q * V + sub, g_ref[at + q], 0.0) for q in range(tiles)]
            diagonal = jnp.sum(tree(on_diagonal), axis=0, keepdims=True)
            scale = jnp.broadcast_to(lax.rsqrt(diagonal), (V, B))
            lane_ref[i] = scale
            for q in range(tiles):
                row_ref[i, q * V : (q + 1) * V, :] = jnp.take_along_axis(scale, q * V + sub, axis=1)

    def remote(peer, sender):
        return pltpu.make_async_remote_copy(
            src_ref=x_ref.at[pl.ds(peer * rows_each, rows_each), :],
            dst_ref=out_ref.at[:, pl.ds(pl.multiple_of(sender * width, width), width)],
            send_sem=send_sem.at[peer],
            recv_sem=recv_sem.at[sender],
            device_id={"band": peer},
            device_id_type=MESH,
        )

    own = pltpu.make_async_copy(
        x_ref.at[pl.ds(me * rows_each, rows_each), :],
        out_ref.at[:, pl.ds(pl.multiple_of(me * width, width), width)],
        own_sem,
    )

    load([0, 1])

    def step(i, carry):
        @pl.when(i == 1)
        def _():
            late.stage6()

        @pl.when(i == 2)
        def _():
            late.stage7()
            load(range(2, n))
            for j in range(2, n):
                high, low = [hi_ref[k] for k in range(2)], [lo_ref[k] for k in range(2)]
                left = tuple(jnp.concatenate([h[:, j * B : (j + 1) * B] for h in part]) for part in (high, low))
                right = tuple(jnp.concatenate([h[:, j * B :] for h in part]) for part in (high, low))
                a_ref[j, :, j * B :] -= dot3(left, right, ((0,), (0,)))

        here = pl.multiple_of(i * B, B)
        lanes = lane_ref[i]
        rows = [
            a_ref[i, q * V : (q + 1) * V, pl.ds(here, B)] * row_ref[i, q * V : (q + 1) * V, :] * lanes
            for q in range(tiles)
        ]
        for q, inverse in enumerate(factor_inverse(rows)):
            z_ref[q * V : (q + 1) * V, :] = inverse * lanes
        for k in range(n):

            @pl.when(i == k)
            def _():
                panel = dot3(split(z_ref[...]), split(a_ref[k, :, (k + 1) * B :]), ((1,), (0,)))
                x_ref[k * B : (k + 1) * B, :] = panel[:, panel.shape[1] - width :]
                for peer in range(k * per_panel, (k + 1) * per_panel):

                    @pl.when(peer != me)
                    def _():
                        remote(peer, me).start()

                    @pl.when(peer == me)
                    def _():
                        own.start()

                high, low = split(panel)
                if k < 2:
                    hi_ref[k, :, (k + 1) * B :] = high
                    lo_ref[k, :, (k + 1) * B :] = low
                for j in range(k + 1, 2 if k < 2 else n):
                    at_j = (j - k - 1) * B
                    left = (high[:, at_j : at_j + B], low[:, at_j : at_j + B])
                    right = (high[:, at_j:], low[:, at_j:])
                    a_ref[j, :, j * B :] -= dot3(left, right, ((0,), (0,)))

        return carry

    lax.fori_loop(0, n, step, 0)
    early.finish()
    late.finish()
    own.wait()
    for other in range(bands):

        @pl.when(other != me)
        def _():
            remote(other, me).wait_send()
            remote(other, other).wait_recv()


def orthonormalize(p, c, bands):
    rows, width = c.shape
    n = rows // B
    vmem = pl.BlockSpec(memory_space=pltpu.VMEM)
    tiles = lambda *shape: pltpu.VMEM((*shape, V, B), jnp.float32)
    summing = []
    for g in (EARLY, LATE):
        summing += [tiles(FIRST[g]), tiles(SECOND[g]), tiles(3, FIRST[g]), tiles(3, SECOND[g])]
        summing += [tiles(ZS - 1, CHUNK[g])]
    return pl.pallas_call(
        functools.partial(orthonormalize_kernel, n),
        out_shape=jax.ShapeDtypeStruct((rows // bands, width * bands), jnp.float32),
        in_specs=[vmem, vmem],
        out_specs=vmem,
        scratch_shapes=[
            tiles(sum(TOTAL)),
            pltpu.VMEM((n, B, n * B + width), jnp.float32),
            pltpu.VMEM((B, B), jnp.float32),
            pltpu.VMEM((rows, width), jnp.float32),
            pltpu.VMEM((2, B, n * B + width), jnp.bfloat16),
            pltpu.VMEM((2, B, n * B + width), jnp.bfloat16),
            tiles(n),
            pltpu.VMEM((n, B, B), jnp.float32),
            *summing,
            pltpu.SemaphoreType.DMA((2 * COPIES,)),
            pltpu.SemaphoreType.DMA((2 * COPIES,)),
            pltpu.SemaphoreType.DMA((bands,)),
            pltpu.SemaphoreType.DMA((bands,)),
            pltpu.SemaphoreType.DMA,
        ],
        compiler_params=pltpu.CompilerParams(
            collective_id=1, has_side_effects=True, vmem_limit_bytes=48 << 20
        ),
        name="orthonormalize",
    )(p, c)


def local(coeffs):
    bands = lax.axis_size("band")
    columns_all = coeffs.shape[1] * lax.axis_size("ga")
    own, other = exchange(coeffs, bands)
    return orthonormalize(gram(own, other, columns_all), own, bands)


def solution(mesh):
    return jax.shard_map(
        local,
        mesh=mesh,
        in_specs=(P("band", "ga"),),
        out_specs=P("band", "ga"),
        check_vma=False,
    )
```

```python
import functools

import jax
import jax.numpy as jnp
from jax import lax
from jax.experimental import pallas as pl
from jax.experimental.pallas import tpu as pltpu
from jax.sharding import PartitionSpec as P

MESH = pl.DeviceIdType.MESH

B = 128
V = 8


def split(x):
    hi = x.astype(jnp.bfloat16)
    return hi, (x - hi.astype(jnp.float32)).astype(jnp.bfloat16)


def dot3(a, b, dims):
    (ca,), (cb,) = dims
    ah, al = a
    bh, bl = b
    left = jnp.concatenate([ah, al, ah], axis=ca)
    right = jnp.concatenate([bh, bh, bl], axis=cb)
    return lax.dot_general(left, right, (dims, ((), ())), preferred_element_type=jnp.float32)


def lane_col(t, c):
    return jnp.take_along_axis(t, jnp.full((V, B), c, jnp.int32), axis=1)


def sub_row(t, k):
    return jnp.broadcast_to(t[k : k + 1, :], (V, B))


def tree(m):
    while len(m) > 1:
        m = [m[e] + m[e + 1] if e + 1 < len(m) else m[e] for e in range(0, len(m), 2)]
    return m[0]


def factor_inverse(rows):
    n = len(rows)
    rows = list(rows)
    sub = lax.broadcasted_iota(jnp.int32, (V, B), 0)
    lane = lax.broadcasted_iota(jnp.int32, (V, B), 1)
    out = []
    cols = [lane_col(rows[0], k) for k in range(V)]
    for p in range(n):
        c0 = p * V
        last = p == n - 1
        in_block = (lane >= c0) & (lane < c0 + V)
        t = jnp.where(in_block, jnp.where(lane - c0 == sub, 1.0, 0.0), rows[p])
        f = jnp.where(lane < c0 + V, t, 0.0)
        pivots = None
        below_m = {q: [lane_col(rows[q], c0 + k) for k in range(V)] for q in range(p + 1, n)}
        if not last:
            a = list(below_m[p + 1])
            ahead = [lane_col(rows[p + 1], c0 + V + k) for k in range(V)]
        for k in range(0, V, 2):
            h1, h2 = sub == k, sub == k + 1
            here = h1 | h2
            d11, d12, d22 = sub_row(cols[k], k), sub_row(cols[k + 1], k), sub_row(cols[k + 1], k + 1)
            det = d11 * d22 - d12 * d12
            r = 1.0 / det
            m1, m2 = jnp.where(here, 0.0, cols[k]), jnp.where(here, 0.0, cols[k + 1])

            def solve(col):
                v1, v2 = sub_row(col, k), sub_row(col, k + 1)
                return (d22 * v1 - d12 * v2) * r, (d11 * v2 - d12 * v1) * r

            def eliminate(col):
                u1, u2 = solve(col)
                return jnp.where(h1, u1, jnp.where(h2, u2, col - (m1 * u1 + m2 * u2))), u1, u2

            for j in range(k + 2, V):
                cols[j], u1, u2 = eliminate(cols[j])
                if not last:
                    a[j] = a[j] - (a[k] * u1 + a[k + 1] * u2)
            if not last:
                s1 = (d22 * a[k] - d12 * a[k + 1]) * r
                s2 = (d11 * a[k + 1] - d12 * a[k]) * r
                for j in range(V):
                    ahead[j] = ahead[j] - (s1 * sub_row(a[k], j) + s2 * sub_row(a[k + 1], j))
            q = 1.0 / d11
            ratio = d12 * q
            f1 = sub_row(f, k)
            f2 = sub_row(f, k + 1) - ratio * f1
            g2 = d11 * r
            g1 = q
            below = sub > k + 1
            b1 = jnp.where(below, cols[k], 0.0)
            b2 = jnp.where(below, cols[k + 1], 0.0)
            l2 = b2 - b1 * ratio
            f = jnp.where(h2, f2, f - b1 * (f1 * g1) - l2 * (f2 * g2))
            t, _, _ = eliminate(t)
            scale = jnp.where(h1, g1, g2)
            pivots = scale if pivots is None else jnp.where(here, scale, pivots)
        out.append(f * jnp.sqrt(pivots))
        if last:
            break
        cols = ahead
        w = [sub_row(t, k) for k in range(V)]
        for q in range(p + 1, n):
            acc = jnp.where(in_block, 0.0, rows[q])
            rows[q] = acc - tree([below_m[q][k] * w[k] for k in range(V)])
    return out


CORES, YS, XS, ZS = 2, 4, 4, 8
TOTAL = (128, 128, 320)
HALF = tuple(t // 2 for t in TOTAL)
FIRST = tuple(t // 8 for t in TOTAL)
SECOND = tuple(t // 32 for t in TOTAL)
Z_USED = (0, 0, 5)
CHUNK = tuple(t // max(z, 1) for t, z in zip(SECOND, Z_USED))
COPIES = 30


def grouped_blocks(n):
    first = [(0, j) for j in range(n)]
    second = [(1, j) for j in range(1, n)] + [(2, 2)]
    rest = [(i, j) for i in range(2, n) for j in range(i, n) if (i, j) != (2, 2)]
    return first, second, rest


def coordinates():
    band, ga = lax.axis_index("band"), lax.axis_index("ga")
    core, y = lax.rem(band, CORES), lax.rem(band // CORES, YS)
    x = (band // (CORES * YS)) * 2 + lax.rem(ga, 2)
    return core, x, y, ga // 2


def device(core, x, y, z):
    return {"band": ((x // 2) * YS + y) * CORES + core, "ga": z * 2 + lax.rem(x, 2)}


class Summing:
    def __init__(self, group, p_ref, g_ref, scratch, send, recv):
        self.group, self.p_ref, self.g_ref = group, p_ref, g_ref
        self.acc2, self.acc3, self.got1, self.got2, self.got3 = scratch
        self.send, self.recv = send, recv
        self.direct = Z_USED[group] == 0
        core, x, y, z = self.at = coordinates()
        self.core, self.z = core, z
        self.a = jnp.where(core == 0, y, x)
        self.b = jnp.where(core == 0, x, y)
        self.partner = device(1 - core, x, y, z)
        self.from_p = sum(HALF[:group])
        base = sum(TOTAL[:group])
        self.half = base + core * HALF[group]
        self.first = self.half + self.a * FIRST[group]
        self.second = self.first + self.b * SECOND[group]
        self.other_half = base + (1 - core) * HALF[group]
        self.started = []

    def along(self, stage, s):
        core, x, y, z = self.at
        if stage == "z":
            to = lax.rem(z + s, ZS)
            return to, device(core, x, y, to)
        at = self.a if stage == "first" else self.b
        to = lax.rem(at + s, 4)
        on_y = core == (0 if stage == "first" else 1)
        return to, device(core, jnp.where(on_y, x, to), jnp.where(on_y, to, y), z)

    def copy(self, src, dst, index, peer):
        return pltpu.make_async_remote_copy(
            src_ref=src,
            dst_ref=dst,
            send_sem=self.send.at[self.group * COPIES + index],
            recv_sem=self.recv.at[self.group * COPIES + index],
            device_id=peer,
            device_id_type=MESH,
        )

    def start(self, src, dst, index, peer):
        self.copy(src, dst, index, peer).start()
        self.started.append((src.shape[0], index))

    def chunk(self, at, size):
        return self.g_ref.at[pl.ds(at, size)]

    def takes(self, z, then):
        if Z_USED[self.group] == ZS:
            then()
        else:
            pl.when(z < Z_USED[self.group])(then)

    def stage0(self):
        size = FIRST[self.group]
        for s in (2, 1, 3):
            to, peer = self.along("first", s)
            self.start(self.p_ref.at[pl.ds(self.from_p + to * size, size)], self.got1.at[s - 1], s - 1, peer)

    def stage1(self):
        size, step = FIRST[self.group], 8
        for s in range(3):
            self.copy(self.got1.at[s], self.got1.at[s], s, self.partner).wait_recv()

        def add(t, carry):
            at = pl.ds(t * step, step)
            own = self.p_ref[pl.ds(self.from_p + self.a * size + t * step, step)]
            self.acc2[at] = (own + self.got1[0, at]) + (self.got1[1, at] + self.got1[2, at])
            return carry

        lax.fori_loop(0, size // step, add, 0)
        size = SECOND[self.group]
        for s in (2, 1, 3):
            to, peer = self.along("second", s)
            self.start(self.acc2.at[pl.ds(to * size, size)], self.got2.at[s - 1], 2 + s, peer)

    def across_z(self):
        size = SECOND[self.group]
        self.got3[pl.ds(self.z, 1)] = self.acc3[...][None]
        for s in (4, 3, 5, 2, 6, 1, 7):
            to, peer = self.along("z", s)
            self.start(self.acc3, self.got3.at[self.z], 5 + s, peer)

    def stage2(self):
        size = SECOND[self.group]
        for s in range(3):
            self.copy(self.got2.at[s], self.got2.at[s], 3 + s, self.partner).wait_recv()
        own = self.acc2[pl.ds(self.b * size, size)]
        self.acc3[...] = (own + self.got2[0]) + (self.got2[1] + self.got2[2])
        if self.direct:
            self.across_z()
            return
        size = CHUNK[self.group]
        for s in (4, 3, 5, 2, 6, 1, 7):
            to, peer = self.along("z", s)

            def send():
                self.copy(self.acc3.at[pl.ds(to * size, size)], self.got3.at[s - 1], 5 + s, peer).start()

            self.takes(to, send)

    def stage3(self):
        if self.direct:
            for s in range(1, ZS):
                self.copy(self.acc3, self.got3.at[0], 5 + s, self.partner).wait_recv()
            self.g_ref[pl.ds(self.second, SECOND[self.group])] = tree([self.got3[k] for k in range(ZS)])
            self.back()
            return
        size = CHUNK[self.group]
        own = self.second + self.z * size

        def total():
            for s in range(1, ZS):
                self.copy(self.got3.at[s - 1], self.got3.at[s - 1], 5 + s, self.partner).wait_recv()
            terms = [self.acc3[pl.ds(self.z * size, size)]] + [self.got3[s] for s in range(ZS - 1)]
            self.g_ref[pl.ds(own, size)] = tree(terms)
            for s in (4, 3, 5, 2, 6, 1, 7):
                to, peer = self.along("z", s)
                self.copy(self.chunk(own, size), self.chunk(own, size), 12 + s, peer).start()

        self.takes(self.z, total)

    def stage4(self):
        size = CHUNK[self.group]
        for s in range(1, ZS):
            sender = lax.rem(self.z + ZS - s, ZS)

            def receive():
                got = self.chunk(self.second + sender * size, size)
                self.copy(got, got, 12 + s, self.partner).wait_recv()

            self.takes(sender, receive)
        self.back()

    def back(self):
        mine = self.chunk(self.second, SECOND[self.group])
        for s in (2, 1, 3):
            to, peer = self.along("second", s)
            self.start(mine, mine, 19 + s, peer)

    def stage5(self):
        size = SECOND[self.group]
        for s in range(1, 4):
            got = self.chunk(self.first + lax.rem(self.b + 4 - s, 4) * size, size)
            self.copy(got, got, 19 + s, self.partner).wait_recv()
        mine = self.chunk(self.first, FIRST[self.group])
        for s in (2, 1, 3):
            to, peer = self.along("first", s)
            self.start(mine, mine, 22 + s, peer)
        self.start(mine, mine, 26, self.partner)

    def stage6(self):
        size = FIRST[self.group]
        for s in (1, 3, 2):
            got = self.chunk(self.half + lax.rem(self.a + 4 - s, 4) * size, size)
            self.copy(got, got, 22 + s, self.partner).wait_recv()
            self.start(got, got, 26 + s, self.partner)

    def stage7(self):
        size = FIRST[self.group]
        for s in range(4):
            got = self.chunk(self.other_half + lax.rem(self.b + 4 - s, 4) * size, size)
            self.copy(got, got, 26 + s, self.partner).wait_recv()

    def finish(self):
        for size, index in self.started:
            part = self.chunk(0, size)
            self.copy(part, part, index, self.partner).wait_send()
        if self.direct:
            return
        size = CHUNK[self.group]
        for s in range(1, ZS):
            to, peer = self.along("z", s)

            def sent():
                part = self.acc3.at[pl.ds(to * size, size)]
                self.copy(part, part, 5 + s, peer).wait_send()

            self.takes(to, sent)

            def sent_back():
                part = self.chunk(self.second, size)
                self.copy(part, part, 12 + s, peer).wait_send()

            self.takes(self.z, sent_back)


def orthonormalize_kernel(n, scale, src_ref, out_ref, *scratch):
    (own_ref, other_ref, held_hi, held_lo, p_ref, g_ref, cur_ref, d_ref, z_ref, x_ref, hi_ref, lo_ref, lane_ref) = scratch[:13]
    groups_scratch = [scratch[13 + 5 * g : 18 + 5 * g] for g in range(3)]
    (send, recv, x_send, x_recv, in_send, in_recv, pass_send, pass_recv, own_sem) = scratch[28:]
    rows_each, width = src_ref.shape[0], own_ref.shape[1]
    bands = src_ref.shape[1] // width
    per_panel = B // rows_each
    tiles = B // V
    me = lax.axis_index("band")
    core, x, y, z = coordinates()
    partner = device(1 - core, x, y, z)

    barrier = pltpu.get_barrier_semaphore()

    def greet(s, carry):
        pl.semaphore_signal(
            barrier, inc=1, device_id={"band": lax.rem(me + s, bands)}, device_id_type=MESH
        )
        return carry

    others = [device(core, x, y, lax.rem(z + s, ZS)) for s in range(1, ZS)]
    others += [device(core, lax.rem(x + s, XS), y, z) for s in (1, 3)]
    for peer in others:
        pl.semaphore_signal(barrier, inc=1, device_id=peer, device_id_type=MESH)
    lax.fori_loop(1, bands, greet, 0)

    def columns(ref, index):
        return ref.at[:, pl.ds(pl.multiple_of(index * width, width), width)]

    def band(ref, index):
        return ref.at[pl.ds(pl.multiple_of(index * rows_each, rows_each), rows_each), :]

    mine = pltpu.make_async_copy(columns(src_ref, me), band(own_ref, me), own_sem)
    mine.start()
    pl.semaphore_wait(barrier, bands - 1 + len(others))

    def bring(s, source):
        peer = lax.rem(me + s, bands)
        return pltpu.make_async_remote_copy(
            src_ref=columns(src_ref, peer),
            dst_ref=band(own_ref, source),
            send_sem=in_send.at[s],
            recv_sem=in_recv.at[s],
            device_id={"band": peer},
            device_id_type=MESH,
        )

    def hand_over(source):
        return pltpu.make_async_remote_copy(
            src_ref=band(own_ref, source),
            dst_ref=band(other_ref, source),
            send_sem=pass_send.at[source],
            recv_sem=pass_recv.at[source],
            device_id=partner,
            device_id_type=MESH,
        )

    def keep(ref, source, at):
        rows = pl.ds(pl.multiple_of(source * rows_each, rows_each), rows_each)
        high, low = split(ref[rows, :])
        held_hi[rows, at : at + width] = high
        held_lo[rows, at : at + width] = low

    def start(s, carry):
        bring(s, me).start()
        return carry

    def arrive(s, carry):
        source = lax.rem(me - s + bands, bands)
        bring(s, source).wait_recv()
        hand_over(source).start()
        keep(own_ref, source, 0)
        return carry

    def finish(s, carry):
        source = lax.rem(me + 1 - 2 * core - s + bands, bands)
        hand_over(source).wait_recv()
        keep(other_ref, source, width)
        return carry

    def sent(s, carry):
        bring(s, me).wait_send()
        hand_over(lax.rem(me + s, bands)).wait_send()
        return carry

    lax.fori_loop(1, bands, start, 0)
    mine.wait()
    hand_over(me).start()
    keep(own_ref, me, 0)
    lax.fori_loop(1, bands, arrive, 0)
    lax.fori_loop(0, bands, finish, 0)

    groups = grouped_blocks(n)

    def multiply(g):
        half = len(groups[g]) // CORES
        for c in range(CORES):

            @pl.when(core == c)
            def _():
                blocks = groups[g][c * half : (c + 1) * half]
                for i in sorted({i for i, _ in blocks}):
                    wanted = [j for k, j in blocks if k == i]
                    first, end = min(wanted), max(wanted) + 1
                    left = (held_hi[i * B : (i + 1) * B], held_lo[i * B : (i + 1) * B])
                    right = (held_hi[first * B : end * B], held_lo[first * B : end * B])
                    out = dot3(left, right, ((1,), (1,))) * scale
                    for j in wanted:
                        at = sum(HALF[:g]) + blocks.index((i, j)) * tiles
                        block = out[:, (j - first) * B : (j - first + 1) * B]
                        p_ref[at : at + tiles] = block.reshape(tiles, V, B)

    one, two, three = (Summing(g, p_ref, g_ref, groups_scratch[g], send, recv) for g in range(3))
    multiply(0)
    one.stage0()
    multiply(1)
    two.stage0()
    multiply(2)
    three.stage0()
    one.stage1()
    two.stage1()
    one.stage2()
    three.stage1()
    two.stage2()
    one.stage3()
    three.stage2()
    two.stage3()
    one.stage5()
    three.stage3()
    two.stage5()
    one.stage6()
    three.stage4()
    two.stage6()
    one.stage7()
    three.stage5()

    order = [block for group in groups for block in group]
    sub = lax.broadcasted_iota(jnp.int32, (V, B), 0)
    lane = lax.broadcasted_iota(jnp.int32, (V, B), 1)

    def prepare(k):
        at = order.index((k, k)) * tiles
        on_diagonal = [jnp.where(lane == q * V + sub, g_ref[at + q], 0.0) for q in range(tiles)]
        diagonal = jnp.sum(tree(on_diagonal), axis=0, keepdims=True)
        lanes = jnp.broadcast_to(lax.rsqrt(diagonal), (V, B))
        lane_ref[...] = lanes
        taken = None
        if k:
            left = (hi_ref[: k * B, k * B : (k + 1) * B], lo_ref[: k * B, k * B : (k + 1) * B])
            right = (hi_ref[: k * B, k * B :], lo_ref[: k * B, k * B :])
            taken = dot3(left, right, ((0,), (0,)))
        for j in range(k, n + width // B):
            if j < n:
                at = order.index((k, j)) * tiles
                block = g_ref[at : at + tiles].reshape(B, B)
            else:
                block = own_ref[k * B : (k + 1) * B, (j - n) * B : (j - n + 1) * B]
            if k:
                block = block - taken[:, (j - k) * B : (j - k + 1) * B]
            if j > k:
                cur_ref[:, j * B : (j + 1) * B] = block
                continue
            for q in range(tiles):
                rows = jnp.take_along_axis(lanes, q * V + sub, axis=1)
                d_ref[q * V : (q + 1) * V, :] = block[q * V : (q + 1) * V] * rows * lanes

    def remote(peer, sender):
        return pltpu.make_async_remote_copy(
            src_ref=x_ref.at[pl.ds(peer * rows_each, rows_each), :],
            dst_ref=columns(out_ref, sender),
            send_sem=x_send.at[peer],
            recv_sem=x_recv.at[sender],
            device_id={"band": peer},
            device_id_type=MESH,
        )

    stays = pltpu.make_async_copy(band(x_ref, me), columns(out_ref, me), own_sem)

    def step(i, carry):
        for k in range(n):

            @pl.when(i == k)
            def _():
                if k == 1:
                    two.stage7()
                if k == 2:
                    three.stage7()
                prepare(k)

        rows = [d_ref[q * V : (q + 1) * V, :] for q in range(tiles)]
        lanes = lane_ref[...]
        for q, inverse in enumerate(factor_inverse(rows)):
            z_ref[q * V : (q + 1) * V, :] = inverse * lanes
        for k in range(n):

            @pl.when(i == k)
            def _():
                if k == 1:
                    three.stage6()
                panel = dot3(split(z_ref[...]), split(cur_ref[:, (k + 1) * B :]), ((1,), (0,)))
                x_ref[k * B : (k + 1) * B, :] = panel[:, panel.shape[1] - width :]
                for peer in range(k * per_panel, (k + 1) * per_panel):

                    @pl.when(peer != me)
                    def _():
                        remote(peer, me).start()

                    @pl.when(peer == me)
                    def _():
                        stays.start()

                if k < n - 1:
                    high, low = split(panel)
                    hi_ref[k * B : (k + 1) * B, (k + 1) * B :] = high
                    lo_ref[k * B : (k + 1) * B, (k + 1) * B :] = low

        return carry

    lax.fori_loop(0, n, step, 0)
    lax.fori_loop(1, bands, sent, 0)
    hand_over(me).wait_send()
    for group in (one, two, three):
        group.finish()
    stays.wait()
    for other in range(bands):

        @pl.when(other != me)
        def _():
            remote(other, me).wait_send()
            remote(other, other).wait_recv()


def orthonormalize(coeffs, bands, columns_all):
    rows_each, columns = coeffs.shape
    rows, width = rows_each * bands, columns // bands
    n = rows // B
    tiles = lambda *shape: pltpu.VMEM((*shape, V, B), jnp.float32)
    whole = n * B + width
    summing = []
    for g in range(3):
        summing += [tiles(FIRST[g]), tiles(SECOND[g]), tiles(3, FIRST[g]), tiles(3, SECOND[g])]
        summing += [tiles(ZS - 1, CHUNK[g]) if Z_USED[g] else tiles(ZS, SECOND[g])]
    return pl.pallas_call(
        functools.partial(orthonormalize_kernel, n, 1.0 / columns_all),
        out_shape=jax.ShapeDtypeStruct(coeffs.shape, jnp.float32),
        in_specs=[pl.BlockSpec(memory_space=pltpu.HBM)],
        out_specs=pl.BlockSpec(memory_space=pltpu.VMEM),
        scratch_shapes=[
            pltpu.VMEM((rows, width), jnp.float32),
            pltpu.VMEM((rows, width), jnp.float32),
            pltpu.VMEM((rows, CORES * width), jnp.bfloat16),
            pltpu.VMEM((rows, CORES * width), jnp.bfloat16),
            tiles(sum(HALF)),
            tiles(sum(TOTAL)),
            pltpu.VMEM((B, whole), jnp.float32),
            pltpu.VMEM((B, B), jnp.float32),
            pltpu.VMEM((B, B), jnp.float32),
            pltpu.VMEM((rows, width), jnp.float32),
            pltpu.VMEM((rows, whole), jnp.bfloat16),
            pltpu.VMEM((rows, whole), jnp.bfloat16),
            pltpu.VMEM((V, B), jnp.float32),
            *summing,
            pltpu.SemaphoreType.DMA((3 * COPIES,)),
            pltpu.SemaphoreType.DMA((3 * COPIES,)),
            *[pltpu.SemaphoreType.DMA((bands,))] * 6,
            pltpu.SemaphoreType.DMA,
        ],
        compiler_params=pltpu.CompilerParams(
            collective_id=0, has_side_effects=True, vmem_limit_bytes=40 << 20
        ),
        name="orthonormalize",
    )(coeffs)


def local(coeffs):
    bands = lax.axis_size("band")
    return orthonormalize(coeffs, bands, coeffs.shape[1] * lax.axis_size("ga"))


def solution(mesh):
    return jax.shard_map(
        local,
        mesh=mesh,
        in_specs=(P("band", "ga"),),
        out_specs=P("band", "ga"),
        check_vma=False,
    )
```

```python
import functools

import jax
import jax.numpy as jnp
from jax import lax
from jax.experimental import pallas as pl
from jax.experimental.pallas import tpu as pltpu
from jax.sharding import PartitionSpec as P

MESH = pl.DeviceIdType.MESH

B = 128
V = 8


def split(x):
    hi = x.astype(jnp.bfloat16)
    return hi, (x - hi.astype(jnp.float32)).astype(jnp.bfloat16)


def dot3(a, b, dims):
    (ca,), (cb,) = dims
    ah, al = a
    bh, bl = b
    left = jnp.concatenate([ah, al, ah], axis=ca)
    right = jnp.concatenate([bh, bh, bl], axis=cb)
    return lax.dot_general(left, right, (dims, ((), ())), preferred_element_type=jnp.float32)


def lane_col(t, c):
    return jnp.take_along_axis(t, jnp.full((V, B), c, jnp.int32), axis=1)


def sub_row(t, k):
    return jnp.broadcast_to(t[k : k + 1, :], (V, B))


def tree(m):
    while len(m) > 1:
        m = [m[e] + m[e + 1] if e + 1 < len(m) else m[e] for e in range(0, len(m), 2)]
    return m[0]


def factor_inverse(rows):
    n = len(rows)
    rows = list(rows)
    sub = lax.broadcasted_iota(jnp.int32, (V, B), 0)
    lane = lax.broadcasted_iota(jnp.int32, (V, B), 1)
    out = []
    cols = [lane_col(rows[0], k) for k in range(V)]
    for p in range(n):
        c0 = p * V
        last = p == n - 1
        in_block = (lane >= c0) & (lane < c0 + V)
        t = jnp.where(in_block, jnp.where(lane - c0 == sub, 1.0, 0.0), rows[p])
        f = jnp.where(lane < c0 + V, t, 0.0)
        pivots = None
        below_m = {q: [lane_col(rows[q], c0 + k) for k in range(V)] for q in range(p + 1, n)}
        if not last:
            a = list(below_m[p + 1])
            ahead = [lane_col(rows[p + 1], c0 + V + k) for k in range(V)]
        for k in range(0, V, 2):
            h1, h2 = sub == k, sub == k + 1
            here = h1 | h2
            d11, d12, d22 = sub_row(cols[k], k), sub_row(cols[k + 1], k), sub_row(cols[k + 1], k + 1)
            det = d11 * d22 - d12 * d12
            r = 1.0 / det
            m1, m2 = jnp.where(here, 0.0, cols[k]), jnp.where(here, 0.0, cols[k + 1])

            def solve(col):
                v1, v2 = sub_row(col, k), sub_row(col, k + 1)
                return (d22 * v1 - d12 * v2) * r, (d11 * v2 - d12 * v1) * r

            def eliminate(col):
                u1, u2 = solve(col)
                return jnp.where(h1, u1, jnp.where(h2, u2, col - (m1 * u1 + m2 * u2))), u1, u2

            for j in range(k + 2, V):
                cols[j], u1, u2 = eliminate(cols[j])
                if not last:
                    a[j] = a[j] - (a[k] * u1 + a[k + 1] * u2)
            if not last:
                s1 = (d22 * a[k] - d12 * a[k + 1]) * r
                s2 = (d11 * a[k + 1] - d12 * a[k]) * r
                for j in range(V):
                    ahead[j] = ahead[j] - (s1 * sub_row(a[k], j) + s2 * sub_row(a[k + 1], j))
            q = 1.0 / d11
            ratio = d12 * q
            f1 = sub_row(f, k)
            f2 = sub_row(f, k + 1) - ratio * f1
            g2 = d11 * r
            g1 = q
            below = sub > k + 1
            b1 = jnp.where(below, cols[k], 0.0)
            b2 = jnp.where(below, cols[k + 1], 0.0)
            l2 = b2 - b1 * ratio
            f = jnp.where(h2, f2, f - b1 * (f1 * g1) - l2 * (f2 * g2))
            t, _, _ = eliminate(t)
            scale = jnp.where(h1, g1, g2)
            pivots = scale if pivots is None else jnp.where(here, scale, pivots)
        out.append(f * jnp.sqrt(pivots))
        if last:
            break
        cols = ahead
        w = [sub_row(t, k) for k in range(V)]
        for q in range(p + 1, n):
            acc = jnp.where(in_block, 0.0, rows[q])
            rows[q] = acc - tree([below_m[q][k] * w[k] for k in range(V)])
    return out


CORES, YS, XS, ZS = 2, 4, 4, 8
TOTAL = (128, 224, 224)
HALF = tuple(t // 2 for t in TOTAL)
FIRST = tuple(t // 8 for t in TOTAL)
SECOND = tuple(t // 32 for t in TOTAL)
Z_USED = (0, 0, 7)
CHUNK = tuple(t // max(z, 1) for t, z in zip(SECOND, Z_USED))
COPIES = 30


def grouped_blocks(n):
    first = [(0, j) for j in range(n)]
    second = [(i, j) for i in (1, 2) for j in range(i, n)] + [(3, 3)]
    rest = [(i, j) for i in range(3, n) for j in range(i, n) if (i, j) != (3, 3)]
    return first, second, rest


def coordinates():
    band, ga = lax.axis_index("band"), lax.axis_index("ga")
    core, y = lax.rem(band, CORES), lax.rem(band // CORES, YS)
    x = (band // (CORES * YS)) * 2 + lax.rem(ga, 2)
    return core, x, y, ga // 2


def device(core, x, y, z):
    return {"band": ((x // 2) * YS + y) * CORES + core, "ga": z * 2 + lax.rem(x, 2)}


class Summing:
    def __init__(self, group, p_ref, g_ref, scratch, send, recv):
        self.group, self.p_ref, self.g_ref = group, p_ref, g_ref
        self.acc2, self.acc3, self.got1, self.got2, self.got3 = scratch
        self.send, self.recv = send, recv
        self.direct = Z_USED[group] == 0
        core, x, y, z = self.at = coordinates()
        self.core, self.z = core, z
        self.a = jnp.where(core == 0, y, x)
        self.b = jnp.where(core == 0, x, y)
        self.partner = device(1 - core, x, y, z)
        self.from_p = sum(HALF[:group])
        base = sum(TOTAL[:group])
        self.half = base + core * HALF[group]
        self.first = self.half + self.a * FIRST[group]
        self.second = self.first + self.b * SECOND[group]
        self.other_half = base + (1 - core) * HALF[group]
        self.started = []

    def along(self, stage, s):
        core, x, y, z = self.at
        if stage == "z":
            to = lax.rem(z + s, ZS)
            return to, device(core, x, y, to)
        at = self.a if stage == "first" else self.b
        to = lax.rem(at + s, 4)
        on_y = core == (0 if stage == "first" else 1)
        return to, device(core, jnp.where(on_y, x, to), jnp.where(on_y, to, y), z)

    def copy(self, src, dst, index, peer):
        return pltpu.make_async_remote_copy(
            src_ref=src,
            dst_ref=dst,
            send_sem=self.send.at[self.group * COPIES + index],
            recv_sem=self.recv.at[self.group * COPIES + index],
            device_id=peer,
            device_id_type=MESH,
        )

    def start(self, src, dst, index, peer):
        self.copy(src, dst, index, peer).start()
        self.started.append((src.shape[0], index))

    def chunk(self, at, size):
        return self.g_ref.at[pl.ds(at, size)]

    def takes(self, z, then):
        if Z_USED[self.group] == ZS:
            then()
        else:
            pl.when(z < Z_USED[self.group])(then)

    def stage0(self):
        size = FIRST[self.group]
        for s in (2, 1, 3):
            to, peer = self.along("first", s)
            self.start(self.p_ref.at[pl.ds(self.from_p + to * size, size)], self.got1.at[s - 1], s - 1, peer)

    def stage1(self):
        size, step = FIRST[self.group], 4
        for s in range(3):
            self.copy(self.got1.at[s], self.got1.at[s], s, self.partner).wait_recv()

        def add(t, carry):
            at = pl.ds(t * step, step)
            own = self.p_ref[pl.ds(self.from_p + self.a * size + t * step, step)]
            self.acc2[at] = (own + self.got1[0, at]) + (self.got1[1, at] + self.got1[2, at])
            return carry

        lax.fori_loop(0, size // step, add, 0)
        size = SECOND[self.group]
        for s in (2, 1, 3):
            to, peer = self.along("second", s)
            self.start(self.acc2.at[pl.ds(to * size, size)], self.got2.at[s - 1], 2 + s, peer)

    def across_z(self):
        size = SECOND[self.group]
        self.got3[pl.ds(self.z, 1)] = self.acc3[...][None]
        for s in (4, 3, 5, 2, 6, 1, 7):
            to, peer = self.along("z", s)
            self.start(self.acc3, self.got3.at[self.z], 5 + s, peer)

    def stage2(self):
        size = SECOND[self.group]
        for s in range(3):
            self.copy(self.got2.at[s], self.got2.at[s], 3 + s, self.partner).wait_recv()
        own = self.acc2[pl.ds(self.b * size, size)]
        self.acc3[...] = (own + self.got2[0]) + (self.got2[1] + self.got2[2])
        if self.direct:
            self.across_z()
            return
        size = CHUNK[self.group]
        for s in (4, 3, 5, 2, 6, 1, 7):
            to, peer = self.along("z", s)

            def send():
                self.copy(self.acc3.at[pl.ds(to * size, size)], self.got3.at[s - 1], 5 + s, peer).start()

            self.takes(to, send)

    def stage3(self):
        if self.direct:
            for s in range(1, ZS):
                self.copy(self.acc3, self.got3.at[0], 5 + s, self.partner).wait_recv()
            self.g_ref[pl.ds(self.second, SECOND[self.group])] = tree([self.got3[k] for k in range(ZS)])
            self.back()
            return
        size = CHUNK[self.group]
        own = self.second + self.z * size

        def total():
            for s in range(1, ZS):
                self.copy(self.got3.at[s - 1], self.got3.at[s - 1], 5 + s, self.partner).wait_recv()
            terms = [self.acc3[pl.ds(self.z * size, size)]] + [self.got3[s] for s in range(ZS - 1)]
            self.g_ref[pl.ds(own, size)] = tree(terms)
            for s in (4, 3, 5, 2, 6, 1, 7):
                to, peer = self.along("z", s)
                self.copy(self.chunk(own, size), self.chunk(own, size), 12 + s, peer).start()

        self.takes(self.z, total)

    def stage4(self):
        size = CHUNK[self.group]
        for s in range(1, ZS):
            sender = lax.rem(self.z + ZS - s, ZS)

            def receive():
                got = self.chunk(self.second + sender * size, size)
                self.copy(got, got, 12 + s, self.partner).wait_recv()

            self.takes(sender, receive)
        self.back()

    def back(self):
        mine = self.chunk(self.second, SECOND[self.group])
        for s in (2, 1, 3):
            to, peer = self.along("second", s)
            self.start(mine, mine, 19 + s, peer)

    def stage5(self):
        size = SECOND[self.group]
        for s in range(1, 4):
            got = self.chunk(self.first + lax.rem(self.b + 4 - s, 4) * size, size)
            self.copy(got, got, 19 + s, self.partner).wait_recv()
        mine = self.chunk(self.first, FIRST[self.group])
        for s in (2, 1, 3):
            to, peer = self.along("first", s)
            self.start(mine, mine, 22 + s, peer)
        self.start(mine, mine, 26, self.partner)

    def stage6(self):
        size = FIRST[self.group]
        for s in (1, 3, 2):
            got = self.chunk(self.half + lax.rem(self.a + 4 - s, 4) * size, size)
            self.copy(got, got, 22 + s, self.partner).wait_recv()
            self.start(got, got, 26 + s, self.partner)

    def stage7(self):
        size = FIRST[self.group]
        for s in range(4):
            got = self.chunk(self.other_half + lax.rem(self.b + 4 - s, 4) * size, size)
            self.copy(got, got, 26 + s, self.partner).wait_recv()

    def finish(self):
        for size, index in self.started:
            part = self.chunk(0, size)
            self.copy(part, part, index, self.partner).wait_send()
        if self.direct:
            return
        size = CHUNK[self.group]
        for s in range(1, ZS):
            to, peer = self.along("z", s)

            def sent():
                part = self.acc3.at[pl.ds(to * size, size)]
                self.copy(part, part, 5 + s, peer).wait_send()

            self.takes(to, sent)

            def sent_back():
                part = self.chunk(self.second, size)
                self.copy(part, part, 12 + s, peer).wait_send()

            self.takes(self.z, sent_back)


def orthonormalize_kernel(n, scale, src_ref, out_ref, *scratch):
    (own_ref, other_ref, held_hi, held_lo, p_ref, g_ref, cur_ref, d_ref, z_ref, x_ref, hi_ref, lo_ref, lane_ref) = scratch[:13]
    groups_scratch = [scratch[13 + 5 * g : 18 + 5 * g] for g in range(3)]
    (send, recv, x_send, x_recv, in_send, in_recv, pass_send, pass_recv, own_sem) = scratch[28:]
    rows_each, width = src_ref.shape[0], own_ref.shape[1]
    bands = src_ref.shape[1] // width
    per_panel = B // rows_each
    tiles = B // V
    me = lax.axis_index("band")
    core, x, y, z = coordinates()
    partner = device(1 - core, x, y, z)

    barrier = pltpu.get_barrier_semaphore()

    def greet(s, carry):
        pl.semaphore_signal(
            barrier, inc=1, device_id={"band": lax.rem(me + s, bands)}, device_id_type=MESH
        )
        return carry

    others = [device(core, x, y, lax.rem(z + s, ZS)) for s in range(1, ZS)]
    others += [device(core, lax.rem(x + s, XS), y, z) for s in (1, 3)]
    for peer in others:
        pl.semaphore_signal(barrier, inc=1, device_id=peer, device_id_type=MESH)
    lax.fori_loop(1, bands, greet, 0)

    def columns(ref, index):
        return ref.at[:, pl.ds(pl.multiple_of(index * width, width), width)]

    def band(ref, index):
        return ref.at[pl.ds(pl.multiple_of(index * rows_each, rows_each), rows_each), :]

    mine = pltpu.make_async_copy(columns(src_ref, me), band(own_ref, me), own_sem)
    mine.start()
    pl.semaphore_wait(barrier, bands - 1 + len(others))

    def bring(s, source):
        peer = lax.rem(me + s, bands)
        return pltpu.make_async_remote_copy(
            src_ref=columns(src_ref, peer),
            dst_ref=band(own_ref, source),
            send_sem=in_send.at[s],
            recv_sem=in_recv.at[s],
            device_id={"band": peer},
            device_id_type=MESH,
        )

    def hand_over(source):
        return pltpu.make_async_remote_copy(
            src_ref=band(own_ref, source),
            dst_ref=band(other_ref, source),
            send_sem=pass_send.at[source],
            recv_sem=pass_recv.at[source],
            device_id=partner,
            device_id_type=MESH,
        )

    def keep(ref, source, at):
        rows = pl.ds(pl.multiple_of(source * rows_each, rows_each), rows_each)
        high, low = split(ref[rows, :])
        held_hi[rows, at : at + width] = high
        held_lo[rows, at : at + width] = low

    def start(s, carry):
        bring(s, me).start()
        return carry

    def arrive(s, carry):
        source = lax.rem(me - s + bands, bands)
        bring(s, source).wait_recv()
        hand_over(source).start()
        keep(own_ref, source, 0)
        return carry

    def finish(s, carry):
        source = lax.rem(me + 1 - 2 * core - s + bands, bands)
        hand_over(source).wait_recv()
        keep(other_ref, source, width)
        return carry

    def sent(s, carry):
        bring(s, me).wait_send()
        hand_over(lax.rem(me + s, bands)).wait_send()
        return carry

    lax.fori_loop(1, bands, start, 0)
    mine.wait()
    hand_over(me).start()
    keep(own_ref, me, 0)
    lax.fori_loop(1, bands, lambda s, carry: finish(s - 1, arrive(s, carry)), 0)
    finish(bands - 1, 0)

    groups = grouped_blocks(n)

    def multiply(g):
        half = len(groups[g]) // CORES
        for c in range(CORES):

            @pl.when(core == c)
            def _():
                blocks = groups[g][c * half : (c + 1) * half]
                for i in sorted({i for i, _ in blocks}):
                    wanted = [j for k, j in blocks if k == i]
                    first, end = min(wanted), max(wanted) + 1
                    left = (held_hi[i * B : (i + 1) * B], held_lo[i * B : (i + 1) * B])
                    right = (held_hi[first * B : end * B], held_lo[first * B : end * B])
                    out = dot3(left, right, ((1,), (1,))) * scale
                    for j in wanted:
                        at = sum(HALF[:g]) + blocks.index((i, j)) * tiles
                        block = out[:, (j - first) * B : (j - first + 1) * B]
                        p_ref[at : at + tiles] = block.reshape(tiles, V, B)

    one, two, three = (Summing(g, p_ref, g_ref, groups_scratch[g], send, recv) for g in range(3))
    multiply(0)
    one.stage0()
    multiply(1)
    two.stage0()
    multiply(2)
    three.stage0()
    one.stage1()
    two.stage1()
    one.stage2()
    three.stage1()
    two.stage2()
    one.stage3()
    three.stage2()
    two.stage3()
    one.stage5()
    three.stage3()
    two.stage5()
    one.stage6()
    three.stage4()
    one.stage7()

    order = [block for group in groups for block in group]
    sub = lax.broadcasted_iota(jnp.int32, (V, B), 0)
    lane = lax.broadcasted_iota(jnp.int32, (V, B), 1)

    def prepare(k):
        at = order.index((k, k)) * tiles
        on_diagonal = [jnp.where(lane == q * V + sub, g_ref[at + q], 0.0) for q in range(tiles)]
        diagonal = jnp.sum(tree(on_diagonal), axis=0, keepdims=True)
        lanes = jnp.broadcast_to(lax.rsqrt(diagonal), (V, B))
        lane_ref[...] = lanes
        taken = None
        if k:
            left = (hi_ref[: k * B, k * B : (k + 1) * B], lo_ref[: k * B, k * B : (k + 1) * B])
            right = (hi_ref[: k * B, k * B :], lo_ref[: k * B, k * B :])
            taken = dot3(left, right, ((0,), (0,)))
        for j in range(k, n + width // B):
            if j < n:
                at = order.index((k, j)) * tiles
                block = g_ref[at : at + tiles].reshape(B, B)
            else:
                block = own_ref[k * B : (k + 1) * B, (j - n) * B : (j - n + 1) * B]
            if k:
                block = block - taken[:, (j - k) * B : (j - k + 1) * B]
            if j > k:
                cur_ref[:, j * B : (j + 1) * B] = block
                continue
            for q in range(tiles):
                rows = jnp.take_along_axis(lanes, q * V + sub, axis=1)
                d_ref[q * V : (q + 1) * V, :] = block[q * V : (q + 1) * V] * rows * lanes

    def remote(peer, sender):
        return pltpu.make_async_remote_copy(
            src_ref=x_ref.at[pl.ds(peer * rows_each, rows_each), :],
            dst_ref=columns(out_ref, sender),
            send_sem=x_send.at[peer],
            recv_sem=x_recv.at[sender],
            device_id={"band": peer},
            device_id_type=MESH,
        )

    stays = pltpu.make_async_copy(band(x_ref, me), columns(out_ref, me), own_sem)

    def step(i, carry):
        for k in range(n):

            @pl.when(i == k)
            def _():
                if k == 1:
                    two.stage7()
                if k == 3:
                    three.stage7()
                prepare(k)

        rows = [d_ref[q * V : (q + 1) * V, :] for q in range(tiles)]
        lanes = lane_ref[...]
        for q, inverse in enumerate(factor_inverse(rows)):
            z_ref[q * V : (q + 1) * V, :] = inverse * lanes
        for k in range(n):

            @pl.when(i == k)
            def _():
                if k == 0:
                    two.stage6()
                    three.stage5()
                if k == 2:
                    three.stage6()
                panel = dot3(split(z_ref[...]), split(cur_ref[:, (k + 1) * B :]), ((1,), (0,)))
                x_ref[k * B : (k + 1) * B, :] = panel[:, panel.shape[1] - width :]
                for peer in range(k * per_panel, (k + 1) * per_panel):

                    @pl.when(peer != me)
                    def _():
                        remote(peer, me).start()

                    @pl.when(peer == me)
                    def _():
                        stays.start()

                if k < n - 1:
                    high, low = split(panel)
                    hi_ref[k * B : (k + 1) * B, (k + 1) * B :] = high
                    lo_ref[k * B : (k + 1) * B, (k + 1) * B :] = low

        return carry

    lax.fori_loop(0, n, step, 0)
    lax.fori_loop(1, bands, sent, 0)
    hand_over(me).wait_send()
    for group in (one, two, three):
        group.finish()
    stays.wait()
    for other in range(bands):

        @pl.when(other != me)
        def _():
            remote(other, me).wait_send()
            remote(other, other).wait_recv()


def orthonormalize(coeffs, bands, columns_all):
    rows_each, columns = coeffs.shape
    rows, width = rows_each * bands, columns // bands
    n = rows // B
    tiles = lambda *shape: pltpu.VMEM((*shape, V, B), jnp.float32)
    whole = n * B + width
    summing = []
    for g in range(3):
        summing += [tiles(FIRST[g]), tiles(SECOND[g]), tiles(3, FIRST[g]), tiles(3, SECOND[g])]
        summing += [tiles(ZS - 1, CHUNK[g]) if Z_USED[g] else tiles(ZS, SECOND[g])]
    return pl.pallas_call(
        functools.partial(orthonormalize_kernel, n, 1.0 / columns_all),
        out_shape=jax.ShapeDtypeStruct(coeffs.shape, jnp.float32),
        in_specs=[pl.BlockSpec(memory_space=pltpu.HBM)],
        out_specs=pl.BlockSpec(memory_space=pltpu.VMEM),
        scratch_shapes=[
            pltpu.VMEM((rows, width), jnp.float32),
            pltpu.VMEM((rows, width), jnp.float32),
            pltpu.VMEM((rows, CORES * width), jnp.bfloat16),
            pltpu.VMEM((rows, CORES * width), jnp.bfloat16),
            tiles(sum(HALF)),
            tiles(sum(TOTAL)),
            pltpu.VMEM((B, whole), jnp.float32),
            pltpu.VMEM((B, B), jnp.float32),
            pltpu.VMEM((B, B), jnp.float32),
            pltpu.VMEM((rows, width), jnp.float32),
            pltpu.VMEM((rows, whole), jnp.bfloat16),
            pltpu.VMEM((rows, whole), jnp.bfloat16),
            pltpu.VMEM((V, B), jnp.float32),
            *summing,
            pltpu.SemaphoreType.DMA((3 * COPIES,)),
            pltpu.SemaphoreType.DMA((3 * COPIES,)),
            *[pltpu.SemaphoreType.DMA((bands,))] * 6,
            pltpu.SemaphoreType.DMA,
        ],
        compiler_params=pltpu.CompilerParams(
            collective_id=0, has_side_effects=True, vmem_limit_bytes=52 << 20
        ),
        name="orthonormalize",
    )(coeffs)


def local(coeffs):
    bands = lax.axis_size("band")
    return orthonormalize(coeffs, bands, coeffs.shape[1] * lax.axis_size("ga"))


def solution(mesh):
    return jax.shard_map(
        local,
        mesh=mesh,
        in_specs=(P("band", "ga"),),
        out_specs=P("band", "ga"),
        check_vma=False,
    )
```

```python
import functools

import jax
import jax.numpy as jnp
from jax import lax
from jax.experimental import pallas as pl
from jax.experimental.pallas import tpu as pltpu
from jax.sharding import PartitionSpec as P

MESH = pl.DeviceIdType.MESH

B = 128
V = 8


def split(x):
    hi = x.astype(jnp.bfloat16)
    return hi, (x - hi.astype(jnp.float32)).astype(jnp.bfloat16)


def dot3(a, b, dims):
    (ca,), (cb,) = dims
    ah, al = a
    bh, bl = b
    left = jnp.concatenate([ah, al, ah], axis=ca)
    right = jnp.concatenate([bh, bh, bl], axis=cb)
    return lax.dot_general(left, right, (dims, ((), ())), preferred_element_type=jnp.float32)


def lane_col(t, c):
    return jnp.take_along_axis(t, jnp.full((V, B), c, jnp.int32), axis=1)


def sub_row(t, k):
    return jnp.broadcast_to(t[k : k + 1, :], (V, B))


def tree(m):
    while len(m) > 1:
        m = [m[e] + m[e + 1] if e + 1 < len(m) else m[e] for e in range(0, len(m), 2)]
    return m[0]


def factor_inverse(rows):
    n = len(rows)
    rows = list(rows)
    sub = lax.broadcasted_iota(jnp.int32, (V, B), 0)
    lane = lax.broadcasted_iota(jnp.int32, (V, B), 1)
    out = []
    cols = [lane_col(rows[0], k) for k in range(V)]
    for p in range(n):
        c0 = p * V
        last = p == n - 1
        in_block = (lane >= c0) & (lane < c0 + V)
        t = jnp.where(in_block, jnp.where(lane - c0 == sub, 1.0, 0.0), rows[p])
        f = jnp.where(lane < c0 + V, t, 0.0)
        pivots = None
        below_m = {q: [lane_col(rows[q], c0 + k) for k in range(V)] for q in range(p + 1, n)}
        if not last:
            a = list(below_m[p + 1])
            ahead = [lane_col(rows[p + 1], c0 + V + k) for k in range(V)]
        for k in range(0, V, 2):
            h1, h2 = sub == k, sub == k + 1
            here = h1 | h2
            d11, d12, d22 = sub_row(cols[k], k), sub_row(cols[k + 1], k), sub_row(cols[k + 1], k + 1)
            det = d11 * d22 - d12 * d12
            r = 1.0 / det
            m1, m2 = jnp.where(here, 0.0, cols[k]), jnp.where(here, 0.0, cols[k + 1])

            def solve(col):
                v1, v2 = sub_row(col, k), sub_row(col, k + 1)
                return (d22 * v1 - d12 * v2) * r, (d11 * v2 - d12 * v1) * r

            def eliminate(col):
                u1, u2 = solve(col)
                return jnp.where(h1, u1, jnp.where(h2, u2, col - (m1 * u1 + m2 * u2))), u1, u2

            for j in range(k + 2, V):
                cols[j], u1, u2 = eliminate(cols[j])
                if not last:
                    a[j] = a[j] - (a[k] * u1 + a[k + 1] * u2)
            if not last:
                s1 = (d22 * a[k] - d12 * a[k + 1]) * r
                s2 = (d11 * a[k + 1] - d12 * a[k]) * r
                for j in range(V):
                    ahead[j] = ahead[j] - (s1 * sub_row(a[k], j) + s2 * sub_row(a[k + 1], j))
            q = 1.0 / d11
            ratio = d12 * q
            f1 = sub_row(f, k)
            f2 = sub_row(f, k + 1) - ratio * f1
            g2 = d11 * r
            g1 = q
            below = sub > k + 1
            b1 = jnp.where(below, cols[k], 0.0)
            b2 = jnp.where(below, cols[k + 1], 0.0)
            l2 = b2 - b1 * ratio
            f = jnp.where(h2, f2, f - b1 * (f1 * g1) - l2 * (f2 * g2))
            t, _, _ = eliminate(t)
            scale = jnp.where(h1, g1, g2)
            pivots = scale if pivots is None else jnp.where(here, scale, pivots)
        out.append(f * jnp.sqrt(pivots))
        if last:
            break
        cols = ahead
        w = [sub_row(t, k) for k in range(V)]
        for q in range(p + 1, n):
            acc = jnp.where(in_block, 0.0, rows[q])
            rows[q] = acc - tree([below_m[q][k] * w[k] for k in range(V)])
    return out


CORES, YS, XS, ZS = 2, 4, 4, 8
TOTAL = (128, 128, 160, 160)
HALF = tuple(t // 2 for t in TOTAL)
FIRST = tuple(t // 8 for t in TOTAL)
SECOND = tuple(t // 32 for t in TOTAL)
Z_USED = (0, 0, 5, 5)
CHUNK = tuple(t // max(z, 1) for t, z in zip(SECOND, Z_USED))
COPIES = 30


def grouped_blocks(n):
    first = [(0, j) for j in range(n)]
    second = [(1, j) for j in range(1, n)] + [(2, 2)]
    third = [(i, j) for i in (2, 3) for j in range(3, n)]
    rest = [(i, j) for i in range(4, n) for j in range(i, n)]
    return first, second, third, rest


def coordinates():
    band, ga = lax.axis_index("band"), lax.axis_index("ga")
    core, y = lax.rem(band, CORES), lax.rem(band // CORES, YS)
    x = (band // (CORES * YS)) * 2 + lax.rem(ga, 2)
    return core, x, y, ga // 2


def device(core, x, y, z):
    return {"band": ((x // 2) * YS + y) * CORES + core, "ga": z * 2 + lax.rem(x, 2)}


class Summing:
    def __init__(self, group, p_ref, g_ref, scratch, send, recv):
        self.group, self.p_ref, self.g_ref = group, p_ref, g_ref
        self.acc2, self.acc3, self.got1, self.got2, self.got3 = scratch
        self.send, self.recv = send, recv
        self.direct = Z_USED[group] == 0
        core, x, y, z = self.at = coordinates()
        self.core, self.z = core, z
        self.a = jnp.where(core == 0, y, x)
        self.b = jnp.where(core == 0, x, y)
        self.partner = device(1 - core, x, y, z)
        self.from_p = sum(HALF[:group])
        base = sum(TOTAL[:group])
        self.half = base + core * HALF[group]
        self.first = self.half + self.a * FIRST[group]
        self.second = self.first + self.b * SECOND[group]
        self.other_half = base + (1 - core) * HALF[group]
        self.started = []

    def along(self, stage, s):
        core, x, y, z = self.at
        if stage == "z":
            to = lax.rem(z + s, ZS)
            return to, device(core, x, y, to)
        at = self.a if stage == "first" else self.b
        to = lax.rem(at + s, 4)
        on_y = core == (0 if stage == "first" else 1)
        return to, device(core, jnp.where(on_y, x, to), jnp.where(on_y, to, y), z)

    def copy(self, src, dst, index, peer):
        return pltpu.make_async_remote_copy(
            src_ref=src,
            dst_ref=dst,
            send_sem=self.send.at[self.group * COPIES + index],
            recv_sem=self.recv.at[self.group * COPIES + index],
            device_id=peer,
            device_id_type=MESH,
        )

    def start(self, src, dst, index, peer):
        self.copy(src, dst, index, peer).start()
        self.started.append((src.shape[0], index))

    def chunk(self, at, size):
        return self.g_ref.at[pl.ds(at, size)]

    def takes(self, z, then):
        if Z_USED[self.group] == ZS:
            then()
        else:
            pl.when(z < Z_USED[self.group])(then)

    def stage0(self):
        size = FIRST[self.group]
        for s in (2, 1, 3):
            to, peer = self.along("first", s)
            self.start(self.p_ref.at[pl.ds(self.from_p + to * size, size)], self.got1.at[s - 1], s - 1, peer)

    def stage1(self):
        size, step = FIRST[self.group], 4
        for s in range(3):
            self.copy(self.got1.at[s], self.got1.at[s], s, self.partner).wait_recv()

        def add(t, carry):
            at = pl.ds(t * step, step)
            own = self.p_ref[pl.ds(self.from_p + self.a * size + t * step, step)]
            self.acc2[at] = (own + self.got1[0, at]) + (self.got1[1, at] + self.got1[2, at])
            return carry

        lax.fori_loop(0, size // step, add, 0)
        size = SECOND[self.group]
        for s in (2, 1, 3):
            to, peer = self.along("second", s)
            self.start(self.acc2.at[pl.ds(to * size, size)], self.got2.at[s - 1], 2 + s, peer)

    def across_z(self):
        size = SECOND[self.group]
        self.got3[pl.ds(self.z, 1)] = self.acc3[...][None]
        for s in (4, 3, 5, 2, 6, 1, 7):
            to, peer = self.along("z", s)
            self.start(self.acc3, self.got3.at[self.z], 5 + s, peer)

    def stage2(self):
        size = SECOND[self.group]
        for s in range(3):
            self.copy(self.got2.at[s], self.got2.at[s], 3 + s, self.partner).wait_recv()
        own = self.acc2[pl.ds(self.b * size, size)]
        self.acc3[...] = (own + self.got2[0]) + (self.got2[1] + self.got2[2])
        if self.direct:
            self.across_z()
            return
        size = CHUNK[self.group]
        for s in (4, 3, 5, 2, 6, 1, 7):
            to, peer = self.along("z", s)

            def send():
                self.copy(self.acc3.at[pl.ds(to * size, size)], self.got3.at[s - 1], 5 + s, peer).start()

            self.takes(to, send)

    def stage3(self):
        if self.direct:
            for s in range(1, ZS):
                self.copy(self.acc3, self.got3.at[0], 5 + s, self.partner).wait_recv()
            self.g_ref[pl.ds(self.second, SECOND[self.group])] = tree([self.got3[k] for k in range(ZS)])
            self.back()
            return
        size = CHUNK[self.group]
        own = self.second + self.z * size

        def total():
            for s in range(1, ZS):
                self.copy(self.got3.at[s - 1], self.got3.at[s - 1], 5 + s, self.partner).wait_recv()
            terms = [self.acc3[pl.ds(self.z * size, size)]] + [self.got3[s] for s in range(ZS - 1)]
            self.g_ref[pl.ds(own, size)] = tree(terms)
            for s in (4, 3, 5, 2, 6, 1, 7):
                to, peer = self.along("z", s)
                self.copy(self.chunk(own, size), self.chunk(own, size), 12 + s, peer).start()

        self.takes(self.z, total)

    def stage4(self):
        size = CHUNK[self.group]
        for s in range(1, ZS):
            sender = lax.rem(self.z + ZS - s, ZS)

            def receive():
                got = self.chunk(self.second + sender * size, size)
                self.copy(got, got, 12 + s, self.partner).wait_recv()

            self.takes(sender, receive)
        self.back()

    def back(self):
        mine = self.chunk(self.second, SECOND[self.group])
        for s in (2, 1, 3):
            to, peer = self.along("second", s)
            self.start(mine, mine, 19 + s, peer)

    def stage5(self):
        size = SECOND[self.group]
        for s in range(1, 4):
            got = self.chunk(self.first + lax.rem(self.b + 4 - s, 4) * size, size)
            self.copy(got, got, 19 + s, self.partner).wait_recv()
        mine = self.chunk(self.first, FIRST[self.group])
        for s in (2, 1, 3):
            to, peer = self.along("first", s)
            self.start(mine, mine, 22 + s, peer)
        self.start(mine, mine, 26, self.partner)

    def stage6(self):
        size = FIRST[self.group]
        for s in (1, 3, 2):
            got = self.chunk(self.half + lax.rem(self.a + 4 - s, 4) * size, size)
            self.copy(got, got, 22 + s, self.partner).wait_recv()
            self.start(got, got, 26 + s, self.partner)

    def stage7(self):
        size = FIRST[self.group]
        for s in range(4):
            got = self.chunk(self.other_half + lax.rem(self.b + 4 - s, 4) * size, size)
            self.copy(got, got, 26 + s, self.partner).wait_recv()

    def finish(self):
        for size, index in self.started:
            part = self.chunk(0, size)
            self.copy(part, part, index, self.partner).wait_send()
        if self.direct:
            return
        size = CHUNK[self.group]
        for s in range(1, ZS):
            to, peer = self.along("z", s)

            def sent():
                part = self.acc3.at[pl.ds(to * size, size)]
                self.copy(part, part, 5 + s, peer).wait_send()

            self.takes(to, sent)

            def sent_back():
                part = self.chunk(self.second, size)
                self.copy(part, part, 12 + s, peer).wait_send()

            self.takes(self.z, sent_back)


def orthonormalize_kernel(n, scale, src_ref, out_ref, *scratch):
    (own_ref, other_ref, held_hi, held_lo, p_ref, g_ref, cur_ref, d_ref, z_ref, x_ref, hi_ref, lo_ref, lane_ref) = scratch[:13]
    groups_scratch = [scratch[13 + 5 * g : 18 + 5 * g] for g in range(4)]
    (send, recv, x_send, x_recv, in_send, in_recv, pass_send, pass_recv, own_sem) = scratch[33:]
    rows_each, width = src_ref.shape[0], own_ref.shape[1]
    bands = src_ref.shape[1] // width
    per_panel = B // rows_each
    tiles = B // V
    me = lax.axis_index("band")
    core, x, y, z = coordinates()
    partner = device(1 - core, x, y, z)

    barrier = pltpu.get_barrier_semaphore()

    def greet(s, carry):
        pl.semaphore_signal(
            barrier, inc=1, device_id={"band": lax.rem(me + s, bands)}, device_id_type=MESH
        )
        return carry

    others = [device(core, x, y, lax.rem(z + s, ZS)) for s in range(1, ZS)]
    others += [device(core, lax.rem(x + s, XS), y, z) for s in (1, 3)]
    for peer in others:
        pl.semaphore_signal(barrier, inc=1, device_id=peer, device_id_type=MESH)
    lax.fori_loop(1, bands, greet, 0)

    def columns(ref, index):
        return ref.at[:, pl.ds(pl.multiple_of(index * width, width), width)]

    def band(ref, index):
        return ref.at[pl.ds(pl.multiple_of(index * rows_each, rows_each), rows_each), :]

    mine = pltpu.make_async_copy(columns(src_ref, me), band(own_ref, me), own_sem)
    mine.start()
    pl.semaphore_wait(barrier, bands - 1 + len(others))

    def bring(s, source):
        peer = lax.rem(me + s, bands)
        return pltpu.make_async_remote_copy(
            src_ref=columns(src_ref, peer),
            dst_ref=band(own_ref, source),
            send_sem=in_send.at[s],
            recv_sem=in_recv.at[s],
            device_id={"band": peer},
            device_id_type=MESH,
        )

    def hand_over(source):
        return pltpu.make_async_remote_copy(
            src_ref=band(own_ref, source),
            dst_ref=band(other_ref, source),
            send_sem=pass_send.at[source],
            recv_sem=pass_recv.at[source],
            device_id=partner,
            device_id_type=MESH,
        )

    def keep(ref, source, at):
        rows = pl.ds(pl.multiple_of(source * rows_each, rows_each), rows_each)
        high, low = split(ref[rows, :])
        held_hi[rows, at : at + width] = high
        held_lo[rows, at : at + width] = low

    def start(s, carry):
        bring(s, me).start()
        return carry

    def arrive(s, carry):
        source = lax.rem(me - s + bands, bands)
        bring(s, source).wait_recv()
        hand_over(source).start()
        keep(own_ref, source, 0)
        return carry

    def finish(s, carry):
        source = lax.rem(me + 1 - 2 * core - s + bands, bands)
        hand_over(source).wait_recv()
        keep(other_ref, source, width)
        return carry

    def sent(s, carry):
        bring(s, me).wait_send()
        hand_over(lax.rem(me + s, bands)).wait_send()
        return carry

    lax.fori_loop(1, bands, start, 0)
    mine.wait()
    hand_over(me).start()
    keep(own_ref, me, 0)
    lax.fori_loop(1, bands, arrive, 0)
    lax.fori_loop(0, bands, finish, 0)

    groups = grouped_blocks(n)

    def multiply(g):
        half = len(groups[g]) // CORES
        for c in range(CORES):

            @pl.when(core == c)
            def _():
                blocks = groups[g][c * half : (c + 1) * half]
                for i in sorted({i for i, _ in blocks}):
                    wanted = [j for k, j in blocks if k == i]
                    first, end = min(wanted), max(wanted) + 1
                    left = (held_hi[i * B : (i + 1) * B], held_lo[i * B : (i + 1) * B])
                    right = (held_hi[first * B : end * B], held_lo[first * B : end * B])
                    out = dot3(left, right, ((1,), (1,))) * scale
                    for j in wanted:
                        at = sum(HALF[:g]) + blocks.index((i, j)) * tiles
                        block = out[:, (j - first) * B : (j - first + 1) * B]
                        p_ref[at : at + tiles] = block.reshape(tiles, V, B)

    one, two, three, four = (Summing(g, p_ref, g_ref, groups_scratch[g], send, recv) for g in range(4))
    multiply(0)
    one.stage0()
    multiply(1)
    two.stage0()
    multiply(2)
    three.stage0()
    multiply(3)
    four.stage0()
    one.stage1()
    two.stage1()
    one.stage2()
    three.stage1()
    two.stage2()
    four.stage1()
    three.stage2()
    one.stage3()
    four.stage2()
    two.stage3()
    three.stage3()
    one.stage5()
    four.stage3()
    two.stage5()
    three.stage4()
    one.stage6()
    four.stage4()
    two.stage6()
    one.stage7()
    three.stage5()

    order = [block for group in groups for block in group]
    sub = lax.broadcasted_iota(jnp.int32, (V, B), 0)
    lane = lax.broadcasted_iota(jnp.int32, (V, B), 1)

    def prepare(k):
        at = order.index((k, k)) * tiles
        on_diagonal = [jnp.where(lane == q * V + sub, g_ref[at + q], 0.0) for q in range(tiles)]
        diagonal = jnp.sum(tree(on_diagonal), axis=0, keepdims=True)
        lanes = jnp.broadcast_to(lax.rsqrt(diagonal), (V, B))
        lane_ref[...] = lanes
        taken = None
        if k:
            left = (hi_ref[: k * B, k * B : (k + 1) * B], lo_ref[: k * B, k * B : (k + 1) * B])
            right = (hi_ref[: k * B, k * B :], lo_ref[: k * B, k * B :])
            taken = dot3(left, right, ((0,), (0,)))
        for j in range(k, n + width // B):
            if j < n:
                at = order.index((k, j)) * tiles
                block = g_ref[at : at + tiles].reshape(B, B)
            else:
                block = own_ref[k * B : (k + 1) * B, (j - n) * B : (j - n + 1) * B]
            if k:
                block = block - taken[:, (j - k) * B : (j - k + 1) * B]
            if j > k:
                cur_ref[:, j * B : (j + 1) * B] = block
                continue
            for q in range(tiles):
                rows = jnp.take_along_axis(lanes, q * V + sub, axis=1)
                d_ref[q * V : (q + 1) * V, :] = block[q * V : (q + 1) * V] * rows * lanes

    def remote(peer, sender):
        return pltpu.make_async_remote_copy(
            src_ref=x_ref.at[pl.ds(peer * rows_each, rows_each), :],
            dst_ref=columns(out_ref, sender),
            send_sem=x_send.at[peer],
            recv_sem=x_recv.at[sender],
            device_id={"band": peer},
            device_id_type=MESH,
        )

    stays = pltpu.make_async_copy(band(x_ref, me), columns(out_ref, me), own_sem)

    def step(i, carry):
        for k in range(n):

            @pl.when(i == k)
            def _():
                if k == 1:
                    two.stage7()
                if k == 2:
                    three.stage7()
                if k == 4:
                    four.stage7()
                prepare(k)

        rows = [d_ref[q * V : (q + 1) * V, :] for q in range(tiles)]
        lanes = lane_ref[...]
        for q, inverse in enumerate(factor_inverse(rows)):
            z_ref[q * V : (q + 1) * V, :] = inverse * lanes
        for k in range(n):

            @pl.when(i == k)
            def _():
                if k == 0:
                    four.stage5()
                    three.stage6()
                if k == 1:
                    four.stage6()
                panel = dot3(split(z_ref[...]), split(cur_ref[:, (k + 1) * B :]), ((1,), (0,)))
                x_ref[k * B : (k + 1) * B, :] = panel[:, panel.shape[1] - width :]
                for peer in range(k * per_panel, (k + 1) * per_panel):

                    @pl.when(peer != me)
                    def _():
                        remote(peer, me).start()

                    @pl.when(peer == me)
                    def _():
                        stays.start()

                if k < n - 1:
                    high, low = split(panel)
                    hi_ref[k * B : (k + 1) * B, (k + 1) * B :] = high
                    lo_ref[k * B : (k + 1) * B, (k + 1) * B :] = low

        return carry

    lax.fori_loop(0, n, step, 0)
    lax.fori_loop(1, bands, sent, 0)
    hand_over(me).wait_send()
    for group in (one, two, three, four):
        group.finish()
    stays.wait()
    for other in range(bands):

        @pl.when(other != me)
        def _():
            remote(other, me).wait_send()
            remote(other, other).wait_recv()


def orthonormalize(coeffs, bands, columns_all):
    rows_each, columns = coeffs.shape
    rows, width = rows_each * bands, columns // bands
    n = rows // B
    tiles = lambda *shape: pltpu.VMEM((*shape, V, B), jnp.float32)
    whole = n * B + width
    summing = []
    for g in range(4):
        summing += [tiles(FIRST[g]), tiles(SECOND[g]), tiles(3, FIRST[g]), tiles(3, SECOND[g])]
        summing += [tiles(ZS - 1, CHUNK[g]) if Z_USED[g] else tiles(ZS, SECOND[g])]
    return pl.pallas_call(
        functools.partial(orthonormalize_kernel, n, 1.0 / columns_all),
        out_shape=jax.ShapeDtypeStruct(coeffs.shape, jnp.float32),
        in_specs=[pl.BlockSpec(memory_space=pltpu.HBM)],
        out_specs=pl.BlockSpec(memory_space=pltpu.VMEM),
        scratch_shapes=[
            pltpu.VMEM((rows, width), jnp.float32),
            pltpu.VMEM((rows, width), jnp.float32),
            pltpu.VMEM((rows, CORES * width), jnp.bfloat16),
            pltpu.VMEM((rows, CORES * width), jnp.bfloat16),
            tiles(sum(HALF)),
            tiles(sum(TOTAL)),
            pltpu.VMEM((B, whole), jnp.float32),
            pltpu.VMEM((B, B), jnp.float32),
            pltpu.VMEM((B, B), jnp.float32),
            pltpu.VMEM((rows, width), jnp.float32),
            pltpu.VMEM((rows, whole), jnp.bfloat16),
            pltpu.VMEM((rows, whole), jnp.bfloat16),
            pltpu.VMEM((V, B), jnp.float32),
            *summing,
            pltpu.SemaphoreType.DMA((4 * COPIES,)),
            pltpu.SemaphoreType.DMA((4 * COPIES,)),
            *[pltpu.SemaphoreType.DMA((bands,))] * 6,
            pltpu.SemaphoreType.DMA,
        ],
        compiler_params=pltpu.CompilerParams(
            collective_id=0, has_side_effects=True, vmem_limit_bytes=52 << 20
        ),
        name="orthonormalize",
    )(coeffs)


def local(coeffs):
    bands = lax.axis_size("band")
    return orthonormalize(coeffs, bands, coeffs.shape[1] * lax.axis_size("ga"))


def solution(mesh):
    return jax.shard_map(
        local,
        mesh=mesh,
        in_specs=(P("band", "ga"),),
        out_specs=P("band", "ga"),
        check_vma=False,
    )
```

```python
import functools

import jax
import jax.numpy as jnp
from jax import lax
from jax.experimental import pallas as pl
from jax.experimental.pallas import tpu as pltpu
from jax.sharding import PartitionSpec as P

MESH = pl.DeviceIdType.MESH

B = 128
V = 8


def split(x):
    hi = x.astype(jnp.bfloat16)
    return hi, (x - hi.astype(jnp.float32)).astype(jnp.bfloat16)


def dot3(a, b, dims):
    (ca,), (cb,) = dims
    ah, al = a
    bh, bl = b
    left = jnp.concatenate([ah, al, ah], axis=ca)
    right = jnp.concatenate([bh, bh, bl], axis=cb)
    return lax.dot_general(left, right, (dims, ((), ())), preferred_element_type=jnp.float32)


def lane_col(t, c):
    return jnp.take_along_axis(t, jnp.full((V, B), c, jnp.int32), axis=1)


def sub_row(t, k):
    return jnp.broadcast_to(t[k : k + 1, :], (V, B))


def tree(m):
    while len(m) > 1:
        m = [m[e] + m[e + 1] if e + 1 < len(m) else m[e] for e in range(0, len(m), 2)]
    return m[0]


def factor_inverse(rows):
    n = len(rows)
    rows = list(rows)
    sub = lax.broadcasted_iota(jnp.int32, (V, B), 0)
    lane = lax.broadcasted_iota(jnp.int32, (V, B), 1)
    out = []
    cols = [lane_col(rows[0], k) for k in range(V)]
    for p in range(n):
        c0 = p * V
        last = p == n - 1
        in_block = (lane >= c0) & (lane < c0 + V)
        t = jnp.where(in_block, jnp.where(lane - c0 == sub, 1.0, 0.0), rows[p])
        f = jnp.where(lane < c0 + V, t, 0.0)
        pivots = None
        below_m = {q: [lane_col(rows[q], c0 + k) for k in range(V)] for q in range(p + 1, n)}
        if not last:
            a = list(below_m[p + 1])
            ahead = [lane_col(rows[p + 1], c0 + V + k) for k in range(V)]
        for k in range(0, V, 2):
            h1, h2 = sub == k, sub == k + 1
            here = h1 | h2
            d11, d12, d22 = sub_row(cols[k], k), sub_row(cols[k + 1], k), sub_row(cols[k + 1], k + 1)
            det = d11 * d22 - d12 * d12
            r = 1.0 / det
            m1, m2 = jnp.where(here, 0.0, cols[k]), jnp.where(here, 0.0, cols[k + 1])

            def solve(col):
                v1, v2 = sub_row(col, k), sub_row(col, k + 1)
                return (d22 * v1 - d12 * v2) * r, (d11 * v2 - d12 * v1) * r

            def eliminate(col):
                u1, u2 = solve(col)
                return jnp.where(h1, u1, jnp.where(h2, u2, col - (m1 * u1 + m2 * u2))), u1, u2

            for j in range(k + 2, V):
                cols[j], u1, u2 = eliminate(cols[j])
                if not last:
                    a[j] = a[j] - (a[k] * u1 + a[k + 1] * u2)
            if not last:
                s1 = (d22 * a[k] - d12 * a[k + 1]) * r
                s2 = (d11 * a[k + 1] - d12 * a[k]) * r
                for j in range(V):
                    ahead[j] = ahead[j] - (s1 * sub_row(a[k], j) + s2 * sub_row(a[k + 1], j))
            q = 1.0 / d11
            ratio = d12 * q
            f1 = sub_row(f, k)
            f2 = sub_row(f, k + 1) - ratio * f1
            g2 = d11 * r
            g1 = q
            below = sub > k + 1
            b1 = jnp.where(below, cols[k], 0.0)
            b2 = jnp.where(below, cols[k + 1], 0.0)
            l2 = b2 - b1 * ratio
            f = jnp.where(h2, f2, f - b1 * (f1 * g1) - l2 * (f2 * g2))
            t, _, _ = eliminate(t)
            scale = jnp.where(h1, g1, g2)
            pivots = scale if pivots is None else jnp.where(here, scale, pivots)
        out.append(f * jnp.sqrt(pivots))
        if last:
            break
        cols = ahead
        w = [sub_row(t, k) for k in range(V)]
        for q in range(p + 1, n):
            acc = jnp.where(in_block, 0.0, rows[q])
            rows[q] = acc - tree([below_m[q][k] * w[k] for k in range(V)])
    return out


CORES, YS, XS, ZS = 2, 4, 4, 8
TOTAL = (128, 128, 160, 160)
HALF = tuple(t // 2 for t in TOTAL)
FIRST = tuple(t // 8 for t in TOTAL)
SECOND = tuple(t // 32 for t in TOTAL)
Z_USED = (0, 0, 5, 5)
CHUNK = tuple(t // max(z, 1) for t, z in zip(SECOND, Z_USED))
COPIES = 43
PLANE = (0,)


def grouped_blocks(n):
    first = [(0, j) for j in range(n)]
    second = [(1, j) for j in range(1, n)] + [(2, 2)]
    third = [(i, j) for i in (2, 3) for j in range(3, n)]
    rest = [(i, j) for i in range(4, n) for j in range(i, n)]
    return first, second, third, rest


def coordinates():
    band, ga = lax.axis_index("band"), lax.axis_index("ga")
    core, y = lax.rem(band, CORES), lax.rem(band // CORES, YS)
    x = (band // (CORES * YS)) * 2 + lax.rem(ga, 2)
    return core, x, y, ga // 2


def device(core, x, y, z):
    return {"band": ((x // 2) * YS + y) * CORES + core, "ga": z * 2 + lax.rem(x, 2)}


class Summing:
    def __init__(self, group, p_ref, g_ref, scratch, send, recv):
        self.group, self.p_ref, self.g_ref = group, p_ref, g_ref
        self.acc2, self.acc3, self.got1, self.got2, self.got3 = scratch
        self.send, self.recv = send, recv
        self.direct = Z_USED[group] == 0
        core, x, y, z = self.at = coordinates()
        self.core, self.z = core, z
        self.a = jnp.where(core == 0, y, x)
        self.b = jnp.where(core == 0, x, y)
        self.partner = device(1 - core, x, y, z)
        self.from_p = sum(HALF[:group])
        base = sum(TOTAL[:group])
        self.half = base + core * HALF[group]
        self.first = self.half + self.a * FIRST[group]
        self.second = self.first + self.b * SECOND[group]
        self.other_half = base + (1 - core) * HALF[group]
        self.started = []

    def along(self, stage, s):
        core, x, y, z = self.at
        if stage == "z":
            to = lax.rem(z + s, ZS)
            return to, device(core, x, y, to)
        at = self.a if stage == "first" else self.b
        to = lax.rem(at + s, 4)
        on_y = core == (0 if stage == "first" else 1)
        return to, device(core, jnp.where(on_y, x, to), jnp.where(on_y, to, y), z)

    def copy(self, src, dst, index, peer):
        return pltpu.make_async_remote_copy(
            src_ref=src,
            dst_ref=dst,
            send_sem=self.send.at[self.group * COPIES + index],
            recv_sem=self.recv.at[self.group * COPIES + index],
            device_id=peer,
            device_id_type=MESH,
        )

    def start(self, src, dst, index, peer):
        self.copy(src, dst, index, peer).start()
        self.started.append((src.shape[0], index))

    def chunk(self, at, size):
        return self.g_ref.at[pl.ds(at, size)]

    def takes(self, z, then):
        if Z_USED[self.group] == ZS:
            then()
        else:
            pl.when(z < Z_USED[self.group])(then)

    def plane_peer(self, s):
        core, x, y, z = self.at
        to = lax.rem(self.a * 4 + self.b + s, 16)
        a, b = to // 4, lax.rem(to, 4)
        return to, device(core, jnp.where(core == 0, b, a), jnp.where(core == 0, a, b), z)

    def plane_out(self):
        size = SECOND[self.group]
        for s in range(1, 16):
            to, peer = self.plane_peer(s)
            self.start(self.p_ref.at[pl.ds(self.from_p + to * size, size)], self.got1.at[s - 1], 12 + s, peer)

    def plane_sum(self):
        size = SECOND[self.group]
        for s in range(1, 16):
            self.copy(self.got1.at[s - 1], self.got1.at[s - 1], 12 + s, self.partner).wait_recv()
        own = self.p_ref[pl.ds(self.from_p + (self.a * 4 + self.b) * size, size)]
        self.acc3[...] = tree([own] + [self.got1[s] for s in range(15)])
        self.across_z()

    def plane_back(self):
        mine = self.chunk(self.second, SECOND[self.group])
        for s in range(1, 16):
            to, peer = self.plane_peer(s)
            self.start(mine, mine, 27 + s, peer)

    def plane_pass(self):
        size = SECOND[self.group]
        for s in range(1, 16):
            sender = lax.rem(self.a * 4 + self.b + 16 - s, 16)
            got = self.chunk(self.half + sender * size, size)
            self.copy(got, got, 27 + s, self.partner).wait_recv()
        mine = self.chunk(self.half, HALF[self.group])
        self.start(mine, mine, 0, self.partner)

    def plane_done(self):
        got = self.chunk(self.other_half, HALF[self.group])
        self.copy(got, got, 0, self.partner).wait_recv()

    def stage0(self):
        size = FIRST[self.group]
        for s in (2, 1, 3):
            to, peer = self.along("first", s)
            self.start(self.p_ref.at[pl.ds(self.from_p + to * size, size)], self.got1.at[s - 1], s - 1, peer)

    def stage1(self):
        size, step = FIRST[self.group], 4
        for s in range(3):
            self.copy(self.got1.at[s], self.got1.at[s], s, self.partner).wait_recv()

        def add(t, carry):
            at = pl.ds(t * step, step)
            own = self.p_ref[pl.ds(self.from_p + self.a * size + t * step, step)]
            self.acc2[at] = (own + self.got1[0, at]) + (self.got1[1, at] + self.got1[2, at])
            return carry

        lax.fori_loop(0, size // step, add, 0)
        size = SECOND[self.group]
        for s in (2, 1, 3):
            to, peer = self.along("second", s)
            self.start(self.acc2.at[pl.ds(to * size, size)], self.got2.at[s - 1], 2 + s, peer)

    def across_z(self):
        size = SECOND[self.group]
        self.got3[pl.ds(self.z, 1)] = self.acc3[...][None]
        for s in (4, 3, 5, 2, 6, 1, 7):
            to, peer = self.along("z", s)
            self.start(self.acc3, self.got3.at[self.z], 5 + s, peer)

    def stage2(self):
        size = SECOND[self.group]
        for s in range(3):
            self.copy(self.got2.at[s], self.got2.at[s], 3 + s, self.partner).wait_recv()
        own = self.acc2[pl.ds(self.b * size, size)]
        self.acc3[...] = (own + self.got2[0]) + (self.got2[1] + self.got2[2])
        if self.direct:
            self.across_z()
            return
        size = CHUNK[self.group]
        for s in (4, 3, 5, 2, 6, 1, 7):
            to, peer = self.along("z", s)

            def send():
                self.copy(self.acc3.at[pl.ds(to * size, size)], self.got3.at[s - 1], 5 + s, peer).start()

            self.takes(to, send)

    def stage3(self):
        if self.direct:
            for s in range(1, ZS):
                self.copy(self.acc3, self.got3.at[0], 5 + s, self.partner).wait_recv()
            self.g_ref[pl.ds(self.second, SECOND[self.group])] = tree([self.got3[k] for k in range(ZS)])
            self.plane_back() if self.group in PLANE else self.back()
            return
        size = CHUNK[self.group]
        own = self.second + self.z * size

        def total():
            for s in range(1, ZS):
                self.copy(self.got3.at[s - 1], self.got3.at[s - 1], 5 + s, self.partner).wait_recv()
            terms = [self.acc3[pl.ds(self.z * size, size)]] + [self.got3[s] for s in range(ZS - 1)]
            self.g_ref[pl.ds(own, size)] = tree(terms)
            for s in (4, 3, 5, 2, 6, 1, 7):
                to, peer = self.along("z", s)
                self.copy(self.chunk(own, size), self.chunk(own, size), 12 + s, peer).start()

        self.takes(self.z, total)

    def stage4(self):
        size = CHUNK[self.group]
        for s in range(1, ZS):
            sender = lax.rem(self.z + ZS - s, ZS)

            def receive():
                got = self.chunk(self.second + sender * size, size)
                self.copy(got, got, 12 + s, self.partner).wait_recv()

            self.takes(sender, receive)
        self.back()

    def back(self):
        mine = self.chunk(self.second, SECOND[self.group])
        for s in (2, 1, 3):
            to, peer = self.along("second", s)
            self.start(mine, mine, 19 + s, peer)

    def stage5(self):
        size = SECOND[self.group]
        for s in range(1, 4):
            got = self.chunk(self.first + lax.rem(self.b + 4 - s, 4) * size, size)
            self.copy(got, got, 19 + s, self.partner).wait_recv()
        mine = self.chunk(self.first, FIRST[self.group])
        for s in (2, 1, 3):
            to, peer = self.along("first", s)
            self.start(mine, mine, 22 + s, peer)
        self.start(mine, mine, 26, self.partner)

    def stage6(self):
        size = FIRST[self.group]
        for s in (1, 3, 2):
            got = self.chunk(self.half + lax.rem(self.a + 4 - s, 4) * size, size)
            self.copy(got, got, 22 + s, self.partner).wait_recv()
            self.start(got, got, 26 + s, self.partner)

    def stage7(self):
        size = FIRST[self.group]
        for s in range(4):
            got = self.chunk(self.other_half + lax.rem(self.b + 4 - s, 4) * size, size)
            self.copy(got, got, 26 + s, self.partner).wait_recv()

    def finish(self):
        for size, index in self.started:
            part = self.chunk(0, size)
            self.copy(part, part, index, self.partner).wait_send()
        if self.direct:
            return
        size = CHUNK[self.group]
        for s in range(1, ZS):
            to, peer = self.along("z", s)

            def sent():
                part = self.acc3.at[pl.ds(to * size, size)]
                self.copy(part, part, 5 + s, peer).wait_send()

            self.takes(to, sent)

            def sent_back():
                part = self.chunk(self.second, size)
                self.copy(part, part, 12 + s, peer).wait_send()

            self.takes(self.z, sent_back)


def orthonormalize_kernel(n, scale, src_ref, out_ref, *scratch):
    (own_ref, other_ref, held_hi, held_lo, p_ref, g_ref, cur_ref, d_ref, z_ref, x_ref, hi_ref, lo_ref, lane_ref) = scratch[:13]
    groups_scratch = [scratch[13 + 5 * g : 18 + 5 * g] for g in range(4)]
    (send, recv, x_send, x_recv, in_send, in_recv, pass_send, pass_recv, own_sem) = scratch[33:]
    rows_each, width = src_ref.shape[0], own_ref.shape[1]
    bands = src_ref.shape[1] // width
    per_panel = B // rows_each
    tiles = B // V
    me = lax.axis_index("band")
    core, x, y, z = coordinates()
    partner = device(1 - core, x, y, z)

    barrier = pltpu.get_barrier_semaphore()

    def greet(s, carry):
        pl.semaphore_signal(
            barrier, inc=1, device_id={"band": lax.rem(me + s, bands)}, device_id_type=MESH
        )
        return carry

    others = [device(core, x, y, lax.rem(z + s, ZS)) for s in range(1, ZS)]
    others += [device(core, lax.rem(x + s, XS), lax.rem(y + t, YS), z) for s in (1, 3) for t in range(YS)]
    for peer in others:
        pl.semaphore_signal(barrier, inc=1, device_id=peer, device_id_type=MESH)
    lax.fori_loop(1, bands, greet, 0)

    def columns(ref, index):
        return ref.at[:, pl.ds(pl.multiple_of(index * width, width), width)]

    def band(ref, index):
        return ref.at[pl.ds(pl.multiple_of(index * rows_each, rows_each), rows_each), :]

    mine = pltpu.make_async_copy(columns(src_ref, me), band(own_ref, me), own_sem)
    mine.start()
    pl.semaphore_wait(barrier, bands - 1 + len(others))

    def bring(s, source):
        peer = lax.rem(me + s, bands)
        return pltpu.make_async_remote_copy(
            src_ref=columns(src_ref, peer),
            dst_ref=band(own_ref, source),
            send_sem=in_send.at[s],
            recv_sem=in_recv.at[s],
            device_id={"band": peer},
            device_id_type=MESH,
        )

    def hand_over(source):
        return pltpu.make_async_remote_copy(
            src_ref=band(own_ref, source),
            dst_ref=band(other_ref, source),
            send_sem=pass_send.at[source],
            recv_sem=pass_recv.at[source],
            device_id=partner,
            device_id_type=MESH,
        )

    def keep(ref, source, at):
        rows = pl.ds(pl.multiple_of(source * rows_each, rows_each), rows_each)
        high, low = split(ref[rows, :])
        held_hi[rows, at : at + width] = high
        held_lo[rows, at : at + width] = low

    def start(s, carry):
        bring(s, me).start()
        return carry

    def arrive(s, carry):
        source = lax.rem(me - s + bands, bands)
        bring(s, source).wait_recv()
        hand_over(source).start()
        keep(own_ref, source, 0)
        return carry

    def finish(s, carry):
        source = lax.rem(me + 1 - 2 * core - s + bands, bands)
        hand_over(source).wait_recv()
        keep(other_ref, source, width)
        return carry

    def sent(s, carry):
        bring(s, me).wait_send()
        hand_over(lax.rem(me + s, bands)).wait_send()
        return carry

    lax.fori_loop(1, bands, start, 0)
    mine.wait()
    hand_over(me).start()
    keep(own_ref, me, 0)
    lax.fori_loop(1, bands, arrive, 0)
    lax.fori_loop(0, bands, finish, 0)

    groups = grouped_blocks(n)

    def multiply(g):
        half = len(groups[g]) // CORES
        for c in range(CORES):

            @pl.when(core == c)
            def _():
                blocks = groups[g][c * half : (c + 1) * half]
                for i in sorted({i for i, _ in blocks}):
                    wanted = [j for k, j in blocks if k == i]
                    first, end = min(wanted), max(wanted) + 1
                    left = (held_hi[i * B : (i + 1) * B], held_lo[i * B : (i + 1) * B])
                    right = (held_hi[first * B : end * B], held_lo[first * B : end * B])
                    out = dot3(left, right, ((1,), (1,))) * scale
                    for j in wanted:
                        at = sum(HALF[:g]) + blocks.index((i, j)) * tiles
                        block = out[:, (j - first) * B : (j - first + 1) * B]
                        p_ref[at : at + tiles] = block.reshape(tiles, V, B)

    one, two, three, four = (Summing(g, p_ref, g_ref, groups_scratch[g], send, recv) for g in range(4))
    multiply(0)
    one.plane_out()
    multiply(1)
    two.stage0()
    multiply(2)
    three.stage0()
    multiply(3)
    four.stage0()
    two.stage1()
    one.plane_sum()
    three.stage1()
    two.stage2()
    four.stage1()
    three.stage2()
    one.stage3()
    four.stage2()
    two.stage3()
    three.stage3()
    two.stage5()
    four.stage3()
    three.stage4()
    one.plane_pass()
    four.stage4()
    two.stage6()
    one.plane_done()
    three.stage5()

    order = [block for group in groups for block in group]
    sub = lax.broadcasted_iota(jnp.int32, (V, B), 0)
    lane = lax.broadcasted_iota(jnp.int32, (V, B), 1)

    def prepare(k):
        at = order.index((k, k)) * tiles
        on_diagonal = [jnp.where(lane == q * V + sub, g_ref[at + q], 0.0) for q in range(tiles)]
        diagonal = jnp.sum(tree(on_diagonal), axis=0, keepdims=True)
        lanes = jnp.broadcast_to(lax.rsqrt(diagonal), (V, B))
        lane_ref[...] = lanes
        taken = None
        if k:
            left = (hi_ref[: k * B, k * B : (k + 1) * B], lo_ref[: k * B, k * B : (k + 1) * B])
            right = (hi_ref[: k * B, k * B :], lo_ref[: k * B, k * B :])
            taken = dot3(left, right, ((0,), (0,)))
        for j in range(k, n + width // B):
            if j < n:
                at = order.index((k, j)) * tiles
                block = g_ref[at : at + tiles].reshape(B, B)
            else:
                block = own_ref[k * B : (k + 1) * B, (j - n) * B : (j - n + 1) * B]
            if k:
                block = block - taken[:, (j - k) * B : (j - k + 1) * B]
            if j > k:
                cur_ref[:, j * B : (j + 1) * B] = block
                continue
            for q in range(tiles):
                rows = jnp.take_along_axis(lanes, q * V + sub, axis=1)
                d_ref[q * V : (q + 1) * V, :] = block[q * V : (q + 1) * V] * rows * lanes

    def remote(peer, sender):
        return pltpu.make_async_remote_copy(
            src_ref=x_ref.at[pl.ds(peer * rows_each, rows_each), :],
            dst_ref=columns(out_ref, sender),
            send_sem=x_send.at[peer],
            recv_sem=x_recv.at[sender],
            device_id={"band": peer},
            device_id_type=MESH,
        )

    stays = pltpu.make_async_copy(band(x_ref, me), columns(out_ref, me), own_sem)

    def step(i, carry):
        for k in range(n):

            @pl.when(i == k)
            def _():
                if k == 1:
                    two.stage7()
                if k == 2:
                    three.stage7()
                if k == 4:
                    four.stage7()
                prepare(k)

        rows = [d_ref[q * V : (q + 1) * V, :] for q in range(tiles)]
        lanes = lane_ref[...]
        for q, inverse in enumerate(factor_inverse(rows)):
            z_ref[q * V : (q + 1) * V, :] = inverse * lanes
        for k in range(n):

            @pl.when(i == k)
            def _():
                if k == 0:
                    four.stage5()
                    three.stage6()
                if k == 1:
                    four.stage6()
                panel = dot3(split(z_ref[...]), split(cur_ref[:, (k + 1) * B :]), ((1,), (0,)))
                x_ref[k * B : (k + 1) * B, :] = panel[:, panel.shape[1] - width :]
                for peer in range(k * per_panel, (k + 1) * per_panel):

                    @pl.when(peer != me)
                    def _():
                        remote(peer, me).start()

                    @pl.when(peer == me)
                    def _():
                        stays.start()

                if k < n - 1:
                    high, low = split(panel)
                    hi_ref[k * B : (k + 1) * B, (k + 1) * B :] = high
                    lo_ref[k * B : (k + 1) * B, (k + 1) * B :] = low

        return carry

    lax.fori_loop(0, n, step, 0)
    lax.fori_loop(1, bands, sent, 0)
    hand_over(me).wait_send()
    for group in (one, two, three, four):
        group.finish()
    stays.wait()
    for other in range(bands):

        @pl.when(other != me)
        def _():
            remote(other, me).wait_send()
            remote(other, other).wait_recv()


def orthonormalize(coeffs, bands, columns_all):
    rows_each, columns = coeffs.shape
    rows, width = rows_each * bands, columns // bands
    n = rows // B
    tiles = lambda *shape: pltpu.VMEM((*shape, V, B), jnp.float32)
    whole = n * B + width
    summing = []
    for g in range(4):
        summing += [tiles(FIRST[g]), tiles(SECOND[g]), tiles(*((15, SECOND[g]) if g in PLANE else (3, FIRST[g]))), tiles(3, SECOND[g])]
        summing += [tiles(ZS - 1, CHUNK[g]) if Z_USED[g] else tiles(ZS, SECOND[g])]
    return pl.pallas_call(
        functools.partial(orthonormalize_kernel, n, 1.0 / columns_all),
        out_shape=jax.ShapeDtypeStruct(coeffs.shape, jnp.float32),
        in_specs=[pl.BlockSpec(memory_space=pltpu.HBM)],
        out_specs=pl.BlockSpec(memory_space=pltpu.VMEM),
        scratch_shapes=[
            pltpu.VMEM((rows, width), jnp.float32),
            pltpu.VMEM((rows, width), jnp.float32),
            pltpu.VMEM((rows, CORES * width), jnp.bfloat16),
            pltpu.VMEM((rows, CORES * width), jnp.bfloat16),
            tiles(sum(HALF)),
            tiles(sum(TOTAL)),
            pltpu.VMEM((B, whole), jnp.float32),
            pltpu.VMEM((B, B), jnp.float32),
            pltpu.VMEM((B, B), jnp.float32),
            pltpu.VMEM((rows, width), jnp.float32),
            pltpu.VMEM((rows, whole), jnp.bfloat16),
            pltpu.VMEM((rows, whole), jnp.bfloat16),
            pltpu.VMEM((V, B), jnp.float32),
            *summing,
            pltpu.SemaphoreType.DMA((4 * COPIES,)),
            pltpu.SemaphoreType.DMA((4 * COPIES,)),
            *[pltpu.SemaphoreType.DMA((bands,))] * 6,
            pltpu.SemaphoreType.DMA,
        ],
        compiler_params=pltpu.CompilerParams(
            collective_id=0, has_side_effects=True, vmem_limit_bytes=52 << 20
        ),
        name="orthonormalize",
    )(coeffs)


def local(coeffs):
    bands = lax.axis_size("band")
    return orthonormalize(coeffs, bands, coeffs.shape[1] * lax.axis_size("ga"))


def solution(mesh):
    return jax.shard_map(
        local,
        mesh=mesh,
        in_specs=(P("band", "ga"),),
        out_specs=P("band", "ga"),
        check_vma=False,
    )
```

```python
import functools

import jax
import jax.numpy as jnp
from jax import lax
from jax.experimental import pallas as pl
from jax.experimental.pallas import tpu as pltpu
from jax.sharding import PartitionSpec as P

MESH = pl.DeviceIdType.MESH

B = 128
V = 8


def split(x):
    hi = x.astype(jnp.bfloat16)
    return hi, (x - hi.astype(jnp.float32)).astype(jnp.bfloat16)


def dot3(a, b, dims):
    (ca,), (cb,) = dims
    ah, al = a
    bh, bl = b
    left = jnp.concatenate([ah, al, ah], axis=ca)
    right = jnp.concatenate([bh, bh, bl], axis=cb)
    return lax.dot_general(left, right, (dims, ((), ())), preferred_element_type=jnp.float32)


def lane_col(t, c):
    return jnp.take_along_axis(t, jnp.full((V, B), c, jnp.int32), axis=1)


def sub_row(t, k):
    return jnp.broadcast_to(t[k : k + 1, :], (V, B))


def tree(m):
    while len(m) > 1:
        m = [m[e] + m[e + 1] if e + 1 < len(m) else m[e] for e in range(0, len(m), 2)]
    return m[0]


def factor_inverse(rows):
    n = len(rows)
    rows = list(rows)
    sub = lax.broadcasted_iota(jnp.int32, (V, B), 0)
    lane = lax.broadcasted_iota(jnp.int32, (V, B), 1)
    out = []
    cols = [lane_col(rows[0], k) for k in range(V)]
    for p in range(n):
        c0 = p * V
        last = p == n - 1
        in_block = (lane >= c0) & (lane < c0 + V)
        t = jnp.where(in_block, jnp.where(lane - c0 == sub, 1.0, 0.0), rows[p])
        f = jnp.where(lane < c0 + V, t, 0.0)
        pivots = None
        below_m = {q: [lane_col(rows[q], c0 + k) for k in range(V)] for q in range(p + 1, n)}
        if not last:
            a = list(below_m[p + 1])
            ahead = [lane_col(rows[p + 1], c0 + V + k) for k in range(V)]
        for k in range(0, V, 2):
            h1, h2 = sub == k, sub == k + 1
            here = h1 | h2
            d11, d12, d22 = sub_row(cols[k], k), sub_row(cols[k + 1], k), sub_row(cols[k + 1], k + 1)
            det = d11 * d22 - d12 * d12
            r = 1.0 / det
            m1, m2 = jnp.where(here, 0.0, cols[k]), jnp.where(here, 0.0, cols[k + 1])

            def solve(col):
                v1, v2 = sub_row(col, k), sub_row(col, k + 1)
                return (d22 * v1 - d12 * v2) * r, (d11 * v2 - d12 * v1) * r

            def eliminate(col):
                u1, u2 = solve(col)
                return jnp.where(h1, u1, jnp.where(h2, u2, col - (m1 * u1 + m2 * u2))), u1, u2

            for j in range(k + 2, V):
                cols[j], u1, u2 = eliminate(cols[j])
                if not last:
                    a[j] = a[j] - (a[k] * u1 + a[k + 1] * u2)
            if not last:
                s1 = (d22 * a[k] - d12 * a[k + 1]) * r
                s2 = (d11 * a[k + 1] - d12 * a[k]) * r
                for j in range(V):
                    ahead[j] = ahead[j] - (s1 * sub_row(a[k], j) + s2 * sub_row(a[k + 1], j))
            q = 1.0 / d11
            ratio = d12 * q
            f1 = sub_row(f, k)
            f2 = sub_row(f, k + 1) - ratio * f1
            g2 = d11 * r
            g1 = q
            below = sub > k + 1
            b1 = jnp.where(below, cols[k], 0.0)
            b2 = jnp.where(below, cols[k + 1], 0.0)
            l2 = b2 - b1 * ratio
            f = jnp.where(h2, f2, f - b1 * (f1 * g1) - l2 * (f2 * g2))
            t, _, _ = eliminate(t)
            scale = jnp.where(h1, g1, g2)
            pivots = scale if pivots is None else jnp.where(here, scale, pivots)
        out.append(f * jnp.sqrt(pivots))
        if last:
            break
        cols = ahead
        w = [sub_row(t, k) for k in range(V)]
        for q in range(p + 1, n):
            acc = jnp.where(in_block, 0.0, rows[q])
            rows[q] = acc - tree([below_m[q][k] * w[k] for k in range(V)])
    return out


CORES, YS, XS, ZS = 2, 4, 4, 8
TOTAL = (128, 128, 160, 160)
HALF = tuple(t // 2 for t in TOTAL)
FIRST = tuple(t // 8 for t in TOTAL)
SECOND = tuple(t // 32 for t in TOTAL)
Z_USED = (0, 0, 0, 0)
CHUNK = tuple(t // max(z, 1) for t, z in zip(SECOND, Z_USED))
COPIES = 30


def grouped_blocks(n):
    first = [(0, j) for j in range(n)]
    second = [(1, j) for j in range(1, n)] + [(2, 2)]
    third = [(i, j) for i in (2, 3) for j in range(3, n)]
    rest = [(i, j) for i in range(4, n) for j in range(i, n)]
    return first, second, third, rest


def coordinates():
    band, ga = lax.axis_index("band"), lax.axis_index("ga")
    core, y = lax.rem(band, CORES), lax.rem(band // CORES, YS)
    x = (band // (CORES * YS)) * 2 + lax.rem(ga, 2)
    return core, x, y, ga // 2


def device(core, x, y, z):
    return {"band": ((x // 2) * YS + y) * CORES + core, "ga": z * 2 + lax.rem(x, 2)}


class Summing:
    def __init__(self, group, p_ref, g_ref, scratch, send, recv):
        self.group, self.p_ref, self.g_ref = group, p_ref, g_ref
        self.acc2, self.acc3, self.got1, self.got2, self.got3 = scratch
        self.send, self.recv = send, recv
        self.direct = Z_USED[group] == 0
        core, x, y, z = self.at = coordinates()
        self.core, self.z = core, z
        self.a = jnp.where(core == 0, y, x)
        self.b = jnp.where(core == 0, x, y)
        self.partner = device(1 - core, x, y, z)
        self.from_p = sum(HALF[:group])
        base = sum(TOTAL[:group])
        self.half = base + core * HALF[group]
        self.first = self.half + self.a * FIRST[group]
        self.second = self.first + self.b * SECOND[group]
        self.other_half = base + (1 - core) * HALF[group]
        self.started = []

    def along(self, stage, s):
        core, x, y, z = self.at
        if stage == "z":
            to = lax.rem(z + s, ZS)
            return to, device(core, x, y, to)
        at = self.a if stage == "first" else self.b
        to = lax.rem(at + s, 4)
        on_y = core == (0 if stage == "first" else 1)
        return to, device(core, jnp.where(on_y, x, to), jnp.where(on_y, to, y), z)

    def copy(self, src, dst, index, peer):
        return pltpu.make_async_remote_copy(
            src_ref=src,
            dst_ref=dst,
            send_sem=self.send.at[self.group * COPIES + index],
            recv_sem=self.recv.at[self.group * COPIES + index],
            device_id=peer,
            device_id_type=MESH,
        )

    def start(self, src, dst, index, peer):
        self.copy(src, dst, index, peer).start()
        self.started.append((src.shape[0], index))

    def chunk(self, at, size):
        return self.g_ref.at[pl.ds(at, size)]

    def takes(self, z, then):
        if Z_USED[self.group] == ZS:
            then()
        else:
            pl.when(z < Z_USED[self.group])(then)

    def stage0(self):
        size = FIRST[self.group]
        for s in (2, 1, 3):
            to, peer = self.along("first", s)
            self.start(self.p_ref.at[pl.ds(self.from_p + to * size, size)], self.got1.at[s - 1], s - 1, peer)

    def stage1(self):
        size, step = FIRST[self.group], 4
        for s in range(3):
            self.copy(self.got1.at[s], self.got1.at[s], s, self.partner).wait_recv()

        def add(t, carry):
            at = pl.ds(t * step, step)
            own = self.p_ref[pl.ds(self.from_p + self.a * size + t * step, step)]
            self.acc2[at] = (own + self.got1[0, at]) + (self.got1[1, at] + self.got1[2, at])
            return carry

        lax.fori_loop(0, size // step, add, 0)
        size = SECOND[self.group]
        for s in (2, 1, 3):
            to, peer = self.along("second", s)
            self.start(self.acc2.at[pl.ds(to * size, size)], self.got2.at[s - 1], 2 + s, peer)

    def across_z(self):
        size = SECOND[self.group]
        self.got3[pl.ds(self.z, 1)] = self.acc3[...][None]
        for s in (4, 3, 5, 2, 6, 1, 7):
            to, peer = self.along("z", s)
            self.start(self.acc3, self.got3.at[self.z], 5 + s, peer)

    def stage2(self):
        size = SECOND[self.group]
        for s in range(3):
            self.copy(self.got2.at[s], self.got2.at[s], 3 + s, self.partner).wait_recv()
        own = self.acc2[pl.ds(self.b * size, size)]
        self.acc3[...] = (own + self.got2[0]) + (self.got2[1] + self.got2[2])
        if self.direct:
            self.across_z()
            return
        size = CHUNK[self.group]
        for s in (4, 3, 5, 2, 6, 1, 7):
            to, peer = self.along("z", s)

            def send():
                self.copy(self.acc3.at[pl.ds(to * size, size)], self.got3.at[s - 1], 5 + s, peer).start()

            self.takes(to, send)

    def stage3(self):
        if self.direct:
            for s in range(1, ZS):
                self.copy(self.acc3, self.got3.at[0], 5 + s, self.partner).wait_recv()
            self.g_ref[pl.ds(self.second, SECOND[self.group])] = tree([self.got3[k] for k in range(ZS)])
            self.back()
            return
        size = CHUNK[self.group]
        own = self.second + self.z * size

        def total():
            for s in range(1, ZS):
                self.copy(self.got3.at[s - 1], self.got3.at[s - 1], 5 + s, self.partner).wait_recv()
            terms = [self.acc3[pl.ds(self.z * size, size)]] + [self.got3[s] for s in range(ZS - 1)]
            self.g_ref[pl.ds(own, size)] = tree(terms)
            for s in (4, 3, 5, 2, 6, 1, 7):
                to, peer = self.along("z", s)
                self.copy(self.chunk(own, size), self.chunk(own, size), 12 + s, peer).start()

        self.takes(self.z, total)

    def stage4(self):
        size = CHUNK[self.group]
        for s in range(1, ZS):
            sender = lax.rem(self.z + ZS - s, ZS)

            def receive():
                got = self.chunk(self.second + sender * size, size)
                self.copy(got, got, 12 + s, self.partner).wait_recv()

            self.takes(sender, receive)
        self.back()

    def back(self):
        mine = self.chunk(self.second, SECOND[self.group])
        for s in (2, 1, 3):
            to, peer = self.along("second", s)
            self.start(mine, mine, 19 + s, peer)

    def stage5(self):
        size = SECOND[self.group]
        for s in range(1, 4):
            got = self.chunk(self.first + lax.rem(self.b + 4 - s, 4) * size, size)
            self.copy(got, got, 19 + s, self.partner).wait_recv()
        mine = self.chunk(self.first, FIRST[self.group])
        for s in (2, 1, 3):
            to, peer = self.along("first", s)
            self.start(mine, mine, 22 + s, peer)
        self.start(mine, mine, 26, self.partner)

    def stage6(self):
        size = FIRST[self.group]
        for s in (1, 3, 2):
            got = self.chunk(self.half + lax.rem(self.a + 4 - s, 4) * size, size)
            self.copy(got, got, 22 + s, self.partner).wait_recv()
            self.start(got, got, 26 + s, self.partner)

    def stage7(self):
        size = FIRST[self.group]
        for s in range(4):
            got = self.chunk(self.other_half + lax.rem(self.b + 4 - s, 4) * size, size)
            self.copy(got, got, 26 + s, self.partner).wait_recv()

    def finish(self):
        for size, index in self.started:
            part = self.chunk(0, size)
            self.copy(part, part, index, self.partner).wait_send()
        if self.direct:
            return
        size = CHUNK[self.group]
        for s in range(1, ZS):
            to, peer = self.along("z", s)

            def sent():
                part = self.acc3.at[pl.ds(to * size, size)]
                self.copy(part, part, 5 + s, peer).wait_send()

            self.takes(to, sent)

            def sent_back():
                part = self.chunk(self.second, size)
                self.copy(part, part, 12 + s, peer).wait_send()

            self.takes(self.z, sent_back)


def orthonormalize_kernel(n, scale, src_ref, out_ref, *scratch):
    (own_ref, other_ref, held_hi, held_lo, p_ref, g_ref, cur_ref, d_ref, z_ref, x_ref, hi_ref, lo_ref, lane_ref) = scratch[:13]
    groups_scratch = [scratch[13 + 5 * g : 18 + 5 * g] for g in range(4)]
    (send, recv, x_send, x_recv, in_send, in_recv, pass_send, pass_recv, own_sem) = scratch[33:]
    rows_each, width = src_ref.shape[0], own_ref.shape[1]
    bands = src_ref.shape[1] // width
    per_panel = B // rows_each
    tiles = B // V
    me = lax.axis_index("band")
    core, x, y, z = coordinates()
    partner = device(1 - core, x, y, z)

    barrier = pltpu.get_barrier_semaphore()

    def greet(s, carry):
        pl.semaphore_signal(
            barrier, inc=1, device_id={"band": lax.rem(me + s, bands)}, device_id_type=MESH
        )
        return carry

    others = [device(core, x, y, lax.rem(z + s, ZS)) for s in range(1, ZS)]
    others += [device(core, lax.rem(x + s, XS), y, z) for s in (1, 3)]
    for peer in others:
        pl.semaphore_signal(barrier, inc=1, device_id=peer, device_id_type=MESH)
    lax.fori_loop(1, bands, greet, 0)

    def columns(ref, index):
        return ref.at[:, pl.ds(pl.multiple_of(index * width, width), width)]

    def band(ref, index):
        return ref.at[pl.ds(pl.multiple_of(index * rows_each, rows_each), rows_each), :]

    mine = pltpu.make_async_copy(columns(src_ref, me), band(own_ref, me), own_sem)
    mine.start()
    pl.semaphore_wait(barrier, bands - 1 + len(others))

    def bring(s, source):
        peer = lax.rem(me + s, bands)
        return pltpu.make_async_remote_copy(
            src_ref=columns(src_ref, peer),
            dst_ref=band(own_ref, source),
            send_sem=in_send.at[s],
            recv_sem=in_recv.at[s],
            device_id={"band": peer},
            device_id_type=MESH,
        )

    def hand_over(source):
        return pltpu.make_async_remote_copy(
            src_ref=band(own_ref, source),
            dst_ref=band(other_ref, source),
            send_sem=pass_send.at[source],
            recv_sem=pass_recv.at[source],
            device_id=partner,
            device_id_type=MESH,
        )

    def keep(ref, source, at):
        rows = pl.ds(pl.multiple_of(source * rows_each, rows_each), rows_each)
        high, low = split(ref[rows, :])
        held_hi[rows, at : at + width] = high
        held_lo[rows, at : at + width] = low

    def start(s, carry):
        bring(s, me).start()
        return carry

    def arrive(s, carry):
        source = lax.rem(me - s + bands, bands)
        bring(s, source).wait_recv()
        hand_over(source).start()
        keep(own_ref, source, 0)
        return carry

    def finish(s, carry):
        source = lax.rem(me + 1 - 2 * core - s + bands, bands)
        hand_over(source).wait_recv()
        keep(other_ref, source, width)
        return carry

    def sent(s, carry):
        bring(s, me).wait_send()
        hand_over(lax.rem(me + s, bands)).wait_send()
        return carry

    lax.fori_loop(1, bands, start, 0)
    mine.wait()
    hand_over(me).start()
    keep(own_ref, me, 0)
    lax.fori_loop(1, bands, arrive, 0)
    lax.fori_loop(0, bands, finish, 0)

    groups = grouped_blocks(n)

    def multiply(g):
        half = len(groups[g]) // CORES
        for c in range(CORES):

            @pl.when(core == c)
            def _():
                blocks = groups[g][c * half : (c + 1) * half]
                for i in sorted({i for i, _ in blocks}):
                    wanted = [j for k, j in blocks if k == i]
                    first, end = min(wanted), max(wanted) + 1
                    left = (held_hi[i * B : (i + 1) * B], held_lo[i * B : (i + 1) * B])
                    right = (held_hi[first * B : end * B], held_lo[first * B : end * B])
                    out = dot3(left, right, ((1,), (1,))) * scale
                    for j in wanted:
                        at = sum(HALF[:g]) + blocks.index((i, j)) * tiles
                        block = out[:, (j - first) * B : (j - first + 1) * B]
                        p_ref[at : at + tiles] = block.reshape(tiles, V, B)

    one, two, three, four = (Summing(g, p_ref, g_ref, groups_scratch[g], send, recv) for g in range(4))
    multiply(0)
    one.stage0()
    multiply(1)
    two.stage0()
    multiply(2)
    three.stage0()
    multiply(3)
    four.stage0()
    one.stage1()
    two.stage1()
    one.stage2()
    three.stage1()
    two.stage2()
    four.stage1()
    three.stage2()
    one.stage3()
    four.stage2()
    two.stage3()
    one.stage5()
    three.stage3()
    two.stage5()
    four.stage3()
    one.stage6()
    three.stage5()
    two.stage6()
    one.stage7()
    four.stage5()

    order = [block for group in groups for block in group]
    sub = lax.broadcasted_iota(jnp.int32, (V, B), 0)
    lane = lax.broadcasted_iota(jnp.int32, (V, B), 1)

    def prepare(k):
        at = order.index((k, k)) * tiles
        on_diagonal = [jnp.where(lane == q * V + sub, g_ref[at + q], 0.0) for q in range(tiles)]
        diagonal = jnp.sum(tree(on_diagonal), axis=0, keepdims=True)
        lanes = jnp.broadcast_to(lax.rsqrt(diagonal), (V, B))
        lane_ref[...] = lanes
        taken = None
        if k:
            left = (hi_ref[: k * B, k * B : (k + 1) * B], lo_ref[: k * B, k * B : (k + 1) * B])
            right = (hi_ref[: k * B, k * B :], lo_ref[: k * B, k * B :])
            taken = dot3(left, right, ((0,), (0,)))
        for j in range(k, n + width // B):
            if j < n:
                at = order.index((k, j)) * tiles
                block = g_ref[at : at + tiles].reshape(B, B)
            else:
                block = own_ref[k * B : (k + 1) * B, (j - n) * B : (j - n + 1) * B]
            if k:
                block = block - taken[:, (j - k) * B : (j - k + 1) * B]
            if j > k:
                cur_ref[:, j * B : (j + 1) * B] = block
                continue
            for q in range(tiles):
                rows = jnp.take_along_axis(lanes, q * V + sub, axis=1)
                d_ref[q * V : (q + 1) * V, :] = block[q * V : (q + 1) * V] * rows * lanes

    def remote(peer, sender):
        return pltpu.make_async_remote_copy(
            src_ref=x_ref.at[pl.ds(peer * rows_each, rows_each), :],
            dst_ref=columns(out_ref, sender),
            send_sem=x_send.at[peer],
            recv_sem=x_recv.at[sender],
            device_id={"band": peer},
            device_id_type=MESH,
        )

    stays = pltpu.make_async_copy(band(x_ref, me), columns(out_ref, me), own_sem)

    def step(i, carry):
        for k in range(n):

            @pl.when(i == k)
            def _():
                if k == 1:
                    two.stage7()
                if k == 2:
                    three.stage7()
                if k == 4:
                    four.stage7()
                prepare(k)

        rows = [d_ref[q * V : (q + 1) * V, :] for q in range(tiles)]
        lanes = lane_ref[...]
        for q, inverse in enumerate(factor_inverse(rows)):
            z_ref[q * V : (q + 1) * V, :] = inverse * lanes
        for k in range(n):

            @pl.when(i == k)
            def _():
                if k == 0:
                    three.stage6()
                if k == 1:
                    four.stage6()
                panel = dot3(split(z_ref[...]), split(cur_ref[:, (k + 1) * B :]), ((1,), (0,)))
                x_ref[k * B : (k + 1) * B, :] = panel[:, panel.shape[1] - width :]
                for peer in range(k * per_panel, (k + 1) * per_panel):

                    @pl.when(peer != me)
                    def _():
                        remote(peer, me).start()

                    @pl.when(peer == me)
                    def _():
                        stays.start()

                if k < n - 1:
                    high, low = split(panel)
                    hi_ref[k * B : (k + 1) * B, (k + 1) * B :] = high
                    lo_ref[k * B : (k + 1) * B, (k + 1) * B :] = low

        return carry

    lax.fori_loop(0, n, step, 0)
    lax.fori_loop(1, bands, sent, 0)
    hand_over(me).wait_send()
    for group in (one, two, three, four):
        group.finish()
    stays.wait()
    for other in range(bands):

        @pl.when(other != me)
        def _():
            remote(other, me).wait_send()
            remote(other, other).wait_recv()


def orthonormalize(coeffs, bands, columns_all):
    rows_each, columns = coeffs.shape
    rows, width = rows_each * bands, columns // bands
    n = rows // B
    tiles = lambda *shape: pltpu.VMEM((*shape, V, B), jnp.float32)
    whole = n * B + width
    summing = []
    for g in range(4):
        summing += [tiles(FIRST[g]), tiles(SECOND[g]), tiles(3, FIRST[g]), tiles(3, SECOND[g])]
        summing += [tiles(ZS - 1, CHUNK[g]) if Z_USED[g] else tiles(ZS, SECOND[g])]
    return pl.pallas_call(
        functools.partial(orthonormalize_kernel, n, 1.0 / columns_all),
        out_shape=jax.ShapeDtypeStruct(coeffs.shape, jnp.float32),
        in_specs=[pl.BlockSpec(memory_space=pltpu.HBM)],
        out_specs=pl.BlockSpec(memory_space=pltpu.VMEM),
        scratch_shapes=[
            pltpu.VMEM((rows, width), jnp.float32),
            pltpu.VMEM((rows, width), jnp.float32),
            pltpu.VMEM((rows, CORES * width), jnp.bfloat16),
            pltpu.VMEM((rows, CORES * width), jnp.bfloat16),
            tiles(sum(HALF)),
            tiles(sum(TOTAL)),
            pltpu.VMEM((B, whole), jnp.float32),
            pltpu.VMEM((B, B), jnp.float32),
            pltpu.VMEM((B, B), jnp.float32),
            pltpu.VMEM((rows, width), jnp.float32),
            pltpu.VMEM((rows, whole), jnp.bfloat16),
            pltpu.VMEM((rows, whole), jnp.bfloat16),
            pltpu.VMEM((V, B), jnp.float32),
            *summing,
            pltpu.SemaphoreType.DMA((4 * COPIES,)),
            pltpu.SemaphoreType.DMA((4 * COPIES,)),
            *[pltpu.SemaphoreType.DMA((bands,))] * 6,
            pltpu.SemaphoreType.DMA,
        ],
        compiler_params=pltpu.CompilerParams(
            collective_id=0, has_side_effects=True, vmem_limit_bytes=52 << 20
        ),
        name="orthonormalize",
    )(coeffs)


def local(coeffs):
    bands = lax.axis_size("band")
    return orthonormalize(coeffs, bands, coeffs.shape[1] * lax.axis_size("ga"))


def solution(mesh):
    return jax.shard_map(
        local,
        mesh=mesh,
        in_specs=(P("band", "ga"),),
        out_specs=P("band", "ga"),
        check_vma=False,
    )
```

```python
import functools

import jax
import jax.numpy as jnp
from jax import lax
from jax.experimental import pallas as pl
from jax.experimental.pallas import tpu as pltpu
from jax.sharding import PartitionSpec as P

MESH = pl.DeviceIdType.MESH

B = 128
V = 8


def split(x):
    hi = x.astype(jnp.bfloat16)
    return hi, (x - hi.astype(jnp.float32)).astype(jnp.bfloat16)


def dot3(a, b, dims):
    (ca,), (cb,) = dims
    ah, al = a
    bh, bl = b
    left = jnp.concatenate([ah, al, ah], axis=ca)
    right = jnp.concatenate([bh, bh, bl], axis=cb)
    return lax.dot_general(left, right, (dims, ((), ())), preferred_element_type=jnp.float32)


def lane_col(t, c):
    return jnp.take_along_axis(t, jnp.full((V, B), c, jnp.int32), axis=1)


def sub_row(t, k):
    return jnp.broadcast_to(t[k : k + 1, :], (V, B))


def tree(m):
    while len(m) > 1:
        m = [m[e] + m[e + 1] if e + 1 < len(m) else m[e] for e in range(0, len(m), 2)]
    return m[0]


def factor_inverse(rows):
    n = len(rows)
    rows = list(rows)
    sub = lax.broadcasted_iota(jnp.int32, (V, B), 0)
    lane = lax.broadcasted_iota(jnp.int32, (V, B), 1)
    out = []
    cols = [lane_col(rows[0], k) for k in range(V)]
    for p in range(n):
        c0 = p * V
        last = p == n - 1
        in_block = (lane >= c0) & (lane < c0 + V)
        t = jnp.where(in_block, jnp.where(lane - c0 == sub, 1.0, 0.0), rows[p])
        f = jnp.where(lane < c0 + V, t, 0.0)
        pivots = None
        below_m = {q: [lane_col(rows[q], c0 + k) for k in range(V)] for q in range(p + 1, n)}
        if not last:
            a = list(below_m[p + 1])
            ahead = [lane_col(rows[p + 1], c0 + V + k) for k in range(V)]
        for k in range(0, V, 2):
            h1, h2 = sub == k, sub == k + 1
            here = h1 | h2
            d11, d12, d22 = sub_row(cols[k], k), sub_row(cols[k + 1], k), sub_row(cols[k + 1], k + 1)
            det = d11 * d22 - d12 * d12
            r = 1.0 / det
            m1, m2 = jnp.where(here, 0.0, cols[k]), jnp.where(here, 0.0, cols[k + 1])

            def solve(col):
                v1, v2 = sub_row(col, k), sub_row(col, k + 1)
                return (d22 * v1 - d12 * v2) * r, (d11 * v2 - d12 * v1) * r

            def eliminate(col):
                u1, u2 = solve(col)
                return jnp.where(h1, u1, jnp.where(h2, u2, col - (m1 * u1 + m2 * u2))), u1, u2

            for j in range(k + 2, V):
                cols[j], u1, u2 = eliminate(cols[j])
                if not last:
                    a[j] = a[j] - (a[k] * u1 + a[k + 1] * u2)
            if not last:
                s1 = (d22 * a[k] - d12 * a[k + 1]) * r
                s2 = (d11 * a[k + 1] - d12 * a[k]) * r
                for j in range(V):
                    ahead[j] = ahead[j] - (s1 * sub_row(a[k], j) + s2 * sub_row(a[k + 1], j))
            q = 1.0 / d11
            ratio = d12 * q
            f1 = sub_row(f, k)
            f2 = sub_row(f, k + 1) - ratio * f1
            g2 = d11 * r
            g1 = q
            below = sub > k + 1
            b1 = jnp.where(below, cols[k], 0.0)
            b2 = jnp.where(below, cols[k + 1], 0.0)
            l2 = b2 - b1 * ratio
            f = jnp.where(h2, f2, f - b1 * (f1 * g1) - l2 * (f2 * g2))
            t, _, _ = eliminate(t)
            scale = jnp.where(h1, g1, g2)
            pivots = scale if pivots is None else jnp.where(here, scale, pivots)
        out.append(f * jnp.sqrt(pivots))
        if last:
            break
        cols = ahead
        w = [sub_row(t, k) for k in range(V)]
        for q in range(p + 1, n):
            acc = jnp.where(in_block, 0.0, rows[q])
            rows[q] = acc - tree([below_m[q][k] * w[k] for k in range(V)])
    return out


CORES, YS, XS, ZS = 2, 4, 4, 8
TOTAL = (128, 128, 160, 160)
HALF = tuple(t // 2 for t in TOTAL)
FIRST = tuple(t // 8 for t in TOTAL)
SECOND = tuple(t // 32 for t in TOTAL)
Z_USED = (0, 0, 0, 0)
CHUNK = tuple(t // max(z, 1) for t, z in zip(SECOND, Z_USED))
COPIES = 30


def grouped_blocks(n):
    first = [(0, j) for j in range(n)]
    second = [(1, j) for j in range(1, n)] + [(2, 2)]
    third = [(i, j) for i in (2, 3) for j in range(3, n)]
    rest = [(i, j) for i in range(4, n) for j in range(i, n)]
    return first, second, third, rest


def coordinates():
    band, ga = lax.axis_index("band"), lax.axis_index("ga")
    core, y = lax.rem(band, CORES), lax.rem(band // CORES, YS)
    x = (band // (CORES * YS)) * 2 + lax.rem(ga, 2)
    return core, x, y, ga // 2


def device(core, x, y, z):
    return {"band": ((x // 2) * YS + y) * CORES + core, "ga": z * 2 + lax.rem(x, 2)}


class Summing:
    def __init__(self, group, p_ref, g_ref, scratch, send, recv):
        self.group, self.p_ref, self.g_ref = group, p_ref, g_ref
        self.acc2, self.acc3, self.got1, self.got2, self.got3 = scratch
        self.send, self.recv = send, recv
        self.direct = Z_USED[group] == 0
        core, x, y, z = self.at = coordinates()
        self.core, self.z = core, z
        self.a = jnp.where(core == 0, y, x)
        self.b = jnp.where(core == 0, x, y)
        self.partner = device(1 - core, x, y, z)
        self.from_p = sum(HALF[:group])
        base = sum(TOTAL[:group])
        self.half = base + core * HALF[group]
        self.first = self.half + self.a * FIRST[group]
        self.second = self.first + self.b * SECOND[group]
        self.other_half = base + (1 - core) * HALF[group]
        self.started = []

    def along(self, stage, s):
        core, x, y, z = self.at
        if stage == "z":
            to = lax.rem(z + s, ZS)
            return to, device(core, x, y, to)
        at = self.a if stage == "first" else self.b
        to = lax.rem(at + s, 4)
        on_y = core == (0 if stage == "first" else 1)
        return to, device(core, jnp.where(on_y, x, to), jnp.where(on_y, to, y), z)

    def copy(self, src, dst, index, peer):
        return pltpu.make_async_remote_copy(
            src_ref=src,
            dst_ref=dst,
            send_sem=self.send.at[self.group * COPIES + index],
            recv_sem=self.recv.at[self.group * COPIES + index],
            device_id=peer,
            device_id_type=MESH,
        )

    def start(self, src, dst, index, peer):
        self.copy(src, dst, index, peer).start()
        self.started.append((src.shape[0], index))

    def chunk(self, at, size):
        return self.g_ref.at[pl.ds(at, size)]

    def takes(self, z, then):
        if Z_USED[self.group] == ZS:
            then()
        else:
            pl.when(z < Z_USED[self.group])(then)

    def stage0(self):
        size = FIRST[self.group]
        for s in (2, 1, 3):
            to, peer = self.along("first", s)
            self.start(self.p_ref.at[pl.ds(self.from_p + to * size, size)], self.got1.at[s - 1], s - 1, peer)

    def stage1(self):
        size, step = FIRST[self.group], 4
        for s in range(3):
            self.copy(self.got1.at[s], self.got1.at[s], s, self.partner).wait_recv()

        def add(t, carry):
            at = pl.ds(t * step, step)
            own = self.p_ref[pl.ds(self.from_p + self.a * size + t * step, step)]
            self.acc2[at] = (own + self.got1[0, at]) + (self.got1[1, at] + self.got1[2, at])
            return carry

        lax.fori_loop(0, size // step, add, 0)
        size = SECOND[self.group]
        for s in (2, 1, 3):
            to, peer = self.along("second", s)
            self.start(self.acc2.at[pl.ds(to * size, size)], self.got2.at[s - 1], 2 + s, peer)

    def across_z(self):
        size = SECOND[self.group]
        self.got3[pl.ds(self.z, 1)] = self.acc3[...][None]
        for s in (4, 3, 5, 2, 6, 1, 7):
            to, peer = self.along("z", s)
            self.start(self.acc3, self.got3.at[self.z], 5 + s, peer)

    def stage2(self):
        size = SECOND[self.group]
        for s in range(3):
            self.copy(self.got2.at[s], self.got2.at[s], 3 + s, self.partner).wait_recv()
        own = self.acc2[pl.ds(self.b * size, size)]
        self.acc3[...] = (own + self.got2[0]) + (self.got2[1] + self.got2[2])
        if self.direct:
            self.across_z()
            return
        size = CHUNK[self.group]
        for s in (4, 3, 5, 2, 6, 1, 7):
            to, peer = self.along("z", s)

            def send():
                self.copy(self.acc3.at[pl.ds(to * size, size)], self.got3.at[s - 1], 5 + s, peer).start()

            self.takes(to, send)

    def stage3(self):
        if self.direct:
            for s in range(1, ZS):
                self.copy(self.acc3, self.got3.at[0], 5 + s, self.partner).wait_recv()
            self.g_ref[pl.ds(self.second, SECOND[self.group])] = tree([self.got3[k] for k in range(ZS)])
            self.back()
            return
        size = CHUNK[self.group]
        own = self.second + self.z * size

        def total():
            for s in range(1, ZS):
                self.copy(self.got3.at[s - 1], self.got3.at[s - 1], 5 + s, self.partner).wait_recv()
            terms = [self.acc3[pl.ds(self.z * size, size)]] + [self.got3[s] for s in range(ZS - 1)]
            self.g_ref[pl.ds(own, size)] = tree(terms)
            for s in (4, 3, 5, 2, 6, 1, 7):
                to, peer = self.along("z", s)
                self.copy(self.chunk(own, size), self.chunk(own, size), 12 + s, peer).start()

        self.takes(self.z, total)

    def stage4(self):
        size = CHUNK[self.group]
        for s in range(1, ZS):
            sender = lax.rem(self.z + ZS - s, ZS)

            def receive():
                got = self.chunk(self.second + sender * size, size)
                self.copy(got, got, 12 + s, self.partner).wait_recv()

            self.takes(sender, receive)
        self.back()

    def back(self):
        mine = self.chunk(self.second, SECOND[self.group])
        for s in (2, 1, 3):
            to, peer = self.along("second", s)
            self.start(mine, mine, 19 + s, peer)

    def stage5(self):
        size = SECOND[self.group]
        for s in range(1, 4):
            got = self.chunk(self.first + lax.rem(self.b + 4 - s, 4) * size, size)
            self.copy(got, got, 19 + s, self.partner).wait_recv()
        mine = self.chunk(self.first, FIRST[self.group])
        for s in (2, 1, 3):
            to, peer = self.along("first", s)
            self.start(mine, mine, 22 + s, peer)
        self.start(mine, mine, 26, self.partner)

    def stage6(self):
        size = FIRST[self.group]
        for s in (1, 3, 2):
            got = self.chunk(self.half + lax.rem(self.a + 4 - s, 4) * size, size)
            self.copy(got, got, 22 + s, self.partner).wait_recv()
            self.start(got, got, 26 + s, self.partner)

    def stage7(self):
        size = FIRST[self.group]
        for s in range(4):
            got = self.chunk(self.other_half + lax.rem(self.b + 4 - s, 4) * size, size)
            self.copy(got, got, 26 + s, self.partner).wait_recv()

    def finish(self):
        for size, index in self.started:
            part = self.chunk(0, size)
            self.copy(part, part, index, self.partner).wait_send()
        if self.direct:
            return
        size = CHUNK[self.group]
        for s in range(1, ZS):
            to, peer = self.along("z", s)

            def sent():
                part = self.acc3.at[pl.ds(to * size, size)]
                self.copy(part, part, 5 + s, peer).wait_send()

            self.takes(to, sent)

            def sent_back():
                part = self.chunk(self.second, size)
                self.copy(part, part, 12 + s, peer).wait_send()

            self.takes(self.z, sent_back)


def orthonormalize_kernel(n, scale, src_ref, out_ref, *scratch):
    (own_ref, other_ref, held_hi, held_lo, p_ref, g_ref, cur_ref, d_ref, z_ref, x_ref, hi_ref, lo_ref, lane_ref, row_ref) = scratch[:14]
    groups_scratch = [scratch[14 + 5 * g : 19 + 5 * g] for g in range(4)]
    (send, recv, x_send, x_recv, in_send, in_recv, pass_send, pass_recv, own_sem) = scratch[34:]
    rows_each, width = src_ref.shape[0], own_ref.shape[1]
    bands = src_ref.shape[1] // width
    per_panel = B // rows_each
    tiles = B // V
    me = lax.axis_index("band")
    core, x, y, z = coordinates()
    partner = device(1 - core, x, y, z)

    barrier = pltpu.get_barrier_semaphore()

    def greet(s, carry):
        pl.semaphore_signal(
            barrier, inc=1, device_id={"band": lax.rem(me + s, bands)}, device_id_type=MESH
        )
        return carry

    others = [device(core, x, y, lax.rem(z + s, ZS)) for s in range(1, ZS)]
    others += [device(core, lax.rem(x + s, XS), y, z) for s in (1, 3)]
    for peer in others:
        pl.semaphore_signal(barrier, inc=1, device_id=peer, device_id_type=MESH)
    lax.fori_loop(1, bands, greet, 0)

    def columns(ref, index):
        return ref.at[:, pl.ds(pl.multiple_of(index * width, width), width)]

    def band(ref, index):
        return ref.at[pl.ds(pl.multiple_of(index * rows_each, rows_each), rows_each), :]

    mine = pltpu.make_async_copy(columns(src_ref, me), band(own_ref, me), own_sem)
    mine.start()
    pl.semaphore_wait(barrier, bands - 1 + len(others))

    def bring(s, source):
        peer = lax.rem(me + s, bands)
        return pltpu.make_async_remote_copy(
            src_ref=columns(src_ref, peer),
            dst_ref=band(own_ref, source),
            send_sem=in_send.at[s],
            recv_sem=in_recv.at[s],
            device_id={"band": peer},
            device_id_type=MESH,
        )

    def hand_over(source):
        return pltpu.make_async_remote_copy(
            src_ref=band(own_ref, source),
            dst_ref=band(other_ref, source),
            send_sem=pass_send.at[source],
            recv_sem=pass_recv.at[source],
            device_id=partner,
            device_id_type=MESH,
        )

    def keep(ref, source, at):
        rows = pl.ds(pl.multiple_of(source * rows_each, rows_each), rows_each)
        high, low = split(ref[rows, :])
        held_hi[rows, at : at + width] = high
        held_lo[rows, at : at + width] = low

    def start(s, carry):
        bring(s, me).start()
        return carry

    def arrive(s, carry):
        source = lax.rem(me - s + bands, bands)
        bring(s, source).wait_recv()
        hand_over(source).start()
        keep(own_ref, source, 0)
        return carry

    def finish(s, carry):
        source = lax.rem(me + 1 - 2 * core - s + bands, bands)
        hand_over(source).wait_recv()
        keep(other_ref, source, width)
        return carry

    def sent(s, carry):
        bring(s, me).wait_send()
        hand_over(lax.rem(me + s, bands)).wait_send()
        return carry

    lax.fori_loop(1, bands, start, 0)
    mine.wait()
    hand_over(me).start()
    keep(own_ref, me, 0)
    lax.fori_loop(1, bands, arrive, 0)
    lax.fori_loop(0, bands, finish, 0)

    groups = grouped_blocks(n)

    def multiply(g):
        half = len(groups[g]) // CORES
        for c in range(CORES):

            @pl.when(core == c)
            def _():
                blocks = groups[g][c * half : (c + 1) * half]
                for i in sorted({i for i, _ in blocks}):
                    wanted = [j for k, j in blocks if k == i]
                    first, end = min(wanted), max(wanted) + 1
                    left = (held_hi[i * B : (i + 1) * B], held_lo[i * B : (i + 1) * B])
                    right = (held_hi[first * B : end * B], held_lo[first * B : end * B])
                    out = dot3(left, right, ((1,), (1,))) * scale
                    for j in wanted:
                        at = sum(HALF[:g]) + blocks.index((i, j)) * tiles
                        block = out[:, (j - first) * B : (j - first + 1) * B]
                        p_ref[at : at + tiles] = block.reshape(tiles, V, B)

    one, two, three, four = (Summing(g, p_ref, g_ref, groups_scratch[g], send, recv) for g in range(4))
    multiply(0)
    one.stage0()
    multiply(1)
    two.stage0()
    multiply(2)
    three.stage0()
    multiply(3)
    four.stage0()
    one.stage1()
    two.stage1()
    one.stage2()
    three.stage1()
    two.stage2()
    four.stage1()
    three.stage2()
    one.stage3()
    four.stage2()
    two.stage3()
    one.stage5()
    three.stage3()
    two.stage5()
    four.stage3()
    one.stage6()
    three.stage5()
    two.stage6()
    one.stage7()
    four.stage5()

    order = [block for group in groups for block in group]
    sub = lax.broadcasted_iota(jnp.int32, (V, B), 0)
    lane = lax.broadcasted_iota(jnp.int32, (V, B), 1)

    def scales(k):
        at = order.index((k, k)) * tiles
        on_diagonal = [jnp.where(lane == q * V + sub, g_ref[at + q], 0.0) for q in range(tiles)]
        diagonal = jnp.sum(tree(on_diagonal), axis=0, keepdims=True)
        lanes = jnp.broadcast_to(lax.rsqrt(diagonal), (V, B))
        lane_ref[...] = lanes
        for q in range(tiles):
            row_ref[q * V : (q + 1) * V, :] = jnp.take_along_axis(lanes, q * V + sub, axis=1)

    def prepare(k):
        if k < 2:
            scales(k)
        lanes = lane_ref[...]
        taken = None
        if k:
            left = (hi_ref[: k * B, k * B : (k + 1) * B], lo_ref[: k * B, k * B : (k + 1) * B])
            right = (hi_ref[: k * B, k * B :], lo_ref[: k * B, k * B :])
            taken = dot3(left, right, ((0,), (0,)))
        for j in range(k, n + width // B):
            if j < n:
                at = order.index((k, j)) * tiles
                block = g_ref[at : at + tiles].reshape(B, B)
            else:
                block = own_ref[k * B : (k + 1) * B, (j - n) * B : (j - n + 1) * B]
            if k:
                block = block - taken[:, (j - k) * B : (j - k + 1) * B]
            if j > k:
                cur_ref[:, j * B : (j + 1) * B] = block
                continue
            for q in range(tiles):
                at = slice(q * V, (q + 1) * V)
                d_ref[at, :] = block[at] * row_ref[at, :] * lanes

    def remote(peer, sender):
        return pltpu.make_async_remote_copy(
            src_ref=x_ref.at[pl.ds(peer * rows_each, rows_each), :],
            dst_ref=columns(out_ref, sender),
            send_sem=x_send.at[peer],
            recv_sem=x_recv.at[sender],
            device_id={"band": peer},
            device_id_type=MESH,
        )

    stays = pltpu.make_async_copy(band(x_ref, me), columns(out_ref, me), own_sem)

    def step(i, carry):
        for k in range(n):

            @pl.when(i == k)
            def _():
                if k == 1:
                    two.stage7()
                if k == 2:
                    three.stage7()
                if k == 3:
                    four.stage7()
                prepare(k)

        rows = [d_ref[q * V : (q + 1) * V, :] for q in range(tiles)]
        lanes = lane_ref[...]
        for q, inverse in enumerate(factor_inverse(rows)):
            z_ref[q * V : (q + 1) * V, :] = inverse * lanes
        for k in range(n):

            @pl.when(i == k)
            def _():
                if k == 0:
                    three.stage6()
                if k == 1:
                    four.stage6()
                panel = dot3(split(z_ref[...]), split(cur_ref[:, (k + 1) * B :]), ((1,), (0,)))
                x_ref[k * B : (k + 1) * B, :] = panel[:, panel.shape[1] - width :]
                for peer in range(k * per_panel, (k + 1) * per_panel):

                    @pl.when(peer != me)
                    def _():
                        remote(peer, me).start()

                    @pl.when(peer == me)
                    def _():
                        stays.start()

                if 0 < k < n - 1:
                    scales(k + 1)
                if k < n - 1:
                    high, low = split(panel)
                    hi_ref[k * B : (k + 1) * B, (k + 1) * B :] = high
                    lo_ref[k * B : (k + 1) * B, (k + 1) * B :] = low

        return carry

    lax.fori_loop(0, n, step, 0)
    lax.fori_loop(1, bands, sent, 0)
    hand_over(me).wait_send()
    for group in (one, two, three, four):
        group.finish()
    stays.wait()
    for other in range(bands):

        @pl.when(other != me)
        def _():
            remote(other, me).wait_send()
            remote(other, other).wait_recv()


def orthonormalize(coeffs, bands, columns_all):
    rows_each, columns = coeffs.shape
    rows, width = rows_each * bands, columns // bands
    n = rows // B
    tiles = lambda *shape: pltpu.VMEM((*shape, V, B), jnp.float32)
    whole = n * B + width
    summing = []
    for g in range(4):
        summing += [tiles(FIRST[g]), tiles(SECOND[g]), tiles(3, FIRST[g]), tiles(3, SECOND[g])]
        summing += [tiles(ZS - 1, CHUNK[g]) if Z_USED[g] else tiles(ZS, SECOND[g])]
    return pl.pallas_call(
        functools.partial(orthonormalize_kernel, n, 1.0 / columns_all),
        out_shape=jax.ShapeDtypeStruct(coeffs.shape, jnp.float32),
        in_specs=[pl.BlockSpec(memory_space=pltpu.HBM)],
        out_specs=pl.BlockSpec(memory_space=pltpu.VMEM),
        scratch_shapes=[
            pltpu.VMEM((rows, width), jnp.float32),
            pltpu.VMEM((rows, width), jnp.float32),
            pltpu.VMEM((rows, CORES * width), jnp.bfloat16),
            pltpu.VMEM((rows, CORES * width), jnp.bfloat16),
            tiles(sum(HALF)),
            tiles(sum(TOTAL)),
            pltpu.VMEM((B, whole), jnp.float32),
            pltpu.VMEM((B, B), jnp.float32),
            pltpu.VMEM((B, B), jnp.float32),
            pltpu.VMEM((rows, width), jnp.float32),
            pltpu.VMEM((rows, whole), jnp.bfloat16),
            pltpu.VMEM((rows, whole), jnp.bfloat16),
            pltpu.VMEM((V, B), jnp.float32),
            pltpu.VMEM((B, B), jnp.float32),
            *summing,
            pltpu.SemaphoreType.DMA((4 * COPIES,)),
            pltpu.SemaphoreType.DMA((4 * COPIES,)),
            *[pltpu.SemaphoreType.DMA((bands,))] * 6,
            pltpu.SemaphoreType.DMA,
        ],
        compiler_params=pltpu.CompilerParams(
            collective_id=0, has_side_effects=True, vmem_limit_bytes=52 << 20
        ),
        name="orthonormalize",
    )(coeffs)


def local(coeffs):
    bands = lax.axis_size("band")
    return orthonormalize(coeffs, bands, coeffs.shape[1] * lax.axis_size("ga"))


def solution(mesh):
    return jax.shard_map(
        local,
        mesh=mesh,
        in_specs=(P("band", "ga"),),
        out_specs=P("band", "ga"),
        check_vma=False,
    )
```

```python
import functools

import jax
import jax.numpy as jnp
from jax import lax
from jax.experimental import pallas as pl
from jax.experimental.pallas import tpu as pltpu
from jax.sharding import PartitionSpec as P

MESH = pl.DeviceIdType.MESH

B = 128
V = 8


def split(x):
    hi = x.astype(jnp.bfloat16)
    return hi, (x - hi.astype(jnp.float32)).astype(jnp.bfloat16)


def dot3(a, b, dims):
    (ca,), (cb,) = dims
    ah, al = a
    bh, bl = b
    left = jnp.concatenate([ah, al, ah], axis=ca)
    right = jnp.concatenate([bh, bh, bl], axis=cb)
    return lax.dot_general(left, right, (dims, ((), ())), preferred_element_type=jnp.float32)


def lane_col(t, c):
    return jnp.take_along_axis(t, jnp.full((V, B), c, jnp.int32), axis=1)


def sub_row(t, k):
    return jnp.broadcast_to(t[k : k + 1, :], (V, B))


def tree(m):
    while len(m) > 1:
        m = [m[e] + m[e + 1] if e + 1 < len(m) else m[e] for e in range(0, len(m), 2)]
    return m[0]


def factor_inverse(rows):
    n = len(rows)
    rows = list(rows)
    sub = lax.broadcasted_iota(jnp.int32, (V, B), 0)
    lane = lax.broadcasted_iota(jnp.int32, (V, B), 1)
    out = []
    cols = [lane_col(rows[0], k) for k in range(V)]
    for p in range(n):
        c0 = p * V
        last = p == n - 1
        in_block = (lane >= c0) & (lane < c0 + V)
        t = jnp.where(in_block, jnp.where(lane - c0 == sub, 1.0, 0.0), rows[p])
        f = jnp.where(lane < c0 + V, t, 0.0)
        pivots = None
        below_m = {q: [lane_col(rows[q], c0 + k) for k in range(V)] for q in range(p + 1, n)}
        if not last:
            a = list(below_m[p + 1])
            ahead = [lane_col(rows[p + 1], c0 + V + k) for k in range(V)]
        for k in range(0, V, 2):
            h1, h2 = sub == k, sub == k + 1
            here = h1 | h2
            d11, d12, d22 = sub_row(cols[k], k), sub_row(cols[k + 1], k), sub_row(cols[k + 1], k + 1)
            det = d11 * d22 - d12 * d12
            r = 1.0 / det
            m1, m2 = jnp.where(here, 0.0, cols[k]), jnp.where(here, 0.0, cols[k + 1])

            def solve(col):
                v1, v2 = sub_row(col, k), sub_row(col, k + 1)
                return (d22 * v1 - d12 * v2) * r, (d11 * v2 - d12 * v1) * r

            def eliminate(col):
                u1, u2 = solve(col)
                return jnp.where(h1, u1, jnp.where(h2, u2, col - (m1 * u1 + m2 * u2))), u1, u2

            for j in range(k + 2, V):
                cols[j], u1, u2 = eliminate(cols[j])
                if not last:
                    a[j] = a[j] - (a[k] * u1 + a[k + 1] * u2)
            if not last:
                s1 = (d22 * a[k] - d12 * a[k + 1]) * r
                s2 = (d11 * a[k + 1] - d12 * a[k]) * r
                for j in range(V):
                    ahead[j] = ahead[j] - (s1 * sub_row(a[k], j) + s2 * sub_row(a[k + 1], j))
            q = 1.0 / d11
            ratio = d12 * q
            f1 = sub_row(f, k)
            f2 = sub_row(f, k + 1) - ratio * f1
            g2 = d11 * r
            g1 = q
            below = sub > k + 1
            b1 = jnp.where(below, cols[k], 0.0)
            b2 = jnp.where(below, cols[k + 1], 0.0)
            l2 = b2 - b1 * ratio
            f = jnp.where(h2, f2, f - b1 * (f1 * g1) - l2 * (f2 * g2))
            t, _, _ = eliminate(t)
            scale = jnp.where(h1, g1, g2)
            pivots = scale if pivots is None else jnp.where(here, scale, pivots)
        out.append(f * jnp.sqrt(pivots))
        if last:
            break
        cols = ahead
        w = [sub_row(t, k) for k in range(V)]
        for q in range(p + 1, n):
            acc = jnp.where(in_block, 0.0, rows[q])
            rows[q] = acc - tree([below_m[q][k] * w[k] for k in range(V)])
    return out


CORES, YS, XS, ZS = 2, 4, 4, 8
TOTAL = (128, 224, 224)
HALF = tuple(t // 2 for t in TOTAL)
FIRST = tuple(t // 8 for t in TOTAL)
SECOND = tuple(t // 32 for t in TOTAL)
Z_USED = (0, 0, 0)
CHUNK = tuple(t // max(z, 1) for t, z in zip(SECOND, Z_USED))
COPIES = 30


def grouped_blocks(n):
    first = [(0, j) for j in range(n)]
    second = [(i, j) for i in (1, 2) for j in range(i, n)] + [(3, 3)]
    rest = [(i, j) for i in range(3, n) for j in range(i, n) if (i, j) != (3, 3)]
    return first, second, rest


def coordinates():
    band, ga = lax.axis_index("band"), lax.axis_index("ga")
    core, y = lax.rem(band, CORES), lax.rem(band // CORES, YS)
    x = (band // (CORES * YS)) * 2 + lax.rem(ga, 2)
    return core, x, y, ga // 2


def device(core, x, y, z):
    return {"band": ((x // 2) * YS + y) * CORES + core, "ga": z * 2 + lax.rem(x, 2)}


class Summing:
    def __init__(self, group, p_ref, g_ref, scratch, send, recv):
        self.group, self.p_ref, self.g_ref = group, p_ref, g_ref
        self.acc2, self.acc3, self.got1, self.got2, self.got3 = scratch
        self.send, self.recv = send, recv
        self.direct = Z_USED[group] == 0
        core, x, y, z = self.at = coordinates()
        self.core, self.z = core, z
        self.a = jnp.where(core == 0, y, x)
        self.b = jnp.where(core == 0, x, y)
        self.partner = device(1 - core, x, y, z)
        self.from_p = sum(HALF[:group])
        base = sum(TOTAL[:group])
        self.half = base + core * HALF[group]
        self.first = self.half + self.a * FIRST[group]
        self.second = self.first + self.b * SECOND[group]
        self.other_half = base + (1 - core) * HALF[group]
        self.started = []

    def along(self, stage, s):
        core, x, y, z = self.at
        if stage == "z":
            to = lax.rem(z + s, ZS)
            return to, device(core, x, y, to)
        at = self.a if stage == "first" else self.b
        to = lax.rem(at + s, 4)
        on_y = core == (0 if stage == "first" else 1)
        return to, device(core, jnp.where(on_y, x, to), jnp.where(on_y, to, y), z)

    def copy(self, src, dst, index, peer):
        return pltpu.make_async_remote_copy(
            src_ref=src,
            dst_ref=dst,
            send_sem=self.send.at[self.group * COPIES + index],
            recv_sem=self.recv.at[self.group * COPIES + index],
            device_id=peer,
            device_id_type=MESH,
        )

    def start(self, src, dst, index, peer):
        self.copy(src, dst, index, peer).start()
        self.started.append((src.shape[0], index))

    def chunk(self, at, size):
        return self.g_ref.at[pl.ds(at, size)]

    def takes(self, z, then):
        if Z_USED[self.group] == ZS:
            then()
        else:
            pl.when(z < Z_USED[self.group])(then)

    def stage0(self):
        size = FIRST[self.group]
        for s in (2, 1, 3):
            to, peer = self.along("first", s)
            self.start(self.p_ref.at[pl.ds(self.from_p + to * size, size)], self.got1.at[s - 1], s - 1, peer)

    def stage1(self):
        size, step = FIRST[self.group], 4
        for s in range(3):
            self.copy(self.got1.at[s], self.got1.at[s], s, self.partner).wait_recv()

        def add(t, carry):
            at = pl.ds(t * step, step)
            own = self.p_ref[pl.ds(self.from_p + self.a * size + t * step, step)]
            self.acc2[at] = (own + self.got1[0, at]) + (self.got1[1, at] + self.got1[2, at])
            return carry

        lax.fori_loop(0, size // step, add, 0)
        size = SECOND[self.group]
        for s in (2, 1, 3):
            to, peer = self.along("second", s)
            self.start(self.acc2.at[pl.ds(to * size, size)], self.got2.at[s - 1], 2 + s, peer)

    def across_z(self):
        size = SECOND[self.group]
        self.got3[pl.ds(self.z, 1)] = self.acc3[...][None]
        for s in (4, 3, 5, 2, 6, 1, 7):
            to, peer = self.along("z", s)
            self.start(self.acc3, self.got3.at[self.z], 5 + s, peer)

    def stage2(self):
        size = SECOND[self.group]
        for s in range(3):
            self.copy(self.got2.at[s], self.got2.at[s], 3 + s, self.partner).wait_recv()
        own = self.acc2[pl.ds(self.b * size, size)]
        self.acc3[...] = (own + self.got2[0]) + (self.got2[1] + self.got2[2])
        if self.direct:
            self.across_z()
            return
        size = CHUNK[self.group]
        for s in (4, 3, 5, 2, 6, 1, 7):
            to, peer = self.along("z", s)

            def send():
                self.copy(self.acc3.at[pl.ds(to * size, size)], self.got3.at[s - 1], 5 + s, peer).start()

            self.takes(to, send)

    def stage3(self):
        if self.direct:
            for s in range(1, ZS):
                self.copy(self.acc3, self.got3.at[0], 5 + s, self.partner).wait_recv()
            self.g_ref[pl.ds(self.second, SECOND[self.group])] = tree([self.got3[k] for k in range(ZS)])
            self.back()
            return
        size = CHUNK[self.group]
        own = self.second + self.z * size

        def total():
            for s in range(1, ZS):
                self.copy(self.got3.at[s - 1], self.got3.at[s - 1], 5 + s, self.partner).wait_recv()
            terms = [self.acc3[pl.ds(self.z * size, size)]] + [self.got3[s] for s in range(ZS - 1)]
            self.g_ref[pl.ds(own, size)] = tree(terms)
            for s in (4, 3, 5, 2, 6, 1, 7):
                to, peer = self.along("z", s)
                self.copy(self.chunk(own, size), self.chunk(own, size), 12 + s, peer).start()

        self.takes(self.z, total)

    def stage4(self):
        size = CHUNK[self.group]
        for s in range(1, ZS):
            sender = lax.rem(self.z + ZS - s, ZS)

            def receive():
                got = self.chunk(self.second + sender * size, size)
                self.copy(got, got, 12 + s, self.partner).wait_recv()

            self.takes(sender, receive)
        self.back()

    def back(self):
        mine = self.chunk(self.second, SECOND[self.group])
        for s in (2, 1, 3):
            to, peer = self.along("second", s)
            self.start(mine, mine, 19 + s, peer)

    def stage5(self):
        size = SECOND[self.group]
        for s in range(1, 4):
            got = self.chunk(self.first + lax.rem(self.b + 4 - s, 4) * size, size)
            self.copy(got, got, 19 + s, self.partner).wait_recv()
        mine = self.chunk(self.first, FIRST[self.group])
        for s in (2, 1, 3):
            to, peer = self.along("first", s)
            self.start(mine, mine, 22 + s, peer)
        self.start(mine, mine, 26, self.partner)

    def stage6(self):
        size = FIRST[self.group]
        for s in (1, 3, 2):
            got = self.chunk(self.half + lax.rem(self.a + 4 - s, 4) * size, size)
            self.copy(got, got, 22 + s, self.partner).wait_recv()
            self.start(got, got, 26 + s, self.partner)

    def stage7(self):
        size = FIRST[self.group]
        for s in range(4):
            got = self.chunk(self.other_half + lax.rem(self.b + 4 - s, 4) * size, size)
            self.copy(got, got, 26 + s, self.partner).wait_recv()

    def finish(self):
        for size, index in self.started:
            part = self.chunk(0, size)
            self.copy(part, part, index, self.partner).wait_send()
        if self.direct:
            return
        size = CHUNK[self.group]
        for s in range(1, ZS):
            to, peer = self.along("z", s)

            def sent():
                part = self.acc3.at[pl.ds(to * size, size)]
                self.copy(part, part, 5 + s, peer).wait_send()

            self.takes(to, sent)

            def sent_back():
                part = self.chunk(self.second, size)
                self.copy(part, part, 12 + s, peer).wait_send()

            self.takes(self.z, sent_back)


def orthonormalize_kernel(n, scale, src_ref, out_ref, *scratch):
    (own_ref, other_ref, held_hi, held_lo, p_ref, g_ref, cur_ref, d_ref, z_ref, x_ref, hi_ref, lo_ref, lane_ref) = scratch[:13]
    groups_scratch = [scratch[13 + 5 * g : 18 + 5 * g] for g in range(3)]
    (send, recv, x_send, x_recv, in_send, in_recv, pass_send, pass_recv, own_sem) = scratch[28:]
    rows_each, width = src_ref.shape[0], own_ref.shape[1]
    bands = src_ref.shape[1] // width
    per_panel = B // rows_each
    tiles = B // V
    me = lax.axis_index("band")
    core, x, y, z = coordinates()
    partner = device(1 - core, x, y, z)

    barrier = pltpu.get_barrier_semaphore()

    def greet(s, carry):
        pl.semaphore_signal(
            barrier, inc=1, device_id={"band": lax.rem(me + s, bands)}, device_id_type=MESH
        )
        return carry

    others = [device(core, x, y, lax.rem(z + s, ZS)) for s in range(1, ZS)]
    others += [device(core, lax.rem(x + s, XS), y, z) for s in (1, 3)]
    for peer in others:
        pl.semaphore_signal(barrier, inc=1, device_id=peer, device_id_type=MESH)
    lax.fori_loop(1, bands, greet, 0)

    def columns(ref, index):
        return ref.at[:, pl.ds(pl.multiple_of(index * width, width), width)]

    def band(ref, index):
        return ref.at[pl.ds(pl.multiple_of(index * rows_each, rows_each), rows_each), :]

    mine = pltpu.make_async_copy(columns(src_ref, me), band(own_ref, me), own_sem)
    mine.start()
    pl.semaphore_wait(barrier, bands - 1 + len(others))

    def bring(s, source):
        peer = lax.rem(me + s, bands)
        return pltpu.make_async_remote_copy(
            src_ref=columns(src_ref, peer),
            dst_ref=band(own_ref, source),
            send_sem=in_send.at[s],
            recv_sem=in_recv.at[s],
            device_id={"band": peer},
            device_id_type=MESH,
        )

    def hand_over(source):
        return pltpu.make_async_remote_copy(
            src_ref=band(own_ref, source),
            dst_ref=band(other_ref, source),
            send_sem=pass_send.at[source],
            recv_sem=pass_recv.at[source],
            device_id=partner,
            device_id_type=MESH,
        )

    def keep(ref, source, at):
        rows = pl.ds(pl.multiple_of(source * rows_each, rows_each), rows_each)
        high, low = split(ref[rows, :])
        held_hi[rows, at : at + width] = high
        held_lo[rows, at : at + width] = low

    def start(s, carry):
        bring(s, me).start()
        return carry

    def arrive(s, carry):
        source = lax.rem(me - s + bands, bands)
        bring(s, source).wait_recv()
        hand_over(source).start()
        keep(own_ref, source, 0)
        return carry

    def finish(s, carry):
        source = lax.rem(me + 1 - 2 * core - s + bands, bands)
        hand_over(source).wait_recv()
        keep(other_ref, source, width)
        return carry

    def sent(s, carry):
        bring(s, me).wait_send()
        hand_over(lax.rem(me + s, bands)).wait_send()
        return carry

    lax.fori_loop(1, bands, start, 0)
    mine.wait()
    hand_over(me).start()
    keep(own_ref, me, 0)
    lax.fori_loop(1, bands, arrive, 0)
    lax.fori_loop(0, bands, finish, 0)

    groups = grouped_blocks(n)

    def multiply(g):
        half = len(groups[g]) // CORES
        for c in range(CORES):

            @pl.when(core == c)
            def _():
                blocks = groups[g][c * half : (c + 1) * half]
                for i in sorted({i for i, _ in blocks}):
                    wanted = [j for k, j in blocks if k == i]
                    first, end = min(wanted), max(wanted) + 1
                    left = (held_hi[i * B : (i + 1) * B], held_lo[i * B : (i + 1) * B])
                    right = (held_hi[first * B : end * B], held_lo[first * B : end * B])
                    out = dot3(left, right, ((1,), (1,))) * scale
                    for j in wanted:
                        at = sum(HALF[:g]) + blocks.index((i, j)) * tiles
                        block = out[:, (j - first) * B : (j - first + 1) * B]
                        p_ref[at : at + tiles] = block.reshape(tiles, V, B)

    one, two, three = (Summing(g, p_ref, g_ref, groups_scratch[g], send, recv) for g in range(3))
    multiply(0)
    one.stage0()
    multiply(1)
    two.stage0()
    multiply(2)
    three.stage0()
    one.stage1()
    two.stage1()
    one.stage2()
    three.stage1()
    two.stage2()
    one.stage3()
    three.stage2()
    two.stage3()
    one.stage5()
    three.stage3()
    two.stage5()
    one.stage6()
    three.stage5()
    two.stage6()
    one.stage7()

    order = [block for group in groups for block in group]
    sub = lax.broadcasted_iota(jnp.int32, (V, B), 0)
    lane = lax.broadcasted_iota(jnp.int32, (V, B), 1)

    def prepare(k):
        at = order.index((k, k)) * tiles
        on_diagonal = [jnp.where(lane == q * V + sub, g_ref[at + q], 0.0) for q in range(tiles)]
        diagonal = jnp.sum(tree(on_diagonal), axis=0, keepdims=True)
        lanes = jnp.broadcast_to(lax.rsqrt(diagonal), (V, B))
        lane_ref[...] = lanes
        taken = None
        if k:
            left = (hi_ref[: k * B, k * B : (k + 1) * B], lo_ref[: k * B, k * B : (k + 1) * B])
            right = (hi_ref[: k * B, k * B :], lo_ref[: k * B, k * B :])
            taken = dot3(left, right, ((0,), (0,)))
        for j in range(k, n + width // B):
            if j < n:
                at = order.index((k, j)) * tiles
                block = g_ref[at : at + tiles].reshape(B, B)
            else:
                block = own_ref[k * B : (k + 1) * B, (j - n) * B : (j - n + 1) * B]
            if k:
                block = block - taken[:, (j - k) * B : (j - k + 1) * B]
            if j > k:
                cur_ref[:, j * B : (j + 1) * B] = block
                continue
            for q in range(tiles):
                rows = jnp.take_along_axis(lanes, q * V + sub, axis=1)
                d_ref[q * V : (q + 1) * V, :] = block[q * V : (q + 1) * V] * rows * lanes

    def remote(peer, sender):
        return pltpu.make_async_remote_copy(
            src_ref=x_ref.at[pl.ds(peer * rows_each, rows_each), :],
            dst_ref=columns(out_ref, sender),
            send_sem=x_send.at[peer],
            recv_sem=x_recv.at[sender],
            device_id={"band": peer},
            device_id_type=MESH,
        )

    stays = pltpu.make_async_copy(band(x_ref, me), columns(out_ref, me), own_sem)

    def step(i, carry):
        for k in range(n):

            @pl.when(i == k)
            def _():
                if k == 1:
                    two.stage7()
                if k == 3:
                    three.stage7()
                prepare(k)

        rows = [d_ref[q * V : (q + 1) * V, :] for q in range(tiles)]
        lanes = lane_ref[...]
        for q, inverse in enumerate(factor_inverse(rows)):
            z_ref[q * V : (q + 1) * V, :] = inverse * lanes
        for k in range(n):

            @pl.when(i == k)
            def _():
                if k == 0:
                    three.stage6()
                panel = dot3(split(z_ref[...]), split(cur_ref[:, (k + 1) * B :]), ((1,), (0,)))
                x_ref[k * B : (k + 1) * B, :] = panel[:, panel.shape[1] - width :]
                for peer in range(k * per_panel, (k + 1) * per_panel):

                    @pl.when(peer != me)
                    def _():
                        remote(peer, me).start()

                    @pl.when(peer == me)
                    def _():
                        stays.start()

                if k < n - 1:
                    high, low = split(panel)
                    hi_ref[k * B : (k + 1) * B, (k + 1) * B :] = high
                    lo_ref[k * B : (k + 1) * B, (k + 1) * B :] = low

        return carry

    lax.fori_loop(0, n, step, 0)
    lax.fori_loop(1, bands, sent, 0)
    hand_over(me).wait_send()
    for group in (one, two, three):
        group.finish()
    stays.wait()
    for other in range(bands):

        @pl.when(other != me)
        def _():
            remote(other, me).wait_send()
            remote(other, other).wait_recv()


def orthonormalize(coeffs, bands, columns_all):
    rows_each, columns = coeffs.shape
    rows, width = rows_each * bands, columns // bands
    n = rows // B
    tiles = lambda *shape: pltpu.VMEM((*shape, V, B), jnp.float32)
    whole = n * B + width
    summing = []
    for g in range(3):
        summing += [tiles(FIRST[g]), tiles(SECOND[g]), tiles(3, FIRST[g]), tiles(3, SECOND[g])]
        summing += [tiles(ZS - 1, CHUNK[g]) if Z_USED[g] else tiles(ZS, SECOND[g])]
    return pl.pallas_call(
        functools.partial(orthonormalize_kernel, n, 1.0 / columns_all),
        out_shape=jax.ShapeDtypeStruct(coeffs.shape, jnp.float32),
        in_specs=[pl.BlockSpec(memory_space=pltpu.HBM)],
        out_specs=pl.BlockSpec(memory_space=pltpu.VMEM),
        scratch_shapes=[
            pltpu.VMEM((rows, width), jnp.float32),
            pltpu.VMEM((rows, width), jnp.float32),
            pltpu.VMEM((rows, CORES * width), jnp.bfloat16),
            pltpu.VMEM((rows, CORES * width), jnp.bfloat16),
            tiles(sum(HALF)),
            tiles(sum(TOTAL)),
            pltpu.VMEM((B, whole), jnp.float32),
            pltpu.VMEM((B, B), jnp.float32),
            pltpu.VMEM((B, B), jnp.float32),
            pltpu.VMEM((rows, width), jnp.float32),
            pltpu.VMEM((rows, whole), jnp.bfloat16),
            pltpu.VMEM((rows, whole), jnp.bfloat16),
            pltpu.VMEM((V, B), jnp.float32),
            *summing,
            pltpu.SemaphoreType.DMA((3 * COPIES,)),
            pltpu.SemaphoreType.DMA((3 * COPIES,)),
            *[pltpu.SemaphoreType.DMA((bands,))] * 6,
            pltpu.SemaphoreType.DMA,
        ],
        compiler_params=pltpu.CompilerParams(
            collective_id=0, has_side_effects=True, vmem_limit_bytes=52 << 20
        ),
        name="orthonormalize",
    )(coeffs)


def local(coeffs):
    bands = lax.axis_size("band")
    return orthonormalize(coeffs, bands, coeffs.shape[1] * lax.axis_size("ga"))


def solution(mesh):
    return jax.shard_map(
        local,
        mesh=mesh,
        in_specs=(P("band", "ga"),),
        out_specs=P("band", "ga"),
        check_vma=False,
    )
```

```python
import functools

import jax
import jax.numpy as jnp
from jax import lax
from jax.experimental import pallas as pl
from jax.experimental.pallas import tpu as pltpu
from jax.sharding import PartitionSpec as P

MESH = pl.DeviceIdType.MESH

B = 128
V = 8


def split(x):
    hi = x.astype(jnp.bfloat16)
    return hi, (x - hi.astype(jnp.float32)).astype(jnp.bfloat16)


def dot3(a, b, dims):
    (ca,), (cb,) = dims
    ah, al = a
    bh, bl = b
    left = jnp.concatenate([ah, al, ah], axis=ca)
    right = jnp.concatenate([bh, bh, bl], axis=cb)
    return lax.dot_general(left, right, (dims, ((), ())), preferred_element_type=jnp.float32)


def lane_col(t, c):
    return jnp.take_along_axis(t, jnp.full((V, B), c, jnp.int32), axis=1)


def sub_row(t, k):
    return jnp.broadcast_to(t[k : k + 1, :], (V, B))


def tree(m):
    while len(m) > 1:
        m = [m[e] + m[e + 1] if e + 1 < len(m) else m[e] for e in range(0, len(m), 2)]
    return m[0]


def factor_inverse(rows):
    n = len(rows)
    rows = list(rows)
    sub = lax.broadcasted_iota(jnp.int32, (V, B), 0)
    lane = lax.broadcasted_iota(jnp.int32, (V, B), 1)
    out = []
    cols = [lane_col(rows[0], k) for k in range(V)]
    for p in range(n):
        c0 = p * V
        last = p == n - 1
        in_block = (lane >= c0) & (lane < c0 + V)
        t = jnp.where(in_block, jnp.where(lane - c0 == sub, 1.0, 0.0), rows[p])
        f = jnp.where(lane < c0 + V, t, 0.0)
        pivots = None
        below_m = {q: [lane_col(rows[q], c0 + k) for k in range(V)] for q in range(p + 1, n)}
        if not last:
            a = list(below_m[p + 1])
            ahead = [lane_col(rows[p + 1], c0 + V + k) for k in range(V)]
        for k in range(0, V, 2):
            h1, h2 = sub == k, sub == k + 1
            here = h1 | h2
            d11, d12, d22 = sub_row(cols[k], k), sub_row(cols[k + 1], k), sub_row(cols[k + 1], k + 1)
            det = d11 * d22 - d12 * d12
            r = 1.0 / det
            m1, m2 = jnp.where(here, 0.0, cols[k]), jnp.where(here, 0.0, cols[k + 1])

            def solve(col):
                v1, v2 = sub_row(col, k), sub_row(col, k + 1)
                return (d22 * v1 - d12 * v2) * r, (d11 * v2 - d12 * v1) * r

            def eliminate(col):
                u1, u2 = solve(col)
                return jnp.where(h1, u1, jnp.where(h2, u2, col - (m1 * u1 + m2 * u2))), u1, u2

            for j in range(k + 2, V):
                cols[j], u1, u2 = eliminate(cols[j])
                if not last:
                    a[j] = a[j] - (a[k] * u1 + a[k + 1] * u2)
            if not last:
                s1 = (d22 * a[k] - d12 * a[k + 1]) * r
                s2 = (d11 * a[k + 1] - d12 * a[k]) * r
                for j in range(V):
                    ahead[j] = ahead[j] - (s1 * sub_row(a[k], j) + s2 * sub_row(a[k + 1], j))
            q = 1.0 / d11
            ratio = d12 * q
            f1 = sub_row(f, k)
            f2 = sub_row(f, k + 1) - ratio * f1
            g2 = d11 * r
            g1 = q
            below = sub > k + 1
            b1 = jnp.where(below, cols[k], 0.0)
            b2 = jnp.where(below, cols[k + 1], 0.0)
            l2 = b2 - b1 * ratio
            f = jnp.where(h2, f2, f - b1 * (f1 * g1) - l2 * (f2 * g2))
            t, _, _ = eliminate(t)
            scale = jnp.where(h1, g1, g2)
            pivots = scale if pivots is None else jnp.where(here, scale, pivots)
        out.append(f * jnp.sqrt(pivots))
        if last:
            break
        cols = ahead
        w = [sub_row(t, k) for k in range(V)]
        for q in range(p + 1, n):
            acc = jnp.where(in_block, 0.0, rows[q])
            rows[q] = acc - tree([below_m[q][k] * w[k] for k in range(V)])
    return out


CORES, YS, XS, ZS = 2, 4, 4, 8
TOTAL = (128, 128, 160, 160)
HALF = tuple(t // 2 for t in TOTAL)
FIRST = tuple(t // 8 for t in TOTAL)
SECOND = tuple(t // 32 for t in TOTAL)
Z_USED = (0, 0, 0, 0)
CHUNK = tuple(t // max(z, 1) for t, z in zip(SECOND, Z_USED))
COPIES = 30


def grouped_blocks(n):
    first = [(0, j) for j in range(n)]
    second = [(1, j) for j in range(1, n)] + [(2, 2)]
    third = [(i, j) for i in (2, 3) for j in range(3, n)]
    rest = [(i, j) for i in range(4, n) for j in range(i, n)]
    return first, second, third, rest


def coordinates():
    band, ga = lax.axis_index("band"), lax.axis_index("ga")
    core, y = lax.rem(band, CORES), lax.rem(band // CORES, YS)
    x = (band // (CORES * YS)) * 2 + lax.rem(ga, 2)
    return core, x, y, ga // 2


def device(core, x, y, z):
    return {"band": ((x // 2) * YS + y) * CORES + core, "ga": z * 2 + lax.rem(x, 2)}


class Summing:
    def __init__(self, group, p_ref, g_ref, scratch, send, recv):
        self.group, self.p_ref, self.g_ref = group, p_ref, g_ref
        self.acc2, self.acc3, self.got1, self.got2, self.got3 = scratch
        self.send, self.recv = send, recv
        self.direct = Z_USED[group] == 0
        core, x, y, z = self.at = coordinates()
        self.core, self.z = core, z
        self.a = jnp.where(core == 0, y, x)
        self.b = jnp.where(core == 0, x, y)
        self.partner = device(1 - core, x, y, z)
        self.from_p = sum(HALF[:group])
        base = sum(TOTAL[:group])
        self.half = base + core * HALF[group]
        self.first = self.half + self.a * FIRST[group]
        self.second = self.first + self.b * SECOND[group]
        self.other_half = base + (1 - core) * HALF[group]
        self.started = []

    def along(self, stage, s):
        core, x, y, z = self.at
        if stage == "z":
            to = lax.rem(z + s, ZS)
            return to, device(core, x, y, to)
        at = self.a if stage == "first" else self.b
        to = lax.rem(at + s, 4)
        on_y = core == (0 if stage == "first" else 1)
        return to, device(core, jnp.where(on_y, x, to), jnp.where(on_y, to, y), z)

    def copy(self, src, dst, index, peer):
        return pltpu.make_async_remote_copy(
            src_ref=src,
            dst_ref=dst,
            send_sem=self.send.at[self.group * COPIES + index],
            recv_sem=self.recv.at[self.group * COPIES + index],
            device_id=peer,
            device_id_type=MESH,
        )

    def start(self, src, dst, index, peer):
        self.copy(src, dst, index, peer).start()
        self.started.append((src.shape[0], index))

    def chunk(self, at, size):
        return self.g_ref.at[pl.ds(at, size)]

    def takes(self, z, then):
        if Z_USED[self.group] == ZS:
            then()
        else:
            pl.when(z < Z_USED[self.group])(then)

    def stage0(self):
        size = FIRST[self.group]
        for s in (2, 1, 3):
            to, peer = self.along("first", s)
            self.start(self.p_ref.at[pl.ds(self.from_p + to * size, size)], self.got1.at[s - 1], s - 1, peer)

    def stage1(self):
        size, step = FIRST[self.group], 4
        for s in range(3):
            self.copy(self.got1.at[s], self.got1.at[s], s, self.partner).wait_recv()

        def add(t, carry):
            at = pl.ds(t * step, step)
            own = self.p_ref[pl.ds(self.from_p + self.a * size + t * step, step)]
            self.acc2[at] = (own + self.got1[0, at]) + (self.got1[1, at] + self.got1[2, at])
            return carry

        lax.fori_loop(0, size // step, add, 0)
        size = SECOND[self.group]
        for s in (2, 1, 3):
            to, peer = self.along("second", s)
            self.start(self.acc2.at[pl.ds(to * size, size)], self.got2.at[s - 1], 2 + s, peer)

    def across_z(self):
        size = SECOND[self.group]
        self.got3[pl.ds(self.z, 1)] = self.acc3[...][None]
        for s in (4, 3, 5, 2, 6, 1, 7):
            to, peer = self.along("z", s)
            self.start(self.acc3, self.got3.at[self.z], 5 + s, peer)

    def stage2(self):
        size = SECOND[self.group]
        for s in range(3):
            self.copy(self.got2.at[s], self.got2.at[s], 3 + s, self.partner).wait_recv()
        own = self.acc2[pl.ds(self.b * size, size)]
        self.acc3[...] = (own + self.got2[0]) + (self.got2[1] + self.got2[2])
        if self.direct:
            self.across_z()
            return
        size = CHUNK[self.group]
        for s in (4, 3, 5, 2, 6, 1, 7):
            to, peer = self.along("z", s)

            def send():
                self.copy(self.acc3.at[pl.ds(to * size, size)], self.got3.at[s - 1], 5 + s, peer).start()

            self.takes(to, send)

    def stage3(self):
        if self.direct:
            for s in range(1, ZS):
                self.copy(self.acc3, self.got3.at[0], 5 + s, self.partner).wait_recv()
            self.g_ref[pl.ds(self.second, SECOND[self.group])] = tree([self.got3[k] for k in range(ZS)])
            self.back()
            return
        size = CHUNK[self.group]
        own = self.second + self.z * size

        def total():
            for s in range(1, ZS):
                self.copy(self.got3.at[s - 1], self.got3.at[s - 1], 5 + s, self.partner).wait_recv()
            terms = [self.acc3[pl.ds(self.z * size, size)]] + [self.got3[s] for s in range(ZS - 1)]
            self.g_ref[pl.ds(own, size)] = tree(terms)
            for s in (4, 3, 5, 2, 6, 1, 7):
                to, peer = self.along("z", s)
                self.copy(self.chunk(own, size), self.chunk(own, size), 12 + s, peer).start()

        self.takes(self.z, total)

    def stage4(self):
        size = CHUNK[self.group]
        for s in range(1, ZS):
            sender = lax.rem(self.z + ZS - s, ZS)

            def receive():
                got = self.chunk(self.second + sender * size, size)
                self.copy(got, got, 12 + s, self.partner).wait_recv()

            self.takes(sender, receive)
        self.back()

    def back(self):
        mine = self.chunk(self.second, SECOND[self.group])
        for s in (2, 1, 3):
            to, peer = self.along("second", s)
            self.start(mine, mine, 19 + s, peer)

    def stage5(self):
        size = SECOND[self.group]
        for s in range(1, 4):
            got = self.chunk(self.first + lax.rem(self.b + 4 - s, 4) * size, size)
            self.copy(got, got, 19 + s, self.partner).wait_recv()
        mine = self.chunk(self.first, FIRST[self.group])
        for s in (2, 1, 3):
            to, peer = self.along("first", s)
            self.start(mine, mine, 22 + s, peer)
        self.start(mine, mine, 26, self.partner)

    def stage6(self):
        size = FIRST[self.group]
        for s in (1, 3, 2):
            got = self.chunk(self.half + lax.rem(self.a + 4 - s, 4) * size, size)
            self.copy(got, got, 22 + s, self.partner).wait_recv()
            self.start(got, got, 26 + s, self.partner)

    def stage7(self):
        size = FIRST[self.group]
        for s in range(4):
            got = self.chunk(self.other_half + lax.rem(self.b + 4 - s, 4) * size, size)
            self.copy(got, got, 26 + s, self.partner).wait_recv()

    def finish(self):
        for size, index in self.started:
            part = self.chunk(0, size)
            self.copy(part, part, index, self.partner).wait_send()
        if self.direct:
            return
        size = CHUNK[self.group]
        for s in range(1, ZS):
            to, peer = self.along("z", s)

            def sent():
                part = self.acc3.at[pl.ds(to * size, size)]
                self.copy(part, part, 5 + s, peer).wait_send()

            self.takes(to, sent)

            def sent_back():
                part = self.chunk(self.second, size)
                self.copy(part, part, 12 + s, peer).wait_send()

            self.takes(self.z, sent_back)


def orthonormalize_kernel(n, scale, src_ref, out_ref, *scratch):
    (own_ref, other_ref, held_hi, held_lo, p_ref, g_ref, cur_ref, d_ref, z_ref, x_ref, hi_ref, lo_ref, lane_ref) = scratch[:13]
    groups_scratch = [scratch[13 + 5 * g : 18 + 5 * g] for g in range(4)]
    (send, recv, x_send, x_recv, in_send, in_recv, pass_send, pass_recv, own_sem) = scratch[33:]
    rows_each, width = src_ref.shape[0], own_ref.shape[1]
    bands = src_ref.shape[1] // width
    per_panel = B // rows_each
    tiles = B // V
    me = lax.axis_index("band")
    core, x, y, z = coordinates()
    partner = device(1 - core, x, y, z)

    barrier = pltpu.get_barrier_semaphore()

    def greet(s, carry):
        pl.semaphore_signal(
            barrier, inc=1, device_id={"band": lax.rem(me + s, bands)}, device_id_type=MESH
        )
        return carry

    others = [device(core, x, y, lax.rem(z + s, ZS)) for s in range(1, ZS)]
    others += [device(core, lax.rem(x + s, XS), y, z) for s in (1, 3)]
    for peer in others:
        pl.semaphore_signal(barrier, inc=1, device_id=peer, device_id_type=MESH)
    lax.fori_loop(1, bands, greet, 0)

    def columns(ref, index):
        return ref.at[:, pl.ds(pl.multiple_of(index * width, width), width)]

    def band(ref, index):
        return ref.at[pl.ds(pl.multiple_of(index * rows_each, rows_each), rows_each), :]

    mine = pltpu.make_async_copy(columns(src_ref, me), band(own_ref, me), own_sem)
    mine.start()
    pl.semaphore_wait(barrier, bands - 1 + len(others))

    def bring(s, source):
        peer = lax.rem(me + s, bands)
        return pltpu.make_async_remote_copy(
            src_ref=columns(src_ref, peer),
            dst_ref=band(own_ref, source),
            send_sem=in_send.at[s],
            recv_sem=in_recv.at[s],
            device_id={"band": peer},
            device_id_type=MESH,
        )

    def hand_over(source):
        return pltpu.make_async_remote_copy(
            src_ref=band(own_ref, source),
            dst_ref=band(other_ref, source),
            send_sem=pass_send.at[source],
            recv_sem=pass_recv.at[source],
            device_id=partner,
            device_id_type=MESH,
        )

    def keep(ref, at):
        held_hi[:, at : at + width], held_lo[:, at : at + width] = split(ref[...])

    def start(s, carry):
        bring(s, me).start()
        return carry

    def arrive(s, carry):
        source = lax.rem(me - s + bands, bands)
        bring(s, source).wait_recv()
        hand_over(source).start()
        return carry

    def finish(s, carry):
        source = lax.rem(me + 1 - 2 * core - s + bands, bands)
        hand_over(source).wait_recv()
        return carry

    def sent(s, carry):
        bring(s, me).wait_send()
        hand_over(lax.rem(me + s, bands)).wait_send()
        return carry

    lax.fori_loop(1, bands, start, 0)
    mine.wait()
    hand_over(me).start()
    lax.fori_loop(1, bands, arrive, 0)
    keep(own_ref, 0)
    lax.fori_loop(0, bands, finish, 0)
    keep(other_ref, width)

    groups = grouped_blocks(n)

    def multiply(g):
        half = len(groups[g]) // CORES
        for c in range(CORES):

            @pl.when(core == c)
            def _():
                blocks = groups[g][c * half : (c + 1) * half]
                for i in sorted({i for i, _ in blocks}):
                    wanted = [j for k, j in blocks if k == i]
                    first, end = min(wanted), max(wanted) + 1
                    left = (held_hi[i * B : (i + 1) * B], held_lo[i * B : (i + 1) * B])
                    right = (held_hi[first * B : end * B], held_lo[first * B : end * B])
                    out = dot3(left, right, ((1,), (1,))) * scale
                    for j in wanted:
                        at = sum(HALF[:g]) + blocks.index((i, j)) * tiles
                        block = out[:, (j - first) * B : (j - first + 1) * B]
                        p_ref[at : at + tiles] = block.reshape(tiles, V, B)

    one, two, three, four = (Summing(g, p_ref, g_ref, groups_scratch[g], send, recv) for g in range(4))
    multiply(0)
    one.stage0()
    multiply(1)
    two.stage0()
    multiply(2)
    three.stage0()
    multiply(3)
    four.stage0()
    one.stage1()
    two.stage1()
    one.stage2()
    three.stage1()
    two.stage2()
    four.stage1()
    three.stage2()
    one.stage3()
    four.stage2()
    two.stage3()
    one.stage5()
    three.stage3()
    two.stage5()
    four.stage3()
    one.stage6()
    three.stage5()
    two.stage6()
    one.stage7()
    four.stage5()

    order = [block for group in groups for block in group]
    sub = lax.broadcasted_iota(jnp.int32, (V, B), 0)
    lane = lax.broadcasted_iota(jnp.int32, (V, B), 1)

    def prepare(k):
        at = order.index((k, k)) * tiles
        on_diagonal = [jnp.where(lane == q * V + sub, g_ref[at + q], 0.0) for q in range(tiles)]
        diagonal = jnp.sum(tree(on_diagonal), axis=0, keepdims=True)
        lanes = jnp.broadcast_to(lax.rsqrt(diagonal), (V, B))
        lane_ref[...] = lanes
        taken = None
        if k:
            left = (hi_ref[: k * B, k * B : (k + 1) * B], lo_ref[: k * B, k * B : (k + 1) * B])
            right = (hi_ref[: k * B, k * B :], lo_ref[: k * B, k * B :])
            taken = dot3(left, right, ((0,), (0,)))
        for j in range(k, n + width // B):
            if j < n:
                at = order.index((k, j)) * tiles
                block = g_ref[at : at + tiles].reshape(B, B)
            else:
                block = own_ref[k * B : (k + 1) * B, (j - n) * B : (j - n + 1) * B]
            if k:
                block = block - taken[:, (j - k) * B : (j - k + 1) * B]
            if j > k:
                cur_ref[:, j * B : (j + 1) * B] = block
                continue
            for q in range(tiles):
                rows = jnp.take_along_axis(lanes, q * V + sub, axis=1)
                d_ref[q * V : (q + 1) * V, :] = block[q * V : (q + 1) * V] * rows * lanes

    def remote(peer, sender):
        return pltpu.make_async_remote_copy(
            src_ref=x_ref.at[pl.ds(peer * rows_each, rows_each), :],
            dst_ref=columns(out_ref, sender),
            send_sem=x_send.at[peer],
            recv_sem=x_recv.at[sender],
            device_id={"band": peer},
            device_id_type=MESH,
        )

    stays = pltpu.make_async_copy(band(x_ref, me), columns(out_ref, me), own_sem)

    def step(i, carry):
        for k in range(n):

            @pl.when(i == k)
            def _():
                if k == 1:
                    two.stage7()
                if k == 2:
                    three.stage7()
                if k == 4:
                    four.stage7()
                prepare(k)

        rows = [d_ref[q * V : (q + 1) * V, :] for q in range(tiles)]
        lanes = lane_ref[...]
        for q, inverse in enumerate(factor_inverse(rows)):
            z_ref[q * V : (q + 1) * V, :] = inverse * lanes
        for k in range(n):

            @pl.when(i == k)
            def _():
                if k == 0:
                    three.stage6()
                if k == 1:
                    four.stage6()
                panel = dot3(split(z_ref[...]), split(cur_ref[:, (k + 1) * B :]), ((1,), (0,)))
                x_ref[k * B : (k + 1) * B, :] = panel[:, panel.shape[1] - width :]
                for peer in range(k * per_panel, (k + 1) * per_panel):

                    @pl.when(peer != me)
                    def _():
                        remote(peer, me).start()

                    @pl.when(peer == me)
                    def _():
                        stays.start()

                if k < n - 1:
                    high, low = split(panel)
                    hi_ref[k * B : (k + 1) * B, (k + 1) * B :] = high
                    lo_ref[k * B : (k + 1) * B, (k + 1) * B :] = low

        return carry

    lax.fori_loop(0, n, step, 0)
    lax.fori_loop(1, bands, sent, 0)
    hand_over(me).wait_send()
    for group in (one, two, three, four):
        group.finish()
    stays.wait()
    for other in range(bands):

        @pl.when(other != me)
        def _():
            remote(other, me).wait_send()
            remote(other, other).wait_recv()


def orthonormalize(coeffs, bands, columns_all):
    rows_each, columns = coeffs.shape
    rows, width = rows_each * bands, columns // bands
    n = rows // B
    tiles = lambda *shape: pltpu.VMEM((*shape, V, B), jnp.float32)
    whole = n * B + width
    summing = []
    for g in range(4):
        summing += [tiles(FIRST[g]), tiles(SECOND[g]), tiles(3, FIRST[g]), tiles(3, SECOND[g])]
        summing += [tiles(ZS - 1, CHUNK[g]) if Z_USED[g] else tiles(ZS, SECOND[g])]
    return pl.pallas_call(
        functools.partial(orthonormalize_kernel, n, 1.0 / columns_all),
        out_shape=jax.ShapeDtypeStruct(coeffs.shape, jnp.float32),
        in_specs=[pl.BlockSpec(memory_space=pltpu.HBM)],
        out_specs=pl.BlockSpec(memory_space=pltpu.VMEM),
        scratch_shapes=[
            pltpu.VMEM((rows, width), jnp.float32),
            pltpu.VMEM((rows, width), jnp.float32),
            pltpu.VMEM((rows, CORES * width), jnp.bfloat16),
            pltpu.VMEM((rows, CORES * width), jnp.bfloat16),
            tiles(sum(HALF)),
            tiles(sum(TOTAL)),
            pltpu.VMEM((B, whole), jnp.float32),
            pltpu.VMEM((B, B), jnp.float32),
            pltpu.VMEM((B, B), jnp.float32),
            pltpu.VMEM((rows, width), jnp.float32),
            pltpu.VMEM((rows, whole), jnp.bfloat16),
            pltpu.VMEM((rows, whole), jnp.bfloat16),
            pltpu.VMEM((V, B), jnp.float32),
            *summing,
            pltpu.SemaphoreType.DMA((4 * COPIES,)),
            pltpu.SemaphoreType.DMA((4 * COPIES,)),
            *[pltpu.SemaphoreType.DMA((bands,))] * 6,
            pltpu.SemaphoreType.DMA,
        ],
        compiler_params=pltpu.CompilerParams(
            collective_id=0, has_side_effects=True, vmem_limit_bytes=52 << 20
        ),
        name="orthonormalize",
    )(coeffs)


def local(coeffs):
    bands = lax.axis_size("band")
    return orthonormalize(coeffs, bands, coeffs.shape[1] * lax.axis_size("ga"))


def solution(mesh):
    return jax.shard_map(
        local,
        mesh=mesh,
        in_specs=(P("band", "ga"),),
        out_specs=P("band", "ga"),
        check_vma=False,
    )
```

```python
import functools

import jax
import jax.numpy as jnp
from jax import lax
from jax.experimental import pallas as pl
from jax.experimental.pallas import tpu as pltpu
from jax.sharding import PartitionSpec as P

MESH = pl.DeviceIdType.MESH

B = 128
V = 8


def split(x):
    hi = x.astype(jnp.bfloat16)
    return hi, (x - hi.astype(jnp.float32)).astype(jnp.bfloat16)


def dot3(a, b, dims):
    (ca,), (cb,) = dims
    ah, al = a
    bh, bl = b
    left = jnp.concatenate([ah, al, ah], axis=ca)
    right = jnp.concatenate([bh, bh, bl], axis=cb)
    return lax.dot_general(left, right, (dims, ((), ())), preferred_element_type=jnp.float32)


def lane_col(t, c):
    return jnp.take_along_axis(t, jnp.full((V, B), c, jnp.int32), axis=1)


def sub_row(t, k):
    return jnp.broadcast_to(t[k : k + 1, :], (V, B))


def tree(m):
    while len(m) > 1:
        m = [m[e] + m[e + 1] if e + 1 < len(m) else m[e] for e in range(0, len(m), 2)]
    return m[0]


def factor_inverse(rows):
    n = len(rows)
    rows = list(rows)
    sub = lax.broadcasted_iota(jnp.int32, (V, B), 0)
    lane = lax.broadcasted_iota(jnp.int32, (V, B), 1)
    out = []
    cols = [lane_col(rows[0], k) for k in range(V)]
    for p in range(n):
        c0 = p * V
        last = p == n - 1
        in_block = (lane >= c0) & (lane < c0 + V)
        t = jnp.where(in_block, jnp.where(lane - c0 == sub, 1.0, 0.0), rows[p])
        f = jnp.where(lane < c0 + V, t, 0.0)
        pivots = None
        below_m = {q: [lane_col(rows[q], c0 + k) for k in range(V)] for q in range(p + 1, n)}
        if not last:
            a = list(below_m[p + 1])
            ahead = [lane_col(rows[p + 1], c0 + V + k) for k in range(V)]
        for k in range(0, V, 2):
            h1, h2 = sub == k, sub == k + 1
            here = h1 | h2
            d11, d12, d22 = sub_row(cols[k], k), sub_row(cols[k + 1], k), sub_row(cols[k + 1], k + 1)
            det = d11 * d22 - d12 * d12
            r = 1.0 / det
            m1, m2 = jnp.where(here, 0.0, cols[k]), jnp.where(here, 0.0, cols[k + 1])

            def solve(col):
                v1, v2 = sub_row(col, k), sub_row(col, k + 1)
                return (d22 * v1 - d12 * v2) * r, (d11 * v2 - d12 * v1) * r

            def eliminate(col):
                u1, u2 = solve(col)
                return jnp.where(h1, u1, jnp.where(h2, u2, col - (m1 * u1 + m2 * u2))), u1, u2

            for j in range(k + 2, V):
                cols[j], u1, u2 = eliminate(cols[j])
                if not last:
                    a[j] = a[j] - (a[k] * u1 + a[k + 1] * u2)
            if not last:
                s1 = (d22 * a[k] - d12 * a[k + 1]) * r
                s2 = (d11 * a[k + 1] - d12 * a[k]) * r
                for j in range(V):
                    ahead[j] = ahead[j] - (s1 * sub_row(a[k], j) + s2 * sub_row(a[k + 1], j))
            q = 1.0 / d11
            ratio = d12 * q
            f1 = sub_row(f, k)
            f2 = sub_row(f, k + 1) - ratio * f1
            g2 = d11 * r
            g1 = q
            below = sub > k + 1
            b1 = jnp.where(below, cols[k], 0.0)
            b2 = jnp.where(below, cols[k + 1], 0.0)
            l2 = b2 - b1 * ratio
            f = jnp.where(h2, f2, f - b1 * (f1 * g1) - l2 * (f2 * g2))
            t, _, _ = eliminate(t)
            scale = jnp.where(h1, g1, g2)
            pivots = scale if pivots is None else jnp.where(here, scale, pivots)
        out.append(f * jnp.sqrt(pivots))
        if last:
            break
        cols = ahead
        w = [sub_row(t, k) for k in range(V)]
        for q in range(p + 1, n):
            acc = jnp.where(in_block, 0.0, rows[q])
            rows[q] = acc - tree([below_m[q][k] * w[k] for k in range(V)])
    return out


CORES, YS, XS, ZS = 2, 4, 4, 8
TOTAL = (128, 128, 96, 224)
HALF = tuple(t // 2 for t in TOTAL)
FIRST = tuple(t // 8 for t in TOTAL)
SECOND = tuple(t // 32 for t in TOTAL)
Z_USED = (0, 0, 0, 0)
CHUNK = tuple(t // max(z, 1) for t, z in zip(SECOND, Z_USED))
COPIES = 30


def grouped_blocks(n):
    first = [(0, j) for j in range(n)]
    second = [(1, j) for j in range(1, n)] + [(2, 2)]
    third = [(2, j) for j in range(3, n)] + [(3, 3)]
    rest = [(i, j) for i in range(3, n) for j in range(i, n) if (i, j) != (3, 3)]
    return first, second, third, rest


def coordinates():
    band, ga = lax.axis_index("band"), lax.axis_index("ga")
    core, y = lax.rem(band, CORES), lax.rem(band // CORES, YS)
    x = (band // (CORES * YS)) * 2 + lax.rem(ga, 2)
    return core, x, y, ga // 2


def device(core, x, y, z):
    return {"band": ((x // 2) * YS + y) * CORES + core, "ga": z * 2 + lax.rem(x, 2)}


class Summing:
    def __init__(self, group, p_ref, g_ref, scratch, send, recv):
        self.group, self.p_ref, self.g_ref = group, p_ref, g_ref
        self.acc2, self.acc3, self.got1, self.got2, self.got3 = scratch
        self.send, self.recv = send, recv
        self.direct = Z_USED[group] == 0
        core, x, y, z = self.at = coordinates()
        self.core, self.z = core, z
        self.a = jnp.where(core == 0, y, x)
        self.b = jnp.where(core == 0, x, y)
        self.partner = device(1 - core, x, y, z)
        self.from_p = sum(HALF[:group])
        base = sum(TOTAL[:group])
        self.half = base + core * HALF[group]
        self.first = self.half + self.a * FIRST[group]
        self.second = self.first + self.b * SECOND[group]
        self.other_half = base + (1 - core) * HALF[group]
        self.started = []

    def along(self, stage, s):
        core, x, y, z = self.at
        if stage == "z":
            to = lax.rem(z + s, ZS)
            return to, device(core, x, y, to)
        at = self.a if stage == "first" else self.b
        to = lax.rem(at + s, 4)
        on_y = core == (0 if stage == "first" else 1)
        return to, device(core, jnp.where(on_y, x, to), jnp.where(on_y, to, y), z)

    def copy(self, src, dst, index, peer):
        return pltpu.make_async_remote_copy(
            src_ref=src,
            dst_ref=dst,
            send_sem=self.send.at[self.group * COPIES + index],
            recv_sem=self.recv.at[self.group * COPIES + index],
            device_id=peer,
            device_id_type=MESH,
        )

    def start(self, src, dst, index, peer):
        self.copy(src, dst, index, peer).start()
        self.started.append((src.shape[0], index))

    def chunk(self, at, size):
        return self.g_ref.at[pl.ds(at, size)]

    def takes(self, z, then):
        if Z_USED[self.group] == ZS:
            then()
        else:
            pl.when(z < Z_USED[self.group])(then)

    def stage0(self):
        size = FIRST[self.group]
        for s in (2, 1, 3):
            to, peer = self.along("first", s)
            self.start(self.p_ref.at[pl.ds(self.from_p + to * size, size)], self.got1.at[s - 1], s - 1, peer)

    def stage1(self):
        size, step = FIRST[self.group], 4
        for s in range(3):
            self.copy(self.got1.at[s], self.got1.at[s], s, self.partner).wait_recv()

        def add(t, carry):
            at = pl.ds(t * step, step)
            own = self.p_ref[pl.ds(self.from_p + self.a * size + t * step, step)]
            self.acc2[at] = (own + self.got1[0, at]) + (self.got1[1, at] + self.got1[2, at])
            return carry

        lax.fori_loop(0, size // step, add, 0)
        size = SECOND[self.group]
        for s in (2, 1, 3):
            to, peer = self.along("second", s)
            self.start(self.acc2.at[pl.ds(to * size, size)], self.got2.at[s - 1], 2 + s, peer)

    def across_z(self):
        size = SECOND[self.group]
        self.got3[pl.ds(self.z, 1)] = self.acc3[...][None]
        for s in (4, 3, 5, 2, 6, 1, 7):
            to, peer = self.along("z", s)
            self.start(self.acc3, self.got3.at[self.z], 5 + s, peer)

    def stage2(self):
        size = SECOND[self.group]
        for s in range(3):
            self.copy(self.got2.at[s], self.got2.at[s], 3 + s, self.partner).wait_recv()
        own = self.acc2[pl.ds(self.b * size, size)]
        self.acc3[...] = (own + self.got2[0]) + (self.got2[1] + self.got2[2])
        if self.direct:
            self.across_z()
            return
        size = CHUNK[self.group]
        for s in (4, 3, 5, 2, 6, 1, 7):
            to, peer = self.along("z", s)

            def send():
                self.copy(self.acc3.at[pl.ds(to * size, size)], self.got3.at[s - 1], 5 + s, peer).start()

            self.takes(to, send)

    def stage3(self):
        if self.direct:
            for s in range(1, ZS):
                self.copy(self.acc3, self.got3.at[0], 5 + s, self.partner).wait_recv()
            self.g_ref[pl.ds(self.second, SECOND[self.group])] = tree([self.got3[k] for k in range(ZS)])
            self.back()
            return
        size = CHUNK[self.group]
        own = self.second + self.z * size

        def total():
            for s in range(1, ZS):
                self.copy(self.got3.at[s - 1], self.got3.at[s - 1], 5 + s, self.partner).wait_recv()
            terms = [self.acc3[pl.ds(self.z * size, size)]] + [self.got3[s] for s in range(ZS - 1)]
            self.g_ref[pl.ds(own, size)] = tree(terms)
            for s in (4, 3, 5, 2, 6, 1, 7):
                to, peer = self.along("z", s)
                self.copy(self.chunk(own, size), self.chunk(own, size), 12 + s, peer).start()

        self.takes(self.z, total)

    def stage4(self):
        size = CHUNK[self.group]
        for s in range(1, ZS):
            sender = lax.rem(self.z + ZS - s, ZS)

            def receive():
                got = self.chunk(self.second + sender * size, size)
                self.copy(got, got, 12 + s, self.partner).wait_recv()

            self.takes(sender, receive)
        self.back()

    def back(self):
        mine = self.chunk(self.second, SECOND[self.group])
        for s in (2, 1, 3):
            to, peer = self.along("second", s)
            self.start(mine, mine, 19 + s, peer)

    def stage5(self):
        size = SECOND[self.group]
        for s in range(1, 4):
            got = self.chunk(self.first + lax.rem(self.b + 4 - s, 4) * size, size)
            self.copy(got, got, 19 + s, self.partner).wait_recv()
        mine = self.chunk(self.first, FIRST[self.group])
        for s in (2, 1, 3):
            to, peer = self.along("first", s)
            self.start(mine, mine, 22 + s, peer)
        self.start(mine, mine, 26, self.partner)

    def stage6(self):
        size = FIRST[self.group]
        for s in (1, 3, 2):
            got = self.chunk(self.half + lax.rem(self.a + 4 - s, 4) * size, size)
            self.copy(got, got, 22 + s, self.partner).wait_recv()
            self.start(got, got, 26 + s, self.partner)

    def stage7(self):
        size = FIRST[self.group]
        for s in range(4):
            got = self.chunk(self.other_half + lax.rem(self.b + 4 - s, 4) * size, size)
            self.copy(got, got, 26 + s, self.partner).wait_recv()

    def finish(self):
        for size, index in self.started:
            part = self.chunk(0, size)
            self.copy(part, part, index, self.partner).wait_send()
        if self.direct:
            return
        size = CHUNK[self.group]
        for s in range(1, ZS):
            to, peer = self.along("z", s)

            def sent():
                part = self.acc3.at[pl.ds(to * size, size)]
                self.copy(part, part, 5 + s, peer).wait_send()

            self.takes(to, sent)

            def sent_back():
                part = self.chunk(self.second, size)
                self.copy(part, part, 12 + s, peer).wait_send()

            self.takes(self.z, sent_back)


def orthonormalize_kernel(n, scale, src_ref, out_ref, *scratch):
    (own_ref, other_ref, held_hi, held_lo, p_ref, g_ref, cur_ref, d_ref, z_ref, x_ref, hi_ref, lo_ref, lane_ref) = scratch[:13]
    groups_scratch = [scratch[13 + 5 * g : 18 + 5 * g] for g in range(4)]
    (send, recv, x_send, x_recv, in_send, in_recv, pass_send, pass_recv, own_sem) = scratch[33:]
    rows_each, width = src_ref.shape[0], own_ref.shape[1]
    bands = src_ref.shape[1] // width
    per_panel = B // rows_each
    tiles = B // V
    me = lax.axis_index("band")
    core, x, y, z = coordinates()
    partner = device(1 - core, x, y, z)

    barrier = pltpu.get_barrier_semaphore()

    def greet(s, carry):
        pl.semaphore_signal(
            barrier, inc=1, device_id={"band": lax.rem(me + s, bands)}, device_id_type=MESH
        )
        return carry

    others = [device(core, x, y, lax.rem(z + s, ZS)) for s in range(1, ZS)]
    others += [device(core, lax.rem(x + s, XS), y, z) for s in (1, 3)]
    for peer in others:
        pl.semaphore_signal(barrier, inc=1, device_id=peer, device_id_type=MESH)
    lax.fori_loop(1, bands, greet, 0)

    def columns(ref, index):
        return ref.at[:, pl.ds(pl.multiple_of(index * width, width), width)]

    def band(ref, index):
        return ref.at[pl.ds(pl.multiple_of(index * rows_each, rows_each), rows_each), :]

    mine = pltpu.make_async_copy(columns(src_ref, me), band(own_ref, me), own_sem)
    mine.start()
    pl.semaphore_wait(barrier, bands - 1 + len(others))

    def bring(s, source):
        peer = lax.rem(me + s, bands)
        return pltpu.make_async_remote_copy(
            src_ref=columns(src_ref, peer),
            dst_ref=band(own_ref, source),
            send_sem=in_send.at[s],
            recv_sem=in_recv.at[s],
            device_id={"band": peer},
            device_id_type=MESH,
        )

    def hand_over(source):
        return pltpu.make_async_remote_copy(
            src_ref=band(own_ref, source),
            dst_ref=band(other_ref, source),
            send_sem=pass_send.at[source],
            recv_sem=pass_recv.at[source],
            device_id=partner,
            device_id_type=MESH,
        )

    def keep(ref, source, at):
        rows = pl.ds(pl.multiple_of(source * rows_each, rows_each), rows_each)
        high, low = split(ref[rows, :])
        held_hi[rows, at : at + width] = high
        held_lo[rows, at : at + width] = low

    def start(s, carry):
        bring(s, me).start()
        return carry

    def arrive(s, carry):
        source = lax.rem(me - s + bands, bands)
        bring(s, source).wait_recv()
        hand_over(source).start()
        keep(own_ref, source, 0)
        return carry

    def finish(s, carry):
        source = lax.rem(me + 1 - 2 * core - s + bands, bands)
        hand_over(source).wait_recv()
        keep(other_ref, source, width)
        return carry

    def sent(s, carry):
        bring(s, me).wait_send()
        hand_over(lax.rem(me + s, bands)).wait_send()
        return carry

    lax.fori_loop(1, bands, start, 0)
    mine.wait()
    hand_over(me).start()
    keep(own_ref, me, 0)
    lax.fori_loop(1, bands, arrive, 0)
    lax.fori_loop(0, bands, finish, 0)

    groups = grouped_blocks(n)

    def multiply(g):
        half = len(groups[g]) // CORES
        for c in range(CORES):

            @pl.when(core == c)
            def _():
                blocks = groups[g][c * half : (c + 1) * half]
                for i in sorted({i for i, _ in blocks}):
                    wanted = [j for k, j in blocks if k == i]
                    first, end = min(wanted), max(wanted) + 1
                    left = (held_hi[i * B : (i + 1) * B], held_lo[i * B : (i + 1) * B])
                    right = (held_hi[first * B : end * B], held_lo[first * B : end * B])
                    out = dot3(left, right, ((1,), (1,))) * scale
                    for j in wanted:
                        at = sum(HALF[:g]) + blocks.index((i, j)) * tiles
                        block = out[:, (j - first) * B : (j - first + 1) * B]
                        p_ref[at : at + tiles] = block.reshape(tiles, V, B)

    one, two, three, four = (Summing(g, p_ref, g_ref, groups_scratch[g], send, recv) for g in range(4))
    multiply(0)
    one.stage0()
    multiply(1)
    two.stage0()
    multiply(2)
    three.stage0()
    multiply(3)
    four.stage0()
    one.stage1()
    two.stage1()
    one.stage2()
    three.stage1()
    two.stage2()
    four.stage1()
    three.stage2()
    one.stage3()
    four.stage2()
    two.stage3()
    one.stage5()
    three.stage3()
    two.stage5()
    four.stage3()
    one.stage6()
    three.stage5()
    two.stage6()
    one.stage7()
    four.stage5()

    order = [block for group in groups for block in group]
    sub = lax.broadcasted_iota(jnp.int32, (V, B), 0)
    lane = lax.broadcasted_iota(jnp.int32, (V, B), 1)

    def prepare(k):
        at = order.index((k, k)) * tiles
        on_diagonal = [jnp.where(lane == q * V + sub, g_ref[at + q], 0.0) for q in range(tiles)]
        diagonal = jnp.sum(tree(on_diagonal), axis=0, keepdims=True)
        lanes = jnp.broadcast_to(lax.rsqrt(diagonal), (V, B))
        lane_ref[...] = lanes
        taken = None
        if k:
            left = (hi_ref[: k * B, k * B : (k + 1) * B], lo_ref[: k * B, k * B : (k + 1) * B])
            right = (hi_ref[: k * B, k * B :], lo_ref[: k * B, k * B :])
            taken = dot3(left, right, ((0,), (0,)))
        for j in range(k, n + width // B):
            if j < n:
                at = order.index((k, j)) * tiles
                block = g_ref[at : at + tiles].reshape(B, B)
            else:
                block = own_ref[k * B : (k + 1) * B, (j - n) * B : (j - n + 1) * B]
            if k:
                block = block - taken[:, (j - k) * B : (j - k + 1) * B]
            if j > k:
                cur_ref[:, j * B : (j + 1) * B] = block
                continue
            for q in range(tiles):
                rows = jnp.take_along_axis(lanes, q * V + sub, axis=1)
                d_ref[q * V : (q + 1) * V, :] = block[q * V : (q + 1) * V] * rows * lanes

    def remote(peer, sender):
        return pltpu.make_async_remote_copy(
            src_ref=x_ref.at[pl.ds(peer * rows_each, rows_each), :],
            dst_ref=columns(out_ref, sender),
            send_sem=x_send.at[peer],
            recv_sem=x_recv.at[sender],
            device_id={"band": peer},
            device_id_type=MESH,
        )

    stays = pltpu.make_async_copy(band(x_ref, me), columns(out_ref, me), own_sem)

    def step(i, carry):
        for k in range(n):

            @pl.when(i == k)
            def _():
                if k == 1:
                    two.stage7()
                if k == 2:
                    three.stage7()
                if k == 3:
                    four.stage7()
                prepare(k)

        rows = [d_ref[q * V : (q + 1) * V, :] for q in range(tiles)]
        lanes = lane_ref[...]
        for q, inverse in enumerate(factor_inverse(rows)):
            z_ref[q * V : (q + 1) * V, :] = inverse * lanes
        for k in range(n):

            @pl.when(i == k)
            def _():
                if k == 0:
                    three.stage6()
                if k == 1:
                    four.stage6()
                panel = dot3(split(z_ref[...]), split(cur_ref[:, (k + 1) * B :]), ((1,), (0,)))
                x_ref[k * B : (k + 1) * B, :] = panel[:, panel.shape[1] - width :]
                for peer in range(k * per_panel, (k + 1) * per_panel):

                    @pl.when(peer != me)
                    def _():
                        remote(peer, me).start()

                    @pl.when(peer == me)
                    def _():
                        stays.start()

                if k < n - 1:
                    high, low = split(panel)
                    hi_ref[k * B : (k + 1) * B, (k + 1) * B :] = high
                    lo_ref[k * B : (k + 1) * B, (k + 1) * B :] = low

        return carry

    lax.fori_loop(0, n, step, 0)
    lax.fori_loop(1, bands, sent, 0)
    hand_over(me).wait_send()
    for group in (one, two, three, four):
        group.finish()
    stays.wait()
    for other in range(bands):

        @pl.when(other != me)
        def _():
            remote(other, me).wait_send()
            remote(other, other).wait_recv()


def orthonormalize(coeffs, bands, columns_all):
    rows_each, columns = coeffs.shape
    rows, width = rows_each * bands, columns // bands
    n = rows // B
    tiles = lambda *shape: pltpu.VMEM((*shape, V, B), jnp.float32)
    whole = n * B + width
    summing = []
    for g in range(4):
        summing += [tiles(FIRST[g]), tiles(SECOND[g]), tiles(3, FIRST[g]), tiles(3, SECOND[g])]
        summing += [tiles(ZS - 1, CHUNK[g]) if Z_USED[g] else tiles(ZS, SECOND[g])]
    return pl.pallas_call(
        functools.partial(orthonormalize_kernel, n, 1.0 / columns_all),
        out_shape=jax.ShapeDtypeStruct(coeffs.shape, jnp.float32),
        in_specs=[pl.BlockSpec(memory_space=pltpu.HBM)],
        out_specs=pl.BlockSpec(memory_space=pltpu.VMEM),
        scratch_shapes=[
            pltpu.VMEM((rows, width), jnp.float32),
            pltpu.VMEM((rows, width), jnp.float32),
            pltpu.VMEM((rows, CORES * width), jnp.bfloat16),
            pltpu.VMEM((rows, CORES * width), jnp.bfloat16),
            tiles(sum(HALF)),
            tiles(sum(TOTAL)),
            pltpu.VMEM((B, whole), jnp.float32),
            pltpu.VMEM((B, B), jnp.float32),
            pltpu.VMEM((B, B), jnp.float32),
            pltpu.VMEM((rows, width), jnp.float32),
            pltpu.VMEM((rows, whole), jnp.bfloat16),
            pltpu.VMEM((rows, whole), jnp.bfloat16),
            pltpu.VMEM((V, B), jnp.float32),
            *summing,
            pltpu.SemaphoreType.DMA((4 * COPIES,)),
            pltpu.SemaphoreType.DMA((4 * COPIES,)),
            *[pltpu.SemaphoreType.DMA((bands,))] * 6,
            pltpu.SemaphoreType.DMA,
        ],
        compiler_params=pltpu.CompilerParams(
            collective_id=0, has_side_effects=True, vmem_limit_bytes=52 << 20
        ),
        name="orthonormalize",
    )(coeffs)


def local(coeffs):
    bands = lax.axis_size("band")
    return orthonormalize(coeffs, bands, coeffs.shape[1] * lax.axis_size("ga"))


def solution(mesh):
    return jax.shard_map(
        local,
        mesh=mesh,
        in_specs=(P("band", "ga"),),
        out_specs=P("band", "ga"),
        check_vma=False,
    )
```

```python
import functools

import jax
import jax.numpy as jnp
from jax import lax
from jax.experimental import pallas as pl
from jax.experimental.pallas import tpu as pltpu
from jax.sharding import PartitionSpec as P

MESH = pl.DeviceIdType.MESH

B = 128
V = 8


def split(x):
    hi = x.astype(jnp.bfloat16)
    return hi, (x - hi.astype(jnp.float32)).astype(jnp.bfloat16)


def dot3(a, b, dims):
    (ca,), (cb,) = dims
    ah, al = a
    bh, bl = b
    left = jnp.concatenate([ah, al, ah], axis=ca)
    right = jnp.concatenate([bh, bh, bl], axis=cb)
    return lax.dot_general(left, right, (dims, ((), ())), preferred_element_type=jnp.float32)


def lane_col(t, c):
    return jnp.take_along_axis(t, jnp.full((V, B), c, jnp.int32), axis=1)


def sub_row(t, k):
    return jnp.broadcast_to(t[k : k + 1, :], (V, B))


def tree(m):
    while len(m) > 1:
        m = [m[e] + m[e + 1] if e + 1 < len(m) else m[e] for e in range(0, len(m), 2)]
    return m[0]


def factor_inverse(rows):
    n = len(rows)
    rows = list(rows)
    sub = lax.broadcasted_iota(jnp.int32, (V, B), 0)
    lane = lax.broadcasted_iota(jnp.int32, (V, B), 1)
    out = []
    cols = [lane_col(rows[0], k) for k in range(V)]
    for p in range(n):
        c0 = p * V
        last = p == n - 1
        in_block = (lane >= c0) & (lane < c0 + V)
        t = jnp.where(in_block, jnp.where(lane - c0 == sub, 1.0, 0.0), rows[p])
        f = jnp.where(lane < c0 + V, t, 0.0)
        pivots = None
        below_m = {q: [lane_col(rows[q], c0 + k) for k in range(V)] for q in range(p + 1, n)}
        if not last:
            a = list(below_m[p + 1])
            ahead = [lane_col(rows[p + 1], c0 + V + k) for k in range(V)]
        for k in range(0, V, 2):
            h1, h2 = sub == k, sub == k + 1
            here = h1 | h2
            d11, d12, d22 = sub_row(cols[k], k), sub_row(cols[k + 1], k), sub_row(cols[k + 1], k + 1)
            det = d11 * d22 - d12 * d12
            r = 1.0 / det
            m1, m2 = jnp.where(here, 0.0, cols[k]), jnp.where(here, 0.0, cols[k + 1])

            def solve(col):
                v1, v2 = sub_row(col, k), sub_row(col, k + 1)
                return (d22 * v1 - d12 * v2) * r, (d11 * v2 - d12 * v1) * r

            def eliminate(col):
                u1, u2 = solve(col)
                return jnp.where(h1, u1, jnp.where(h2, u2, col - (m1 * u1 + m2 * u2))), u1, u2

            for j in range(k + 2, V):
                cols[j], u1, u2 = eliminate(cols[j])
                if not last:
                    a[j] = a[j] - (a[k] * u1 + a[k + 1] * u2)
            if not last:
                s1 = (d22 * a[k] - d12 * a[k + 1]) * r
                s2 = (d11 * a[k + 1] - d12 * a[k]) * r
                for j in range(V):
                    ahead[j] = ahead[j] - (s1 * sub_row(a[k], j) + s2 * sub_row(a[k + 1], j))
            q = 1.0 / d11
            ratio = d12 * q
            f1 = sub_row(f, k)
            f2 = sub_row(f, k + 1) - ratio * f1
            g2 = d11 * r
            g1 = q
            below = sub > k + 1
            b1 = jnp.where(below, cols[k], 0.0)
            b2 = jnp.where(below, cols[k + 1], 0.0)
            l2 = b2 - b1 * ratio
            f = jnp.where(h2, f2, f - b1 * (f1 * g1) - l2 * (f2 * g2))
            t, _, _ = eliminate(t)
            scale = jnp.where(h1, g1, g2)
            pivots = scale if pivots is None else jnp.where(here, scale, pivots)
        out.append(f * jnp.sqrt(pivots))
        if last:
            break
        cols = ahead
        w = [sub_row(t, k) for k in range(V)]
        for q in range(p + 1, n):
            acc = jnp.where(in_block, 0.0, rows[q])
            rows[q] = acc - tree([below_m[q][k] * w[k] for k in range(V)])
    return out


CORES, YS, XS, ZS = 2, 4, 4, 8
TOTAL = (128, 128, 160, 160)
HALF = tuple(t // 2 for t in TOTAL)
FIRST = tuple(t // 8 for t in TOTAL)
SECOND = tuple(t // 32 for t in TOTAL)
Z_USED = (0, 0, 0, 0)
CHUNK = tuple(t // max(z, 1) for t, z in zip(SECOND, Z_USED))
COPIES = 30


def grouped_blocks(n):
    first = [(0, j) for j in range(n)]
    second = [(1, j) for j in range(1, n)] + [(2, 2)]
    third = [(i, j) for i in (2, 3) for j in range(3, n)]
    rest = [(i, j) for i in range(4, n) for j in range(i, n)]
    return first, second, third, rest


def coordinates():
    band, ga = lax.axis_index("band"), lax.axis_index("ga")
    core, y = lax.rem(band, CORES), lax.rem(band // CORES, YS)
    x = (band // (CORES * YS)) * 2 + lax.rem(ga, 2)
    return core, x, y, ga // 2


def device(core, x, y, z):
    return {"band": ((x // 2) * YS + y) * CORES + core, "ga": z * 2 + lax.rem(x, 2)}


class Summing:
    def __init__(self, group, p_ref, g_ref, scratch, send, recv):
        self.group, self.p_ref, self.g_ref = group, p_ref, g_ref
        self.acc2, self.acc3, self.got1, self.got2, self.got3 = scratch
        self.send, self.recv = send, recv
        self.direct = Z_USED[group] == 0
        core, x, y, z = self.at = coordinates()
        self.core, self.z = core, z
        self.a = jnp.where(core == 0, y, x)
        self.b = jnp.where(core == 0, x, y)
        self.partner = device(1 - core, x, y, z)
        self.from_p = sum(HALF[:group])
        base = sum(TOTAL[:group])
        self.half = base + core * HALF[group]
        self.first = self.half + self.a * FIRST[group]
        self.second = self.first + self.b * SECOND[group]
        self.other_half = base + (1 - core) * HALF[group]
        self.started = []

    def along(self, stage, s):
        core, x, y, z = self.at
        if stage == "z":
            to = lax.rem(z + s, ZS)
            return to, device(core, x, y, to)
        at = self.a if stage == "first" else self.b
        to = lax.rem(at + s, 4)
        on_y = core == (0 if stage == "first" else 1)
        return to, device(core, jnp.where(on_y, x, to), jnp.where(on_y, to, y), z)

    def copy(self, src, dst, index, peer):
        return pltpu.make_async_remote_copy(
            src_ref=src,
            dst_ref=dst,
            send_sem=self.send.at[self.group * COPIES + index],
            recv_sem=self.recv.at[self.group * COPIES + index],
            device_id=peer,
            device_id_type=MESH,
        )

    def start(self, src, dst, index, peer):
        self.copy(src, dst, index, peer).start()
        self.started.append((src.shape[0], index))

    def chunk(self, at, size):
        return self.g_ref.at[pl.ds(at, size)]

    def takes(self, z, then):
        if Z_USED[self.group] == ZS:
            then()
        else:
            pl.when(z < Z_USED[self.group])(then)

    def stage0(self):
        size = FIRST[self.group]
        for s in (2, 1, 3):
            to, peer = self.along("first", s)
            self.start(self.p_ref.at[pl.ds(self.from_p + to * size, size)], self.got1.at[s - 1], s - 1, peer)

    def stage1(self):
        size, step = FIRST[self.group], 4
        for s in range(3):
            self.copy(self.got1.at[s], self.got1.at[s], s, self.partner).wait_recv()

        def add(t, carry):
            at = pl.ds(t * step, step)
            own = self.p_ref[pl.ds(self.from_p + self.a * size + t * step, step)]
            self.acc2[at] = (own + self.got1[0, at]) + (self.got1[1, at] + self.got1[2, at])
            return carry

        lax.fori_loop(0, size // step, add, 0)
        size = SECOND[self.group]
        for s in (2, 1, 3):
            to, peer = self.along("second", s)
            self.start(self.acc2.at[pl.ds(to * size, size)], self.got2.at[s - 1], 2 + s, peer)

    def across_z(self):
        size = SECOND[self.group]
        self.got3[pl.ds(self.z, 1)] = self.acc3[...][None]
        for s in (4, 3, 5, 2, 6, 1, 7):
            to, peer = self.along("z", s)
            self.start(self.acc3, self.got3.at[self.z], 5 + s, peer)

    def stage2(self):
        size = SECOND[self.group]
        for s in range(3):
            self.copy(self.got2.at[s], self.got2.at[s], 3 + s, self.partner).wait_recv()
        own = self.acc2[pl.ds(self.b * size, size)]
        self.acc3[...] = (own + self.got2[0]) + (self.got2[1] + self.got2[2])
        if self.direct:
            self.across_z()
            return
        size = CHUNK[self.group]
        for s in (4, 3, 5, 2, 6, 1, 7):
            to, peer = self.along("z", s)

            def send():
                self.copy(self.acc3.at[pl.ds(to * size, size)], self.got3.at[s - 1], 5 + s, peer).start()

            self.takes(to, send)

    def stage3(self):
        if self.direct:
            for s in range(1, ZS):
                self.copy(self.acc3, self.got3.at[0], 5 + s, self.partner).wait_recv()
            self.g_ref[pl.ds(self.second, SECOND[self.group])] = tree([self.got3[k] for k in range(ZS)])
            self.back()
            return
        size = CHUNK[self.group]
        own = self.second + self.z * size

        def total():
            for s in range(1, ZS):
                self.copy(self.got3.at[s - 1], self.got3.at[s - 1], 5 + s, self.partner).wait_recv()
            terms = [self.acc3[pl.ds(self.z * size, size)]] + [self.got3[s] for s in range(ZS - 1)]
            self.g_ref[pl.ds(own, size)] = tree(terms)
            for s in (4, 3, 5, 2, 6, 1, 7):
                to, peer = self.along("z", s)
                self.copy(self.chunk(own, size), self.chunk(own, size), 12 + s, peer).start()

        self.takes(self.z, total)

    def stage4(self):
        size = CHUNK[self.group]
        for s in range(1, ZS):
            sender = lax.rem(self.z + ZS - s, ZS)

            def receive():
                got = self.chunk(self.second + sender * size, size)
                self.copy(got, got, 12 + s, self.partner).wait_recv()

            self.takes(sender, receive)
        self.back()

    def back(self):
        mine = self.chunk(self.second, SECOND[self.group])
        for s in (2, 1, 3):
            to, peer = self.along("second", s)
            self.start(mine, mine, 19 + s, peer)

    def stage5(self):
        size = SECOND[self.group]
        for s in range(1, 4):
            got = self.chunk(self.first + lax.rem(self.b + 4 - s, 4) * size, size)
            self.copy(got, got, 19 + s, self.partner).wait_recv()
        mine = self.chunk(self.first, FIRST[self.group])
        for s in (2, 1, 3):
            to, peer = self.along("first", s)
            self.start(mine, mine, 22 + s, peer)
        self.start(mine, mine, 26, self.partner)

    def stage6(self):
        size = FIRST[self.group]
        for s in (1, 3, 2):
            got = self.chunk(self.half + lax.rem(self.a + 4 - s, 4) * size, size)
            self.copy(got, got, 22 + s, self.partner).wait_recv()
            self.start(got, got, 26 + s, self.partner)

    def stage7(self):
        size = FIRST[self.group]
        for s in range(4):
            got = self.chunk(self.other_half + lax.rem(self.b + 4 - s, 4) * size, size)
            self.copy(got, got, 26 + s, self.partner).wait_recv()

    def finish(self):
        for size, index in self.started:
            part = self.chunk(0, size)
            self.copy(part, part, index, self.partner).wait_send()
        if self.direct:
            return
        size = CHUNK[self.group]
        for s in range(1, ZS):
            to, peer = self.along("z", s)

            def sent():
                part = self.acc3.at[pl.ds(to * size, size)]
                self.copy(part, part, 5 + s, peer).wait_send()

            self.takes(to, sent)

            def sent_back():
                part = self.chunk(self.second, size)
                self.copy(part, part, 12 + s, peer).wait_send()

            self.takes(self.z, sent_back)


def orthonormalize_kernel(n, scale, src_ref, out_ref, *scratch):
    (own_ref, other_ref, held_hi, held_lo, p_ref, g_ref, cur_ref, d_ref, z_ref, x_ref, hi_ref, lo_ref, lane_ref, row_ref) = scratch[:14]
    groups_scratch = [scratch[14 + 5 * g : 19 + 5 * g] for g in range(4)]
    (send, recv, x_send, x_recv, in_send, in_recv, pass_send, pass_recv, own_sem) = scratch[34:]
    rows_each, width = src_ref.shape[0], own_ref.shape[1]
    bands = src_ref.shape[1] // width
    per_panel = B // rows_each
    tiles = B // V
    me = lax.axis_index("band")
    core, x, y, z = coordinates()
    partner = device(1 - core, x, y, z)

    barrier = pltpu.get_barrier_semaphore()

    def greet(s, carry):
        pl.semaphore_signal(
            barrier, inc=1, device_id={"band": lax.rem(me + s, bands)}, device_id_type=MESH
        )
        return carry

    others = [device(core, x, y, lax.rem(z + s, ZS)) for s in range(1, ZS)]
    others += [device(core, lax.rem(x + s, XS), y, z) for s in (1, 3)]
    for peer in others:
        pl.semaphore_signal(barrier, inc=1, device_id=peer, device_id_type=MESH)
    lax.fori_loop(1, bands, greet, 0)

    def columns(ref, index):
        return ref.at[:, pl.ds(pl.multiple_of(index * width, width), width)]

    def band(ref, index):
        return ref.at[pl.ds(pl.multiple_of(index * rows_each, rows_each), rows_each), :]

    mine = pltpu.make_async_copy(columns(src_ref, me), band(own_ref, me), own_sem)
    mine.start()
    pl.semaphore_wait(barrier, bands - 1 + len(others))

    def bring(s, source):
        peer = lax.rem(me + s, bands)
        return pltpu.make_async_remote_copy(
            src_ref=columns(src_ref, peer),
            dst_ref=band(own_ref, source),
            send_sem=in_send.at[s],
            recv_sem=in_recv.at[s],
            device_id={"band": peer},
            device_id_type=MESH,
        )

    def hand_over(source):
        return pltpu.make_async_remote_copy(
            src_ref=band(own_ref, source),
            dst_ref=band(other_ref, source),
            send_sem=pass_send.at[source],
            recv_sem=pass_recv.at[source],
            device_id=partner,
            device_id_type=MESH,
        )

    def keep(ref, source, at):
        rows = pl.ds(pl.multiple_of(source * rows_each, rows_each), rows_each)
        high, low = split(ref[rows, :])
        held_hi[rows, at : at + width] = high
        held_lo[rows, at : at + width] = low

    def start(s, carry):
        bring(s, me).start()
        return carry

    def arrive(s, carry):
        source = lax.rem(me - s + bands, bands)
        bring(s, source).wait_recv()
        hand_over(source).start()
        keep(own_ref, source, 0)
        return carry

    def finish(s, carry):
        source = lax.rem(me + 1 - 2 * core - s + bands, bands)
        hand_over(source).wait_recv()
        keep(other_ref, source, width)
        return carry

    def sent(s, carry):
        bring(s, me).wait_send()
        hand_over(lax.rem(me + s, bands)).wait_send()
        return carry

    lax.fori_loop(1, bands, start, 0)
    mine.wait()
    hand_over(me).start()
    keep(own_ref, me, 0)
    lax.fori_loop(1, bands, arrive, 0)
    lax.fori_loop(0, bands, finish, 0)

    groups = grouped_blocks(n)

    def multiply(g):
        half = len(groups[g]) // CORES
        for c in range(CORES):

            @pl.when(core == c)
            def _():
                blocks = groups[g][c * half : (c + 1) * half]
                for i in sorted({i for i, _ in blocks}):
                    wanted = [j for k, j in blocks if k == i]
                    first, end = min(wanted), max(wanted) + 1
                    left = (held_hi[i * B : (i + 1) * B], held_lo[i * B : (i + 1) * B])
                    right = (held_hi[first * B : end * B], held_lo[first * B : end * B])
                    out = dot3(left, right, ((1,), (1,))) * scale
                    for j in wanted:
                        at = sum(HALF[:g]) + blocks.index((i, j)) * tiles
                        block = out[:, (j - first) * B : (j - first + 1) * B]
                        p_ref[at : at + tiles] = block.reshape(tiles, V, B)

    one, two, three, four = (Summing(g, p_ref, g_ref, groups_scratch[g], send, recv) for g in range(4))
    multiply(0)
    one.stage0()
    multiply(1)
    two.stage0()
    multiply(2)
    three.stage0()
    multiply(3)
    four.stage0()
    one.stage1()
    two.stage1()
    one.stage2()
    three.stage1()
    two.stage2()
    four.stage1()
    three.stage2()
    one.stage3()
    four.stage2()
    two.stage3()
    one.stage5()
    three.stage3()
    two.stage5()
    four.stage3()
    one.stage6()
    three.stage5()
    two.stage6()
    one.stage7()
    four.stage5()

    order = [block for group in groups for block in group]
    sub = lax.broadcasted_iota(jnp.int32, (V, B), 0)
    lane = lax.broadcasted_iota(jnp.int32, (V, B), 1)

    def scales(k):
        at = order.index((k, k)) * tiles
        on_diagonal = [jnp.where(lane == q * V + sub, g_ref[at + q], 0.0) for q in range(tiles)]
        diagonal = jnp.sum(tree(on_diagonal), axis=0, keepdims=True)
        lanes = jnp.broadcast_to(lax.rsqrt(diagonal), (V, B))
        lane_ref[...] = lanes
        for q in range(tiles):
            row_ref[q * V : (q + 1) * V, :] = jnp.take_along_axis(lanes, q * V + sub, axis=1)

    def prepare(k):
        if k in (0, 1, 4):
            scales(k)
        lanes = lane_ref[...]
        taken = None
        if k:
            left = (hi_ref[: k * B, k * B : (k + 1) * B], lo_ref[: k * B, k * B : (k + 1) * B])
            right = (hi_ref[: k * B, k * B :], lo_ref[: k * B, k * B :])
            taken = dot3(left, right, ((0,), (0,)))
        for j in range(k, n + width // B):
            if j < n:
                at = order.index((k, j)) * tiles
                block = g_ref[at : at + tiles].reshape(B, B)
            else:
                block = own_ref[k * B : (k + 1) * B, (j - n) * B : (j - n + 1) * B]
            if k:
                block = block - taken[:, (j - k) * B : (j - k + 1) * B]
            if j > k:
                cur_ref[:, j * B : (j + 1) * B] = block
                continue
            for q in range(tiles):
                at = slice(q * V, (q + 1) * V)
                d_ref[at, :] = block[at] * row_ref[at, :] * lanes

    def remote(peer, sender):
        return pltpu.make_async_remote_copy(
            src_ref=x_ref.at[pl.ds(peer * rows_each, rows_each), :],
            dst_ref=columns(out_ref, sender),
            send_sem=x_send.at[peer],
            recv_sem=x_recv.at[sender],
            device_id={"band": peer},
            device_id_type=MESH,
        )

    stays = pltpu.make_async_copy(band(x_ref, me), columns(out_ref, me), own_sem)

    def step(i, carry):
        for k in range(n):

            @pl.when(i == k)
            def _():
                if k == 1:
                    two.stage7()
                if k == 2:
                    three.stage7()
                if k == 4:
                    four.stage7()
                prepare(k)

        rows = [d_ref[q * V : (q + 1) * V, :] for q in range(tiles)]
        lanes = lane_ref[...]
        for q, inverse in enumerate(factor_inverse(rows)):
            z_ref[q * V : (q + 1) * V, :] = inverse * lanes
        for k in range(n):

            @pl.when(i == k)
            def _():
                if k == 0:
                    three.stage6()
                if k == 1:
                    four.stage6()
                panel = dot3(split(z_ref[...]), split(cur_ref[:, (k + 1) * B :]), ((1,), (0,)))
                x_ref[k * B : (k + 1) * B, :] = panel[:, panel.shape[1] - width :]
                for peer in range(k * per_panel, (k + 1) * per_panel):

                    @pl.when(peer != me)
                    def _():
                        remote(peer, me).start()

                    @pl.when(peer == me)
                    def _():
                        stays.start()

                if 0 < k < n - 1 and k != 3:
                    scales(k + 1)
                if k < n - 1:
                    high, low = split(panel)
                    hi_ref[k * B : (k + 1) * B, (k + 1) * B :] = high
                    lo_ref[k * B : (k + 1) * B, (k + 1) * B :] = low

        return carry

    lax.fori_loop(0, n, step, 0)
    lax.fori_loop(1, bands, sent, 0)
    hand_over(me).wait_send()
    for group in (one, two, three, four):
        group.finish()
    stays.wait()
    for other in range(bands):

        @pl.when(other != me)
        def _():
            remote(other, me).wait_send()
            remote(other, other).wait_recv()


def orthonormalize(coeffs, bands, columns_all):
    rows_each, columns = coeffs.shape
    rows, width = rows_each * bands, columns // bands
    n = rows // B
    tiles = lambda *shape: pltpu.VMEM((*shape, V, B), jnp.float32)
    whole = n * B + width
    summing = []
    for g in range(4):
        summing += [tiles(FIRST[g]), tiles(SECOND[g]), tiles(3, FIRST[g]), tiles(3, SECOND[g])]
        summing += [tiles(ZS - 1, CHUNK[g]) if Z_USED[g] else tiles(ZS, SECOND[g])]
    return pl.pallas_call(
        functools.partial(orthonormalize_kernel, n, 1.0 / columns_all),
        out_shape=jax.ShapeDtypeStruct(coeffs.shape, jnp.float32),
        in_specs=[pl.BlockSpec(memory_space=pltpu.HBM)],
        out_specs=pl.BlockSpec(memory_space=pltpu.VMEM),
        scratch_shapes=[
            pltpu.VMEM((rows, width), jnp.float32),
            pltpu.VMEM((rows, width), jnp.float32),
            pltpu.VMEM((rows, CORES * width), jnp.bfloat16),
            pltpu.VMEM((rows, CORES * width), jnp.bfloat16),
            tiles(sum(HALF)),
            tiles(sum(TOTAL)),
            pltpu.VMEM((B, whole), jnp.float32),
            pltpu.VMEM((B, B), jnp.float32),
            pltpu.VMEM((B, B), jnp.float32),
            pltpu.VMEM((rows, width), jnp.float32),
            pltpu.VMEM((rows, whole), jnp.bfloat16),
            pltpu.VMEM((rows, whole), jnp.bfloat16),
            pltpu.VMEM((V, B), jnp.float32),
            pltpu.VMEM((B, B), jnp.float32),
            *summing,
            pltpu.SemaphoreType.DMA((4 * COPIES,)),
            pltpu.SemaphoreType.DMA((4 * COPIES,)),
            *[pltpu.SemaphoreType.DMA((bands,))] * 6,
            pltpu.SemaphoreType.DMA,
        ],
        compiler_params=pltpu.CompilerParams(
            collective_id=0, has_side_effects=True, vmem_limit_bytes=52 << 20
        ),
        name="orthonormalize",
    )(coeffs)


def local(coeffs):
    bands = lax.axis_size("band")
    return orthonormalize(coeffs, bands, coeffs.shape[1] * lax.axis_size("ga"))


def solution(mesh):
    return jax.shard_map(
        local,
        mesh=mesh,
        in_specs=(P("band", "ga"),),
        out_specs=P("band", "ga"),
        check_vma=False,
    )
```
